256 devices in a mesh: seq: 128 (over x, z, y), mp: 2 (over core).
Axes of the slice: x: 4, y: 4, z: 8, core: 2. Of those that a mesh axis runs over, the one named last changes fastest.
Arguments:
- states: bfloat16 [32768, 768], P('seq'), may hold values from -24 to 24
- qkv_weight: bfloat16 [3, 768, 768], P(None, None, 'mp'), may hold values from -0.21875 to 0.21875
- out_weight: bfloat16 [768, 768], P('mp'), may hold values from -0.21875 to 0.21875
- up_weight: bfloat16 [768, 3072], P(None, 'mp'), may hold values from -0.21875 to 0.21875
- down_weight: bfloat16 [3072, 768], P('mp'), may hold values from -0.109375 to 0.109375
- attn_gain: float32 [768], replicated, may hold values from 0.5 to 1.5
- mlp_gain: float32 [768], replicated, may hold values from 0.5 to 1.5
- global_ids: int32 [2], replicated, may hold values from 0 to 511, as said below
- random_owner: int32 [2, 512, 6, 3], P('mp', 'seq'), may hold values from 0 to 127, all different within a row; in each aligned block of 24 rows (0 to 23, 24 to 47, ..., all dimensions but the last counted through in order) at most 2 rows name the same one
- random_local: int32 [2, 512, 6, 3], P('mp', 'seq'), may hold values from 0 to 3
Outputs:
- layer_out: bfloat16 [32768, 768], P('seq')
The draws below stay inside these ranges and needn't reach their ends.
Inputs may be any that keep to these rules, and one draw needn't show every extreme that they name: `global_ids`: 2 different block numbers; the second is 511. The random key block is random_owner * 4 + random_local. For one query block and head the 3 owners differ. Within the rows of one device (aligned blocks of 4 * K rows over the first three dimensions, K the third dimension) no owner is named more than 2 times, a bound that some block reaches.
All inputs are finite; a program needn't handle non-finite values.
Results may differ from the reference program's by a relative error of at most 0.008.
The reference program's roundings to bfloat16 on the way count: a program that leaves them out, or rounds other values in their place, can miss the bound.
Values may be sent and summed in bfloat16 or wider, within the bound.
No kernel may reach another device: no remote copies, remote signals or barrier semaphores. Data moves between devices by JAX's collectives and lax.ppermute only.
A program may use at most 192 MiB of HBM per device.

```python
import math
import jax
import jax.numpy as jnp
import numpy as np
from jax import lax

D = 768
H = 12
HD = 64
FF = 3072
BS = 64
R = 3
G = 2
QB_DEV = 4
TOKENS = 32768
NB = 512
MOST = 2
N_SEQ = 128
N_MP = 2


def chosen_blocks(key):
    first = jax.random.randint(jax.random.fold_in(key, 11), (1,), 0, NB - 1)
    return jnp.concatenate([first, jnp.full((1,), NB - 1)]).astype(jnp.int32)


def draw_global_ids(key, part):
    return chosen_blocks(key)


def draw_states(key, part):
    split_keys = jax.random.split(jax.random.fold_in(key, 23), 5)
    starts = chosen_blocks(key) * BS + 3
    picked = jax.random.randint(split_keys[3], (8,), BS // 2, TOKENS - BS)
    anchors = jnp.concatenate([starts, picked])
    direction = jax.random.uniform(split_keys[2], (D,), jnp.float32, -1.7, 1.7)
    jitter = jax.random.normal(split_keys[4], (2, anchors.shape[0], D), jnp.float32) * 0.05
    sample = jax.random.normal(split_keys[1], (TOKENS, D), jnp.float32)
    strength = jnp.linspace(2.5, 3.5, anchors.shape[0]).astype(jnp.float32)
    first_rows = strength[:, None] * direction[None, :] + jitter[0]
    second_rows = strength[:, None] * direction[None, :] * 1.01 + jitter[1]
    sample = sample.at[anchors].set(first_rows).at[anchors + 1].set(second_rows)
    return jnp.clip(sample, -6.0, 6.0).astype(jnp.bfloat16)


def place_ends(array, rng, low, largest):
    place = [jax.random.randint(jax.random.fold_in(rng, axis), (), 0, length) for axis, length in enumerate(array.shape)]
    longest = array.shape.index(max(array.shape))
    neighbour = place[:longest] + [(place[longest] + 1) % array.shape[longest]] + place[longest + 1:]
    return array.at[tuple(place)].set(low).at[tuple(neighbour)].set(largest)


def levels(key, extent, shards, low, high):
    loudness, own = 1.0, jax.random.fold_in(key, 6)
    for dim, shards_of in shards:
        steps = jnp.exp(jax.random.uniform(jax.random.fold_in(own, dim), (shards_of,), jnp.float32, low / len(shards), high / len(shards)))
        loudness = loudness * jnp.repeat(steps, extent[dim] // shards_of).reshape([-1 if axis == dim else 1 for axis in range(len(extent))])
    return loudness


def shared_out(stream_key, own, number, rows, count, top, most, lean):
    ranking = jax.random.permutation(stream_key, count)
    crowded, usual = shares(count, rows * top, most, lean, True), shares(count, rows * top, most, lean, False)
    places = jnp.arange(count)

    def named(tallies, rotation):
        used = int((tallies > 0).sum())
        fixed = max(1, used // 4)
        moved = fixed + (places - fixed + rotation * (used - fixed)) % max(1, count - fixed)
        return jnp.zeros((count,), jnp.int32).at[ranking[jnp.where(places < fixed, places, moved)]].set(jnp.asarray(tallies, jnp.int32))

    tallies = jnp.where(number % 4 == 0, named(crowded, number // 4), named(usual, number - number // 4 - 1))
    mixed = jax.random.permutation(jax.random.fold_in(own, 3), count)
    donor, sink = mixed[0:count // 2 * 2:2], mixed[1:count // 2 * 2:2]
    room = jnp.minimum(tallies[donor] - 1, most - tallies[sink]) // 2
    room = jnp.where((donor == ranking[0]) | (sink == ranking[0]) | (tallies[sink] == 0), 0, jnp.maximum(room, 0))
    moved = jax.random.randint(jax.random.fold_in(own, 4), (count // 2,), 0, 1 << 20) % (room + 1)
    tallies = tallies.at[donor].add(-moved).at[sink].add(moved)
    items = jnp.searchsorted(jnp.cumsum(tallies), jnp.arange(rows * top), side="right").astype(jnp.int32)
    grid = items.reshape(top, rows).T
    grid = grid[jax.random.permutation(jax.random.fold_in(own, 1), rows)]
    rotation = jax.random.randint(jax.random.fold_in(own, 2), (rows, 1), 0, top)
    return jnp.take_along_axis(grid, (jnp.arange(top)[None, :] + rotation) % top, axis=1)


def shares(number_of, total, reach, skew, full):
    weights = [(1 << 20) // math.isqrt(rank ** skew) + 1 for rank in range(1, number_of + 1)]
    largest = reach if full else min(reach, max(-(-total // number_of), total * weights[0] // sum(weights)))
    least = 1 if total - largest >= number_of - 1 else 0
    holding, spare = [largest] + [least] * (number_of - 1), total - largest - least * (number_of - 1)
    while spare > 0:
        free = [i for i in range(1, number_of) if holding[i] < largest] or [i for i in range(1, number_of) if holding[i] < reach]
        mass, left = sum([weights[i] for i in free]), spare
        for i in free:
            addition = min(reach - holding[i], max(1, left * weights[i] // mass), spare)
            holding[i] = holding[i] + addition
            spare = spare - addition
    return np.array(holding)


def noise(own_key, extent, scale, bound, pieces=(), held_as=jnp.bfloat16):
    array = scale * jax.random.normal(own_key, extent, jnp.float32)
    if pieces:
        array = array * levels(own_key, extent, pieces, -0.22, 0.18)
    return jnp.clip(array, -bound, bound).astype(held_as)


def setup_inputs(seed: int = 0) -> dict:
    seeds = jax.random.split(jax.random.key(seed), 11)
    states = draw_states(jax.random.fold_in(seeds[10], 71), 0)
    qkv_weight = noise(seeds[1], (3, D, D), D ** -0.5, 0.21875, ((2, 2),))
    out_weight = noise(seeds[2], (D, D), D ** -0.5, 0.21875, ((0, 2),))
    up_weight = noise(seeds[3], (D, FF), D ** -0.5, 0.21875, ((1, 2),))
    down_weight = noise(seeds[4], (FF, D), FF ** -0.5, 0.109375, ((0, 2),))
    attn_gain = jnp.clip(1.0 + 0.1 * jax.random.normal(seeds[5], (D,), jnp.float32), 0.5, 1.5)
    mlp_gain = jnp.clip(1.0 + 0.1 * jax.random.normal(seeds[6], (D,), jnp.float32), 0.5, 1.5)
    global_ids = draw_global_ids(jax.random.fold_in(seeds[10], 71), 0)
    random_owner_keys = jax.random.split(jax.random.fold_in(seeds[8], 1), N_MP * NB * (H // N_MP) // (QB_DEV * (H // N_MP)))
    random_owner_turns = jax.random.permutation(jax.random.fold_in(seeds[8], 3), N_MP * NB * (H // N_MP) // (QB_DEV * (H // N_MP)))
    random_owner = jax.vmap(lambda own, number: shared_out(jax.random.fold_in(seeds[8], 2), own, number, QB_DEV * (H // N_MP), N_SEQ, R, MOST, 2))(random_owner_keys, random_owner_turns).reshape((N_MP, NB, H // N_MP, R))
    random_local = place_ends(jax.random.randint(seeds[9], (N_MP, NB, H // N_MP, R), 0, QB_DEV), jax.random.fold_in(seeds[9], 1), 0, QB_DEV - 1).astype(jnp.int32)
    return dict(states=states, qkv_weight=qkv_weight, out_weight=out_weight, up_weight=up_weight, down_weight=down_weight, attn_gain=attn_gain, mlp_gain=mlp_gain, global_ids=global_ids, random_owner=random_owner, random_local=random_local)


EPSILON = 1e-05
NEGATIVE = -1e+30

def layer_norm(inputs, scales):
    center = lax.optimization_barrier(jnp.mean(inputs, axis=-1, keepdims=True))
    shifted = inputs - center
    spread = lax.optimization_barrier(jnp.mean(shifted * shifted, axis=-1, keepdims=True))
    return shifted * lax.rsqrt(spread + EPSILON) * scales.astype(jnp.float32)

def softmax_rows(scores):
    highest = lax.optimization_barrier(jnp.max(scores, axis=-1, keepdims=True))
    raised = jnp.exp(scores - highest)
    return raised / lax.optimization_barrier(jnp.sum(raised, axis=-1, keepdims=True))

def reference(states, qkv_weight, out_weight, up_weight, down_weight, attn_gain, mlp_gain, global_ids, random_owner, random_local):
    block_count = TOKENS // BS
    scaling = HD ** (-0.5)
    highest = lax.Precision.HIGHEST
    query_all = jnp.dot(states, qkv_weight[0], preferred_element_type=jnp.float32).astype(jnp.bfloat16)
    key_all = jnp.dot(states, qkv_weight[1], preferred_element_type=jnp.float32).astype(jnp.bfloat16)
    value_all = jnp.dot(states, qkv_weight[2], preferred_element_type=jnp.float32).astype(jnp.bfloat16)
    query_heads = query_all.reshape(block_count, BS, H, HD)
    key_heads = key_all.reshape(block_count, BS, H, HD).transpose(0, 2, 1, 3)
    value_heads = value_all.reshape(block_count, BS, H, HD).transpose(0, 2, 1, 3)
    random_ids = (random_owner * QB_DEV + random_local).transpose(1, 0, 2, 3).reshape(block_count, H, R)
    head_range = jnp.arange(H, dtype=jnp.int32)
    global_keys = key_heads[global_ids].astype(jnp.float32)
    global_values = value_heads[global_ids].astype(jnp.float32)

    def sparse_group(first_block):
        block_ids = first_block + jnp.arange(QB_DEV, dtype=jnp.int32)
        query_part = lax.dynamic_slice_in_dim(query_heads, first_block, QB_DEV, 0).astype(jnp.float32)
        offsets = block_ids[:, None] + jnp.arange(-1, 2, dtype=jnp.int32)[None, :]
        inside = (offsets >= 0) & (offsets < block_count)
        clipped = jnp.clip(offsets, 0, block_count - 1)
        window_keys = key_heads[clipped].astype(jnp.float32)
        window_values = value_heads[clipped].astype(jnp.float32)
        chosen = random_ids[block_ids]
        random_keys = key_heads[chosen, head_range[None, :, None]].astype(jnp.float32)
        random_values = value_heads[chosen, head_range[None, :, None]].astype(jnp.float32)
        score_window = jnp.einsum('bqhd,bwhkd->bhqwk', query_part, window_keys, precision=highest) * scaling
        score_window = jnp.where(inside[:, None, None, :, None], score_window, NEGATIVE)
        score_random = jnp.einsum('bqhd,bhrkd->bhqrk', query_part, random_keys, precision=highest) * scaling
        score_global = jnp.einsum('bqhd,ghkd->bhqgk', query_part, global_keys, precision=highest) * scaling
        joined = jnp.concatenate([score_window, score_random, score_global], axis=3)
        joined_shape = joined.shape
        flat_weights = softmax_rows(joined.reshape(joined_shape[0], joined_shape[1], joined_shape[2], -1))
        weights = lax.optimization_barrier(flat_weights.astype(jnp.bfloat16)).astype(jnp.float32).reshape(joined_shape)
        result = jnp.einsum('bhqwk,bwhkd->bqhd', weights[:, :, :, :3], window_values, precision=highest)
        result = result + jnp.einsum('bhqrk,bhrkd->bqhd', weights[:, :, :, 3:3 + R], random_values, precision=highest)
        result = result + jnp.einsum('bhqgk,ghkd->bqhd', weights[:, :, :, 3 + R:], global_values, precision=highest)
        return result
    sparse = lax.map(sparse_group, jnp.arange(N_SEQ, dtype=jnp.int32) * QB_DEV)
    sparse = sparse.reshape(block_count, BS, H, HD)
    global_queries = query_heads[global_ids].astype(jnp.float32).transpose(2, 0, 1, 3).reshape(H, G * BS, HD)
    every_key = key_heads.transpose(1, 0, 2, 3).reshape(H, TOKENS, HD)
    every_value = value_heads.transpose(1, 0, 2, 3).reshape(H, TOKENS, HD)

    def global_head(inputs):
        query_rows, key_rows, value_rows = inputs
        scores = jnp.dot(query_rows, key_rows.astype(jnp.float32).T, precision=highest) * scaling
        return jnp.dot(softmax_rows(scores), value_rows.astype(jnp.float32), precision=highest)
    global_out = lax.map(global_head, (global_queries, every_key, every_value))
    global_out = global_out.reshape(H, G, BS, HD).transpose(1, 2, 0, 3)
    sparse = sparse.at[global_ids].set(global_out)
    attended = sparse.astype(jnp.bfloat16).reshape(TOKENS, D)
    projected = jnp.dot(attended, out_weight, preferred_element_type=jnp.float32)
    normed = layer_norm(states.astype(jnp.float32) + projected, attn_gain).astype(jnp.bfloat16)
    hidden = jax.nn.gelu(jnp.dot(normed, up_weight, preferred_element_type=jnp.float32), approximate=False).astype(jnp.bfloat16)
    expanded = jnp.dot(hidden, down_weight, preferred_element_type=jnp.float32)
    return layer_norm(normed.astype(jnp.float32) + expanded, mlp_gain).astype(jnp.bfloat16)
```

```python
import functools

import jax
import jax.numpy as jnp
from jax import lax
from jax.experimental import pallas as pl
from jax.experimental.pallas import tpu as pltpu
from jax.sharding import Mesh
from jax.sharding import PartitionSpec as P

SEQ = ("x", "z", "y")
PLANE = ("x", "y")
EPSILON = 1e-05
NEGATIVE = -1e30
HEADS = 6
BF16 = jnp.bfloat16
F32 = jnp.float32
LIMIT = 48 * 1024 * 1024
VMEM = pl.BlockSpec(memory_space=pltpu.VMEM)
SMEM = pl.BlockSpec(memory_space=pltpu.SMEM)


def nt(a, b):
    return lax.dot_general(a, b, (((1,), (1,)), ((), ())), preferred_element_type=F32)


def nn(a, b):
    return jnp.dot(a, b, preferred_element_type=F32)


def call(kernel, outs, in_specs, out_specs, scratch, cost, *args):
    return pl.pallas_call(
        kernel,
        out_shape=outs,
        in_specs=in_specs,
        out_specs=out_specs,
        scratch_shapes=scratch,
        cost_estimate=pl.CostEstimate(flops=cost[0], bytes_accessed=cost[1], transcendentals=cost[2]),
        compiler_params=pltpu.CompilerParams(vmem_limit_bytes=LIMIT),
    )(*args)


def prepare_kernel(states_ref, weight_ref, wq_ref, wkv_ref, q_ref, kv_ref):
    wq_ref[...] = jnp.zeros_like(wq_ref)
    for h in range(HEADS):
        part = slice(64 * h, 64 * h + 64)
        wq_ref[:, 128 * h : 128 * h + 64] = weight_ref[0, :, part] * BF16(0.125)
        wkv_ref[:, 128 * h : 128 * h + 64] = weight_ref[1, :, part]
        wkv_ref[:, 128 * h + 64 : 128 * h + 128] = weight_ref[2, :, part]
    states = states_ref[...]
    query = nn(states, wq_ref[...]).astype(BF16)
    pair = nn(states, wkv_ref[...]).astype(BF16)
    for h in range(HEADS):
        q_ref[h] = query[:, 128 * h : 128 * h + 128]
        kv_ref[h] = pair[:, 128 * h : 128 * h + 128]


def prepare(states, weight):
    shape = jax.ShapeDtypeStruct
    return call(
        prepare_kernel,
        (shape((768, 768), BF16), shape((768, 768), BF16), shape((HEADS, 256, 128), BF16), shape((HEADS, 256, 128), BF16)),
        [VMEM] * 2,
        [VMEM] * 4,
        [],
        (600_000_000, 6_000_000, 0),
        states,
        weight,
    )


def column_kernel(own_ref, other_ref, wkv_ref, wanted_ref, kv_ref, items_ref):
    for half, source in enumerate((own_ref, other_ref)):

        @pl.loop(0, 4)
        def _(i):
            rows = pl.multiple_of(i * 256, 256)
            pair = nn(source[pl.ds(rows, 256), :], wkv_ref[...]).astype(BF16)
            for h in range(HEADS):
                kv_ref[pl.ds(h * 2048 + half * 1024 + rows, 256), :] = pair[:, 128 * h : 128 * h + 128]

    @pl.loop(0, 32)
    def _(i):
        for k in range(8):
            s = i * 8 + k
            at = pl.multiple_of(wanted_ref[0, s] * 64, 64)
            items_ref[s] = kv_ref[pl.ds(at, 64), :]


def column(own, other, wkv, wanted):
    shape = jax.ShapeDtypeStruct
    return call(
        column_kernel,
        (shape((HEADS * 2048, 128), BF16), shape((256, 64, 128), BF16)),
        [VMEM, VMEM, VMEM, SMEM],
        [VMEM, VMEM],
        [],
        (2_400_000_000, 12_000_000, 0),
        own,
        other,
        wkv,
        wanted,
    )


def partial_kernel(own_ref, other_ref, wq_ref, wkv_ref, kv_ref, out_ref, pair_ref, q_ref, s_ref, ml_ref):
    for half, source in enumerate((own_ref, other_ref)):
        rows = slice(64 * half, 64 * half + 64)
        query = nn(source[...], wq_ref[...]).astype(BF16)
        pair = nn(source[...], wkv_ref[...]).astype(BF16)
        for h in range(HEADS):
            q_ref[h, rows, :] = query[:, 128 * h : 128 * h + 128]
            pair_ref[h, rows, :] = pair[:, 128 * h : 128 * h + 128]
    lane = lax.broadcasted_iota(jnp.int32, (128, 128), 1)
    stats = jnp.zeros((128, 128), F32)
    for h in range(HEADS):
        high = jnp.full((128, 1), NEGATIVE, F32)
        for c in range(4):
            s = nt(q_ref[h], kv_ref[h * 2048 + c * 512 : h * 2048 + c * 512 + 512, :])
            s_ref[h % 2, :, c * 512 : c * 512 + 512] = s
            high = jnp.maximum(high, jnp.max(s, axis=1, keepdims=True))
        total = jnp.zeros((128, 1), F32)
        acc = jnp.zeros((128, 128), F32)
        for c in range(4):
            p = jnp.exp(s_ref[h % 2, :, c * 512 : c * 512 + 512] - high)
            total = total + jnp.sum(p, axis=1, keepdims=True)
            head = p.astype(BF16)
            rest = (p - head.astype(F32)).astype(BF16)
            keys = kv_ref[h * 2048 + c * 512 : h * 2048 + c * 512 + 512, :]
            acc = acc + nn(head, keys) + nn(rest, keys)
        out_ref[h // 2, :, (h % 2) * 64 : (h % 2) * 64 + 64] = acc[:, 64:128]
        stats = jnp.where(lane == h, high, jnp.where(lane == 64 + h, total, stats))
    out_ref[3] = stats


def partial(own, other, wq, wkv, kv):
    shape = jax.ShapeDtypeStruct
    return call(
        partial_kernel,
        (shape((4, 128, 128), F32), shape((HEADS, 128, 128), BF16)),
        [VMEM] * 5,
        [VMEM] * 2,
        [
            pltpu.VMEM((HEADS, 128, 128), BF16),
            pltpu.VMEM((2, 128, 2048), F32),
            pltpu.VMEM((8, 128), F32),
        ],
        (2_000_000_000, 5_000_000, 1_600_000),
        own,
        other,
        wq,
        wkv,
        kv,
    )


def merged(refs):
    stats = [r[3] for r in refs]
    highs, totals, factors = [], [], []
    for h in range(HEADS):
        high = functools.reduce(jnp.maximum, [s[:, h : h + 1] for s in stats])
        factor = [jnp.exp(s[:, h : h + 1] - high) for s in stats]
        highs.append(high)
        factors.append(factor)
        totals.append(sum(s[:, 64 + h : 65 + h] * f for s, f in zip(stats, factor)))
    sums = []
    for h in range(HEADS):
        lanes = slice((h % 2) * 64, (h % 2) * 64 + 64)
        sums.append(sum(r[h // 2, :, lanes] * f for r, f in zip(refs, factors[h])))
    return highs, totals, sums


def merge_kernel(a_ref, b_ref, c_ref, d_ref, out_ref):
    highs, totals, sums = merged((a_ref, b_ref, c_ref, d_ref))
    lane = lax.broadcasted_iota(jnp.int32, (128, 128), 1)
    stats = jnp.zeros((128, 128), F32)
    for h in range(HEADS):
        stats = jnp.where(lane == h, highs[h], jnp.where(lane == 64 + h, totals[h], stats))
        out_ref[h // 2, :, (h % 2) * 64 : (h % 2) * 64 + 64] = sums[h]
    out_ref[3] = stats


def merge(pieces):
    return call(
        merge_kernel,
        jax.ShapeDtypeStruct((4, 128, 128), F32),
        [VMEM] * 4,
        VMEM,
        [],
        (2_000_000, 1_300_000, 10_000),
        *pieces,
    )


def place_kernel(a_ref, b_ref, c_ref, d_ref, attended_ref, place_ref, out_ref, rows_ref):
    _, totals, sums = merged((a_ref, b_ref, c_ref, d_ref))
    for h in range(HEADS):
        rows_ref[:, 64 * h : 64 * h + 64] = (sums[h] / totals[h]).astype(BF16)
    out_ref[...] = attended_ref[...]
    core = place_ref[0, 2]
    for g in range(2):

        @pl.when(place_ref[0, g] >= 0)
        def _():
            start = place_ref[0, g] * 64
            for half, side in ((0, core), (1, 1 - core)):
                at = pl.multiple_of(start + side * 32, 32)
                out_ref[pl.ds(at, 32), :] = rows_ref[half * 64 + g * 32 : half * 64 + g * 32 + 32, :]


def place(pieces, attended, where):
    return call(
        place_kernel,
        jax.ShapeDtypeStruct((256, 384), BF16),
        [VMEM] * 5 + [SMEM],
        VMEM,
        [pltpu.VMEM((128, 384), BF16)],
        (2_000_000, 1_500_000, 10_000),
        *pieces,
        attended,
        where,
    )


def attend_kernel(q_ref, kv_ref, before_ref, after_ref, wkv_ref, remote_ref, pair_ref, slot_ref, edge_ref, out_ref, ext_ref, keys_ref):
    before = nn(before_ref[...], wkv_ref[...]).astype(BF16)
    after = nn(after_ref[...], wkv_ref[...]).astype(BF16)
    for h in range(HEADS):
        ext_ref[h, 0:64, :] = before[:, 128 * h : 128 * h + 128]
        ext_ref[h, 64:320, :] = kv_ref[h]
        ext_ref[h, 320:384, :] = after[:, 128 * h : 128 * h + 128]
    lane = lax.broadcasted_iota(jnp.int32, (64, 512), 1)

    @pl.loop(0, HEADS // 2)
    def _(pair):
        for b in range(4):
            outs = []
            for k in range(2):
                h = pair * 2 + k
                buf = keys_ref.at[b * 2 + k]
                buf[0:192, :] = ext_ref[h, b * 64 : b * 64 + 192, :]
                for r in range(3):
                    slot = slot_ref[0, (b * HEADS + h) * 3 + r]
                    buf[192 + 64 * r : 256 + 64 * r, :] = remote_ref[slot]
                buf[384:512, :] = pair_ref[h]
                keys = buf[...]
                s = nt(q_ref[h, b * 64 : b * 64 + 64, :], keys)
                if b == 0:
                    s = jnp.where((lane < 64) & (edge_ref[0, 0] > 0), NEGATIVE, s)
                if b == 3:
                    s = jnp.where((lane >= 128) & (lane < 192) & (edge_ref[0, 1] > 0), NEGATIVE, s)
                p = jnp.exp(s - jnp.max(s, axis=1, keepdims=True))
                w = (p / jnp.sum(p, axis=1, keepdims=True)).astype(BF16)
                outs.append(nn(w, keys)[:, 64:128])
            lanes = pl.ds(pl.multiple_of(pair * 128, 128), 128)
            out_ref[b * 64 : b * 64 + 64, lanes] = jnp.concatenate(outs, axis=1).astype(BF16)


def attend(q, kv, before, after, wkv, remote, pair, slots, edges):
    return call(
        attend_kernel,
        jax.ShapeDtypeStruct((256, 384), BF16),
        [VMEM] * 7 + [SMEM] * 2,
        VMEM,
        [pltpu.VMEM((HEADS, 384, 128), BF16), pltpu.VMEM((8, 512, 128), BF16)],
        (600_000_000, 7_000_000, 800_000),
        q,
        kv,
        before,
        after,
        wkv,
        remote,
        pair,
        slots,
        edges,
    )


def norm(v, gain):
    shifted = v - jnp.mean(v, axis=1, keepdims=True)
    spread = jnp.mean(shifted * shifted, axis=1, keepdims=True)
    return shifted * lax.rsqrt(spread + EPSILON) * gain


CHUNK = 512
STEPS = 1536 // CHUNK


def finish_kernel(
    own_ref, other_ref, states_ref, wo_own, wo_other, gain_ref, gain2_ref, up_own, up_other, down_own, down_other, out_ref, normed_ref, sum_ref
):
    step = pl.program_id(0)

    @pl.when(step == 0)
    def _():
        projected = nn(own_ref[...], wo_own[...]) + nn(other_ref[...], wo_other[...])
        normed_ref[...] = norm(states_ref[...].astype(F32) + projected, gain_ref[...]).astype(BF16)
        sum_ref[...] = jnp.zeros_like(sum_ref)

    def half(k, up, down):
        v = nn(normed_ref[...], up[...])
        hidden = (v * (1.0 + lax.erf(v * 0.7071067811865476)) * 0.5).astype(BF16)
        sum_ref[k] += nn(hidden, down[...])

    @pl.when(step < STEPS)
    def _():
        half(0, up_own, down_own)

    @pl.when(step >= STEPS)
    def _():
        half(1, up_other, down_other)

    @pl.when(step == 2 * STEPS - 1)
    def _():
        total = normed_ref[...].astype(F32) + (sum_ref[0] + sum_ref[1])
        out_ref[...] = norm(total, gain2_ref[...]).astype(BF16)


def finish(own, other, states, wo_own, wo_other, gain, gain2, up_own, up_other, down_own, down_other):
    whole = lambda *shape: pl.BlockSpec(shape, lambda s: (0, 0), pipeline_mode=pl.Buffered(1))
    first = lambda s: jnp.minimum(s, STEPS - 1)
    second = lambda s: jnp.maximum(s - STEPS, 0)
    return pl.pallas_call(
        finish_kernel,
        out_shape=jax.ShapeDtypeStruct((256, 768), BF16),
        grid=(2 * STEPS,),
        in_specs=[
            whole(256, 384),
            whole(256, 384),
            whole(256, 768),
            whole(384, 768),
            whole(384, 768),
            whole(1, 768),
            whole(1, 768),
            pl.BlockSpec((768, CHUNK), lambda s: (0, first(s))),
            pl.BlockSpec((768, CHUNK), lambda s: (0, second(s))),
            pl.BlockSpec((CHUNK, 768), lambda s: (first(s), 0)),
            pl.BlockSpec((CHUNK, 768), lambda s: (second(s), 0)),
        ],
        out_specs=pl.BlockSpec((256, 768), lambda s: (0, 0)),
        scratch_shapes=[pltpu.VMEM((256, 768), BF16), pltpu.VMEM((2, 256, 768), F32)],
        cost_estimate=pl.CostEstimate(flops=2_700_000_000, bytes_accessed=12_000_000, transcendentals=800_000),
        compiler_params=pltpu.CompilerParams(dimension_semantics=("arbitrary",), vmem_limit_bytes=LIMIT),
    )(own, other, states, wo_own, wo_other, gain, gain2, up_own, up_other, down_own, down_other)


def turned(value, axis, shift):
    count = lax.axis_size(axis)
    return lax.ppermute(value, axis, [(i, (i + shift) % count) for i in range(count)])


def swapped(value):
    return lax.ppermute(value, "mp", [(0, 1), (1, 0)])


def picked(pieces, number, per):
    rows = []
    for g in range(2):
        part = pieces[0][g * per : g * per + per]
        for k in range(1, len(pieces)):
            part = jnp.where(number[g] == k, pieces[k][g * per : g * per + per], part)
        rows.append(part)
    return jnp.concatenate(rows)


def everywhere(rows, here, root, per):
    for axis in ("y", "x"):
        pieces = [rows] + [turned(rows, axis, k) for k in (1, 2, 3)]
        rows = picked(pieces, (here[axis] - root[axis]) & 3, per)
    return rows


def shards(
    states, qkv_weight, out_weight, up_weight, down_weight, attn_gain, mlp_gain, global_ids, random_owner, random_local
):
    here = {axis: lax.axis_index(axis) for axis in ("x", "z", "y", "mp")}
    core = here["mp"]
    seq = (here["x"] * 8 + here["z"]) * 4 + here["y"]

    mine = lax.dynamic_slice_in_dim(states, core * 128, 128, 0)
    ups, downs = [mine], [mine]
    for _ in range(4):
        ups.append(turned(ups[-1], "z", 1))
    for _ in range(3):
        downs.append(turned(downs[-1], "z", -1))
    own = jnp.concatenate(ups + [downs[3], downs[2], downs[1]])
    other = swapped(own)

    owner = random_owner.reshape(-1)
    local = random_local.reshape(-1)
    head = jnp.broadcast_to(jnp.arange(HEADS, dtype=jnp.int32)[None, :, None], (4, HEADS, 3)).reshape(-1)

    def place_in_column(block_owner, block_local):
        away = (here["z"] - ((block_owner >> 2) & 7)) & 7
        far = ((block_local >> 1) != core).astype(jnp.int32)
        return far * 16 + away * 2 + (block_local & 1)

    item = head * 32 + place_in_column(owner, local)
    group = (owner >> 5) * 4 + (owner & 3)
    count = owner.shape[0]
    number = jnp.arange(count, dtype=jnp.int32)
    same = (group[:, None] == group[None, :]) & (number[None, :] < number[:, None])
    slots = group * 16 + jnp.sum(same.astype(jnp.int32), axis=1)
    chosen = slots[:, None] == jnp.arange(256, dtype=jnp.int32)[None, :]
    wanted = jnp.sum(jnp.where(chosen, item[:, None], 0), axis=0).reshape(16, 16)
    wanted = lax.all_to_all(wanted, PLANE, split_axis=0, concat_axis=0, tiled=True)

    ends = [(i, i + 1) for i in range(127)]
    before = lax.ppermute(states[192:], SEQ, ends)
    after = lax.ppermute(states[:64], SEQ, [(j, i) for i, j in ends])
    wo_other, up_other, down_other = swapped(out_weight), swapped(up_weight), swapped(down_weight)

    wq, wkv, q, kv = prepare(states, qkv_weight)
    pairs, items = column(own, other, wkv, wanted.reshape(1, 256))
    remote = lax.all_to_all(items.reshape(16, 1024, 128), PLANE, split_axis=0, concat_axis=0, tiled=True)

    root_owner, root_local = global_ids >> 2, global_ids & 3
    root = {"x": root_owner >> 5, "y": root_owner & 3}
    at = place_in_column(root_owner, root_local)
    parts = []
    for g in range(2):
        start = (at[g] & 15) * 64 + core * 32
        near = lax.dynamic_slice_in_dim(own, start, 32, 0)
        far = lax.dynamic_slice_in_dim(other, start, 32, 0)
        parts.append(jnp.where(at[g] >= 16, far, near))
    rows = everywhere(jnp.concatenate(parts), here, root, 32)
    part, pair = partial(rows, swapped(rows), wq, wkv, pairs)
    part = merge([part] + [turned(part, "y", k) for k in (1, 2, 3)])
    last = [part] + [turned(part, "x", k) for k in (1, 2, 3)]

    edges = jnp.stack([seq == 0, seq == 127]).astype(jnp.int32).reshape(1, 2)
    attended = attend(q, kv, before, after, wkv, remote.reshape(256, 64, 128), pair, slots.reshape(1, -1), edges)
    block = jnp.where(root_owner == seq, root_local, -1)
    where = jnp.concatenate([block, core[None]]).astype(jnp.int32).reshape(1, 3)
    attended = place(last, attended, where)
    return finish(
        attended,
        swapped(attended),
        states,
        out_weight,
        wo_other,
        attn_gain.reshape(1, -1),
        mlp_gain.reshape(1, -1),
        up_weight,
        up_other,
        down_weight,
        down_other,
    )


def solution(mesh):
    split = Mesh(mesh.devices.reshape(4, 8, 4, mesh.shape["mp"]), ("x", "z", "y", "mp"))
    placed = (
        P(SEQ, None),
        P(None, None, "mp"),
        P("mp", None),
        P(None, "mp"),
        P("mp", None),
        P(),
        P(),
        P(),
        P("mp", SEQ, None, None),
        P("mp", SEQ, None, None),
    )
    return jax.shard_map(shards, mesh=split, in_specs=placed, out_specs=P(SEQ, None), check_vma=False)
```

```python
import functools

import jax
import jax.numpy as jnp
from jax import lax
from jax.experimental import pallas as pl
from jax.experimental.pallas import tpu as pltpu
from jax.sharding import Mesh
from jax.sharding import PartitionSpec as P

SEQ = ("x", "z", "y")
PLANE = ("x", "y")
EPSILON = 1e-05
NEGATIVE = -1e30
HEADS = 6
BF16 = jnp.bfloat16
F32 = jnp.float32
LIMIT = 48 * 1024 * 1024
VMEM = pl.BlockSpec(memory_space=pltpu.VMEM)
SMEM = pl.BlockSpec(memory_space=pltpu.SMEM)


def nt(a, b):
    return lax.dot_general(a, b, (((1,), (1,)), ((), ())), preferred_element_type=F32)


def nn(a, b):
    return jnp.dot(a, b, preferred_element_type=F32)


def call(kernel, outs, in_specs, out_specs, scratch, cost, *args):
    return pl.pallas_call(
        kernel,
        out_shape=outs,
        in_specs=in_specs,
        out_specs=out_specs,
        scratch_shapes=scratch,
        cost_estimate=pl.CostEstimate(flops=cost[0], bytes_accessed=cost[1], transcendentals=cost[2]),
        compiler_params=pltpu.CompilerParams(vmem_limit_bytes=LIMIT),
    )(*args)


def prepare_kernel(states_ref, weight_ref, wq_ref, wkv_ref, q_ref, kv_ref):
    wq_ref[...] = jnp.zeros_like(wq_ref)
    for h in range(HEADS):
        part = slice(64 * h, 64 * h + 64)
        wq_ref[:, 128 * h : 128 * h + 64] = weight_ref[0, :, part] * BF16(0.125)
        wkv_ref[:, 128 * h : 128 * h + 64] = weight_ref[1, :, part]
        wkv_ref[:, 128 * h + 64 : 128 * h + 128] = weight_ref[2, :, part]
    states = states_ref[...]
    query = nn(states, wq_ref[...]).astype(BF16)
    pair = nn(states, wkv_ref[...]).astype(BF16)
    for h in range(HEADS):
        q_ref[h] = query[:, 128 * h : 128 * h + 128]
        kv_ref[h] = pair[:, 128 * h : 128 * h + 128]


def prepare(states, weight):
    shape = jax.ShapeDtypeStruct
    return call(
        prepare_kernel,
        (shape((768, 768), BF16), shape((768, 768), BF16), shape((HEADS, 256, 128), BF16), shape((HEADS, 256, 128), BF16)),
        [VMEM] * 2,
        [VMEM] * 4,
        [],
        (600_000_000, 6_000_000, 0),
        states,
        weight,
    )


def early_kernel(*refs):
    wkv_ref, kv_ref = refs[10:]
    for p in range(10):
        pair = nn(refs[p][...], wkv_ref[...]).astype(BF16)
        for h in range(HEADS):
            kv_ref[p, h] = pair[:, 128 * h : 128 * h + 128]


def early(pieces, wkv):
    return call(
        early_kernel,
        jax.ShapeDtypeStruct((10, HEADS, 128, 128), BF16),
        [VMEM] * 11,
        VMEM,
        [],
        (1_500_000_000, 5_000_000, 0),
        *pieces,
        wkv,
    )


def scatter_kernel(*refs):
    wanted_ref, where_ref, out_ref, rows_ref, sem = refs[16:]
    for g in range(2):
        for p in range(16):

            @pl.when(where_ref[0, 2 * g] == p)
            def _():
                start = pl.multiple_of(where_ref[0, 2 * g + 1] * 64, 64)
                pltpu.make_async_copy(refs[p].at[pl.ds(start, 64), :], rows_ref.at[pl.ds(g * 64, 64), :], sem.at[g]).start()

    for g in range(2):
        pltpu.make_async_copy(refs[0].at[pl.ds(0, 64), :], rows_ref.at[pl.ds(g * 64, 64), :], sem.at[g]).wait()
    for p in range(16):
        for c in range(3):
            lanes = (p % 2) * 384 + c * 128
            out_ref[p, 16 * c : 16 * c + 16, :] = rows_ref[p // 2 * 16 : p // 2 * 16 + 16, lanes : lanes + 128]
        out_ref[p, 48:64, :] = jnp.broadcast_to(wanted_ref[p : p + 1, :], (16, 128)).astype(BF16)


def scatter(pieces, wanted, where):
    return call(
        scatter_kernel,
        jax.ShapeDtypeStruct((16, 64, 128), BF16),
        [pl.BlockSpec(memory_space=pl.ANY)] * 16 + [VMEM, SMEM],
        VMEM,
        [pltpu.VMEM((128, 768), BF16), pltpu.SemaphoreType.DMA((2,))],
        (0, 700_000, 0),
        *pieces,
        wanted,
        where,
    )


def column_kernel(*refs):
    wkv_ref, early_ref, received_ref, wanted_ref, kv_ref, items_ref, sem = refs[6:]
    copy = pltpu.make_async_copy(early_ref, kv_ref.at[pl.ds(0, 10 * HEADS)], sem)
    copy.start()
    for p in range(6):
        pair = nn(refs[p][...], wkv_ref[...]).astype(BF16)
        for h in range(HEADS):
            kv_ref[(10 + p) * HEADS + h] = pair[:, 128 * h : 128 * h + 128]
    copy.wait()
    share = received_ref[wanted_ref[0, 256], 0:48, :]
    for p in range(16):
        items_ref[p, 1024:1072, :] = share

    @pl.loop(0, 16)
    def _(p):
        for k in range(16):
            item = wanted_ref[0, p * 16 + k]
            at = pl.multiple_of((item & 1) * 64, 64)
            items_ref[p, 64 * k : 64 * k + 64, :] = kv_ref[item >> 1, pl.ds(at, 64), :]


def column(pieces, wkv, first, received, wanted):
    shape = jax.ShapeDtypeStruct
    return call(
        column_kernel,
        (shape((16 * HEADS, 128, 128), BF16), shape((16, 1072, 128), BF16)),
        [VMEM] * 7 + [pl.BlockSpec(memory_space=pl.ANY), VMEM, SMEM],
        [VMEM, VMEM],
        [pltpu.SemaphoreType.DMA],
        (1_000_000_000, 12_000_000, 0),
        *pieces,
        wkv,
        first,
        received,
        wanted,
    )


def partial_kernel(remote_ref, wq_ref, wkv_ref, kv_ref, out_ref, pair_ref, share_ref, rows_ref, q_ref, s_ref, sem):
    copies = [pltpu.make_async_copy(remote_ref.at[p, pl.ds(1024, 48), :], share_ref.at[p], sem.at[p]) for p in range(16)]
    for copy in copies:
        copy.start()
    for p, copy in enumerate(copies):
        copy.wait()
        for c in range(3):
            lanes = (p % 2) * 384 + c * 128
            rows_ref[p // 2 * 16 : p // 2 * 16 + 16, lanes : lanes + 128] = share_ref[p, 16 * c : 16 * c + 16, :]
    query = nn(rows_ref[...], wq_ref[...]).astype(BF16)
    pair = nn(rows_ref[...], wkv_ref[...]).astype(BF16)
    for h in range(HEADS):
        q_ref[h] = query[:, 128 * h : 128 * h + 128]
        pair_ref[h] = pair[:, 128 * h : 128 * h + 128]
    lane = lax.broadcasted_iota(jnp.int32, (128, 128), 1)
    highs = jnp.zeros((128, 128), F32)
    totals = jnp.zeros((128, 128), F32)
    for h in range(HEADS):
        keys = [kv_ref[4 * c : 4 * c + 4, h].reshape(512, 128) for c in range(4)]
        high = jnp.full((128, 1), NEGATIVE, F32)
        for c in range(4):
            s = nt(q_ref[h], keys[c])
            s_ref[h % 2, :, c * 512 : c * 512 + 512] = s
            high = jnp.maximum(high, jnp.max(s, axis=1, keepdims=True))
        total = jnp.zeros((128, 1), F32)
        acc = jnp.zeros((128, 128), F32)
        for c in range(4):
            p = jnp.exp(s_ref[h % 2, :, c * 512 : c * 512 + 512] - high)
            total = total + jnp.sum(p, axis=1, keepdims=True)
            head = p.astype(BF16)
            rest = (p - head.astype(F32)).astype(BF16)
            acc = acc + nn(head, keys[c]) + nn(rest, keys[c])
        out_ref[:, 64 * h : 64 * h + 64] = acc[:, 64:128]
        highs = jnp.where(lane == h, high, highs)
        totals = jnp.where(lane == h, total, totals)
    out_ref[:, 384:512] = highs
    out_ref[:, 512:640] = totals


def partial(remote, wq, wkv, kv):
    shape = jax.ShapeDtypeStruct
    return call(
        partial_kernel,
        (shape((128, 640), F32), shape((HEADS, 128, 128), BF16)),
        [pl.BlockSpec(memory_space=pl.ANY)] + [VMEM] * 3,
        [VMEM] * 2,
        [
            pltpu.VMEM((16, 48, 128), BF16),
            pltpu.VMEM((128, 768), BF16),
            pltpu.VMEM((HEADS, 128, 128), BF16),
            pltpu.VMEM((2, 128, 2048), F32),
            pltpu.SemaphoreType.DMA((16,)),
        ],
        (2_000_000_000, 5_000_000, 1_600_000),
        remote,
        wq,
        wkv,
        kv,
    )


def merge_kernel(parts_ref, out_ref):
    highs = parts_ref[:, :, 384:512]
    factor = jnp.exp(highs - jnp.max(highs, axis=0, keepdims=True))
    total = jnp.sum(factor * parts_ref[:, :, 512:640], axis=0)
    outs = []
    for h in range(HEADS):
        acc = jnp.sum(parts_ref[:, :, 64 * h : 64 * h + 64] * factor[:, :, h : h + 1], axis=0)
        outs.append(acc / total[:, h : h + 1])
    rows = jnp.concatenate(outs, axis=1).astype(BF16)
    for p in range(32):
        out_ref[p] = rows


def merge(parts):
    return call(
        merge_kernel,
        jax.ShapeDtypeStruct((32, 8, 384), BF16),
        [VMEM],
        VMEM,
        [],
        (2_000_000, 600_000, 10_000),
        parts,
    )


def attend_kernel(q_ref, kv_ref, before_ref, after_ref, wkv_ref, remote_ref, pair_ref, slot_ref, edge_ref, out_ref, ext_ref, keys_ref):
    before = nn(before_ref[...], wkv_ref[...]).astype(BF16)
    after = nn(after_ref[...], wkv_ref[...]).astype(BF16)
    for h in range(HEADS):
        ext_ref[h, 0:64, :] = before[:, 128 * h : 128 * h + 128]
        ext_ref[h, 64:320, :] = kv_ref[h]
        ext_ref[h, 320:384, :] = after[:, 128 * h : 128 * h + 128]
    lane = lax.broadcasted_iota(jnp.int32, (64, 512), 1)

    @pl.loop(0, HEADS // 2)
    def _(pair):
        for b in range(4):
            outs = []
            for k in range(2):
                h = pair * 2 + k
                buf = keys_ref.at[b * 2 + k]
                buf[0:192, :] = ext_ref[h, b * 64 : b * 64 + 192, :]
                for r in range(3):
                    at = pl.multiple_of(slot_ref[0, (b * HEADS + h) * 3 + r], 16)
                    buf[192 + 64 * r : 256 + 64 * r, :] = remote_ref[pl.ds(at, 64), :]
                buf[384:512, :] = pair_ref[h]
                keys = buf[...]
                s = nt(q_ref[h, b * 64 : b * 64 + 64, :], keys)
                if b == 0:
                    s = jnp.where((lane < 64) & (edge_ref[0, 0] > 0), NEGATIVE, s)
                if b == 3:
                    s = jnp.where((lane >= 128) & (lane < 192) & (edge_ref[0, 1] > 0), NEGATIVE, s)
                p = jnp.exp(s - jnp.max(s, axis=1, keepdims=True))
                w = (p / jnp.sum(p, axis=1, keepdims=True)).astype(BF16)
                outs.append(nn(w, keys)[:, 64:128])
            lanes = pl.ds(pl.multiple_of(pair * 128, 128), 128)
            out_ref[b * 64 : b * 64 + 64, lanes] = jnp.concatenate(outs, axis=1).astype(BF16)


def attend(q, kv, before, after, wkv, remote, pair, slots, edges):
    return call(
        attend_kernel,
        jax.ShapeDtypeStruct((256, 384), BF16),
        [VMEM] * 7 + [SMEM] * 2,
        VMEM,
        [pltpu.VMEM((HEADS, 384, 128), BF16), pltpu.VMEM((8, 512, 128), BF16)],
        (600_000_000, 7_000_000, 800_000),
        q,
        kv,
        before,
        after,
        wkv,
        remote,
        pair,
        slots,
        edges,
    )


def norm(v, gain):
    shifted = v - jnp.mean(v, axis=1, keepdims=True)
    spread = jnp.mean(shifted * shifted, axis=1, keepdims=True)
    return shifted * lax.rsqrt(spread + EPSILON) * gain


CHUNK = 512
STEPS = 1536 // CHUNK


def finish_kernel(
    own_ref,
    other_ref,
    states_ref,
    wo_own,
    wo_other,
    gain_ref,
    gain2_ref,
    up_own,
    up_other,
    down_own,
    down_other,
    rows_ref,
    place_ref,
    out_ref,
    normed_ref,
    sum_ref,
    attended_ref,
):
    step = pl.program_id(0)

    @pl.when(step == 0)
    def _():
        attended_ref[0] = own_ref[...]
        attended_ref[1] = other_ref[...]
        core = place_ref[0, 2]
        for g in range(2):

            @pl.when(place_ref[0, g] >= 0)
            def _():
                for k, side in ((0, core), (1, 1 - core)):
                    for i in range(4):
                        first = (g * 8 + 2 * i) * 2 + side
                        at = pl.multiple_of(place_ref[0, g] * 64 + 16 * i, 16)
                        both = jnp.concatenate([rows_ref[first], rows_ref[first + 2]], axis=0)
                        attended_ref[k, pl.ds(at, 16), :] = both

        projected = nn(attended_ref[0], wo_own[...]) + nn(attended_ref[1], wo_other[...])
        normed_ref[...] = norm(states_ref[...].astype(F32) + projected, gain_ref[...]).astype(BF16)
        sum_ref[...] = jnp.zeros_like(sum_ref)

    def half(k, up, down):
        v = nn(normed_ref[...], up[...])
        hidden = (v * (1.0 + lax.erf(v * 0.7071067811865476)) * 0.5).astype(BF16)
        sum_ref[k] += nn(hidden, down[...])

    @pl.when(step < STEPS)
    def _():
        half(0, up_own, down_own)

    @pl.when(step >= STEPS)
    def _():
        half(1, up_other, down_other)

    @pl.when(step == 2 * STEPS - 1)
    def _():
        total = normed_ref[...].astype(F32) + (sum_ref[0] + sum_ref[1])
        out_ref[...] = norm(total, gain2_ref[...]).astype(BF16)


def finish(own, other, states, wo_own, wo_other, gain, gain2, up_own, up_other, down_own, down_other, rows, where):
    whole = lambda *shape: pl.BlockSpec(shape, lambda s: (0, 0), pipeline_mode=pl.Buffered(1))
    first = lambda s: jnp.minimum(s, STEPS - 1)
    second = lambda s: jnp.maximum(s - STEPS, 0)
    return pl.pallas_call(
        finish_kernel,
        out_shape=jax.ShapeDtypeStruct((256, 768), BF16),
        grid=(2 * STEPS,),
        in_specs=[
            whole(256, 384),
            whole(256, 384),
            whole(256, 768),
            whole(384, 768),
            whole(384, 768),
            whole(1, 768),
            whole(1, 768),
            pl.BlockSpec((768, CHUNK), lambda s: (0, first(s))),
            pl.BlockSpec((768, CHUNK), lambda s: (0, second(s))),
            pl.BlockSpec((CHUNK, 768), lambda s: (first(s), 0)),
            pl.BlockSpec((CHUNK, 768), lambda s: (second(s), 0)),
            pl.BlockSpec((32, 8, 384), lambda s: (0, 0, 0), pipeline_mode=pl.Buffered(1)),
            SMEM,
        ],
        out_specs=pl.BlockSpec((256, 768), lambda s: (0, 0)),
        scratch_shapes=[pltpu.VMEM((256, 768), BF16), pltpu.VMEM((2, 256, 768), F32), pltpu.VMEM((2, 256, 384), BF16)],
        cost_estimate=pl.CostEstimate(flops=2_700_000_000, bytes_accessed=12_000_000, transcendentals=800_000),
        compiler_params=pltpu.CompilerParams(dimension_semantics=("arbitrary",), vmem_limit_bytes=LIMIT),
    )(own, other, states, wo_own, wo_other, gain, gain2, up_own, up_other, down_own, down_other, rows, where)


def turned(value, axis, shift):
    count = lax.axis_size(axis)
    return lax.ppermute(value, axis, [(i, (i + shift) % count) for i in range(count)])


def exchanged(value, axes):
    return lax.all_to_all(value, axes, split_axis=0, concat_axis=0, tiled=True)


def swapped(value):
    return lax.ppermute(value, "mp", [(0, 1), (1, 0)])


def shards(
    states, qkv_weight, out_weight, up_weight, down_weight, attn_gain, mlp_gain, global_ids, random_owner, random_local
):
    here = {axis: lax.axis_index(axis) for axis in ("x", "z", "y", "mp")}
    core = here["mp"]
    seq = (here["x"] * 8 + here["z"]) * 4 + here["y"]

    mine = lax.dynamic_slice_in_dim(states, core * 128, 128, 0)
    ups, downs = [mine], [mine]
    for _ in range(4):
        ups.append(turned(ups[-1], "z", 1))
    for _ in range(3):
        downs.append(turned(downs[-1], "z", -1))
    first = [ups[0], ups[1], ups[2], downs[1], downs[2]]
    last = [ups[3], ups[4], downs[3]]
    first = first + [swapped(piece) for piece in first]
    last = last + [swapped(piece) for piece in last]

    owner = random_owner.reshape(-1)
    local = random_local.reshape(-1)
    head = jnp.broadcast_to(jnp.arange(HEADS, dtype=jnp.int32)[None, :, None], (4, HEADS, 3)).reshape(-1)

    def piece_of(block_owner, block_local):
        away = (here["z"] - ((block_owner >> 2) & 7)) & 7
        far = ((block_local >> 1) != core).astype(jnp.int32)
        soon = far * 5 + jnp.where(away >= 6, 10 - away, away)
        return jnp.where((away >= 3) & (away <= 5), 10 + far * 3 + away - 3, soon)

    item = (piece_of(owner, local) * HEADS + head) * 2 + (local & 1)
    group = (owner >> 5) * 4 + (owner & 3)
    number = jnp.arange(owner.shape[0], dtype=jnp.int32)
    same = (group[:, None] == group[None, :]) & (number[None, :] < number[:, None])
    rank = jnp.sum(same.astype(jnp.int32), axis=1)
    slots = group * 1072 + rank * 64
    lanes = jnp.arange(2048, dtype=jnp.int32)
    chosen = (group * 128 + rank)[:, None] == lanes[None, :]
    wanted = jnp.sum(jnp.where(chosen, item[:, None], 0), axis=0).astype(F32).reshape(16, 128)

    root_owner, root_local = global_ids >> 2, global_ids & 3
    pieces = piece_of(root_owner, root_local)
    where = jnp.stack([pieces[0], root_local[0] & 1, pieces[1], root_local[1] & 1]).reshape(1, 4)
    received = exchanged(scatter(first + last, wanted, where), PLANE)
    root = (root_owner >> 5) * 4 + (root_owner & 3)
    source = jnp.where(here["x"] >= 2, root[1], root[0])
    wanted = jnp.concatenate([received[:, 48, :16].astype(jnp.int32).reshape(-1), source[None]]).reshape(1, 257)

    ends = [(i, i + 1) for i in range(127)]
    before = lax.ppermute(states[192:], SEQ, ends)
    after = lax.ppermute(states[:64], SEQ, [(j, i) for i, j in ends])
    wo_other, up_other, down_other = swapped(out_weight), swapped(up_weight), swapped(down_weight)

    wq, wkv, q, kv = prepare(states, qkv_weight)
    pairs, items = column(last, wkv, early(first, wkv).reshape(10 * HEADS, 128, 128), received, wanted)
    remote = exchanged(items, PLANE)
    part, pair = partial(remote, wq, wkv, pairs.reshape(16, HEADS, 128, 128))
    rows = exchanged(merge(exchanged(part.reshape(16, 8, 640), PLANE)), PLANE + ("mp",))

    edges = jnp.stack([seq == 0, seq == 127]).astype(jnp.int32).reshape(1, 2)
    attended = attend(q, kv, before, after, wkv, remote.reshape(16 * 1072, 128), pair, slots.reshape(1, -1), edges)
    block = jnp.where(root_owner == seq, root_local, -1)
    where = jnp.concatenate([block, core[None]]).astype(jnp.int32).reshape(1, 3)
    return finish(
        attended,
        swapped(attended),
        states,
        out_weight,
        wo_other,
        attn_gain.reshape(1, -1),
        mlp_gain.reshape(1, -1),
        up_weight,
        up_other,
        down_weight,
        down_other,
        rows,
        where,
    )


def solution(mesh):
    split = Mesh(mesh.devices.reshape(4, 8, 4, mesh.shape["mp"]), ("x", "z", "y", "mp"))
    placed = (
        P(SEQ, None),
        P(None, None, "mp"),
        P("mp", None),
        P(None, "mp"),
        P("mp", None),
        P(),
        P(),
        P(),
        P("mp", SEQ, None, None),
        P("mp", SEQ, None, None),
    )
    return jax.shard_map(shards, mesh=split, in_specs=placed, out_specs=P(SEQ, None), check_vma=False)
```

```python
import functools

import jax
import jax.numpy as jnp
from jax import lax
from jax.experimental import pallas as pl
from jax.experimental.pallas import tpu as pltpu
from jax.sharding import Mesh
from jax.sharding import PartitionSpec as P

SEQ = ("x", "z", "y")
PLANE = ("x", "y")
EPSILON = 1e-05
NEGATIVE = -1e30
HEADS = 6
BF16 = jnp.bfloat16
F32 = jnp.float32
LIMIT = 56 * 1024 * 1024
FAR = pl.BlockSpec(memory_space=pltpu.HBM)
SMEM = pl.BlockSpec(memory_space=pltpu.SMEM)


def nt(a, b):
    return lax.dot_general(a, b, (((1,), (1,)), ((), ())), preferred_element_type=F32)


def nn(a, b):
    return jnp.dot(a, b, preferred_element_type=F32)


def call(kernel, outs, scratch, cost, arrays, scalars=(), by_hand=()):
    single = not isinstance(outs, tuple)
    results = (outs,) if single else outs
    count, total = len(arrays), len(arrays) + len(scalars)

    def body(*refs):
        inputs, tables = refs[:count], refs[count:total]
        outputs = refs[total : total + len(results)]
        held = refs[total + len(results) :]
        near, made, (sem_in, sem_out), rest = (
            held[:count],
            held[count : count + len(results)],
            held[count + len(results) : count + len(results) + 2],
            held[count + len(results) + 2 :],
        )
        copies = [pltpu.make_async_copy(inputs[i], near[i], sem_in.at[i]) for i in range(count)]
        for copy in copies:
            copy.start()
        for copy in copies:
            copy.wait()
        kernel(*near, *tables, *made, *[outputs[i] for i in by_hand], *rest)
        copies = [pltpu.make_async_copy(made[i], outputs[i], sem_out.at[i]) for i in range(len(results)) if i not in by_hand]
        for copy in copies:
            copy.start()
        for copy in copies:
            copy.wait()

    made = pl.pallas_call(
        body,
        out_shape=results,
        in_specs=[FAR] * count + [SMEM] * len(scalars),
        out_specs=(FAR,) * len(results),
        scratch_shapes=[pltpu.VMEM(v.shape, v.dtype) for v in (*arrays, *results)]
        + [pltpu.SemaphoreType.DMA((count,)), pltpu.SemaphoreType.DMA((len(results),))]
        + list(scratch),
        cost_estimate=pl.CostEstimate(flops=cost[0], bytes_accessed=cost[1], transcendentals=cost[2]),
        compiler_params=pltpu.CompilerParams(vmem_limit_bytes=LIMIT),
    )(*arrays, *scalars)
    return made[0] if single else made


def prepare_kernel(states_ref, weight_ref, wq_ref, wkv_ref, q_ref, kv_ref):
    wq_ref[...] = jnp.zeros_like(wq_ref)
    for h in range(HEADS):
        part = slice(64 * h, 64 * h + 64)
        wq_ref[:, 128 * h : 128 * h + 64] = weight_ref[0, :, part] * BF16(0.125)
        wkv_ref[:, 128 * h : 128 * h + 64] = weight_ref[1, :, part]
        wkv_ref[:, 128 * h + 64 : 128 * h + 128] = weight_ref[2, :, part]
    states = states_ref[...]
    query = nn(states, wq_ref[...]).astype(BF16)
    pair = nn(states, wkv_ref[...]).astype(BF16)
    for h in range(HEADS):
        q_ref[h] = query[:, 128 * h : 128 * h + 128]
        kv_ref[h] = pair[:, 128 * h : 128 * h + 128]


def prepare(states, weight):
    shape = jax.ShapeDtypeStruct
    return call(
        prepare_kernel,
        (shape((768, 768), BF16), shape((768, 768), BF16), shape((HEADS, 256, 128), BF16), shape((HEADS, 256, 128), BF16)),
        [],
        (600_000_000, 6_000_000, 0),
        [states, weight],
    )


def early_kernel(*refs):
    wkv_ref, kv_ref = refs[10:]
    for p in range(10):
        pair = nn(refs[p][...], wkv_ref[...]).astype(BF16)
        for h in range(HEADS):
            kv_ref[p, h] = pair[:, 128 * h : 128 * h + 128]


def early(pieces, wkv):
    return call(
        early_kernel,
        jax.ShapeDtypeStruct((10, HEADS, 128, 128), BF16),
        [],
        (1_500_000_000, 5_000_000, 0),
        [*pieces, wkv],
    )


def scatter_kernel(*refs):
    wanted_ref, where_ref, out_ref, rows_ref = refs[16:]
    for g in range(2):
        for p in range(16):

            @pl.when(where_ref[0, 2 * g] == p)
            def _():
                start = pl.multiple_of(where_ref[0, 2 * g + 1] * 64, 64)
                rows_ref[64 * g : 64 * g + 64, :] = refs[p][pl.ds(start, 64), :]

    for p in range(16):
        for c in range(3):
            lanes = (p % 2) * 384 + c * 128
            out_ref[p, 16 * c : 16 * c + 16, :] = rows_ref[p // 2 * 16 : p // 2 * 16 + 16, lanes : lanes + 128]
        out_ref[p, 48:64, :] = jnp.broadcast_to(wanted_ref[p : p + 1, :], (16, 128)).astype(BF16)


def scatter(pieces, wanted, where):
    return call(
        scatter_kernel,
        jax.ShapeDtypeStruct((16, 64, 128), BF16),
        [pltpu.VMEM((128, 768), BF16)],
        (0, 4_000_000, 0),
        [*pieces, wanted],
        [where],
    )


def column_kernel(*refs):
    wkv_ref, early_ref, received_ref, wanted_ref, kv_ref, items_ref, out_ref, sem, sems = refs[6:]
    copy = pltpu.make_async_copy(early_ref, kv_ref.at[pl.ds(0, 10 * HEADS)], sem)
    copy.start()
    for p in range(6):
        pair = nn(refs[p][...], wkv_ref[...]).astype(BF16)
        for h in range(HEADS):
            kv_ref[(10 + p) * HEADS + h] = pair[:, 128 * h : 128 * h + 128]
    copy.wait()
    share = received_ref[wanted_ref[0, 256], 0:48, :]
    for p in range(16):
        items_ref[p, 1024:1072, :] = share

    @pl.loop(0, 16)
    def _(p):
        for k in range(16):
            item = wanted_ref[0, p * 16 + k]
            at = pl.multiple_of((item & 1) * 64, 64)
            items_ref[p, 64 * k : 64 * k + 64, :] = kv_ref[item >> 1, pl.ds(at, 64), :]
        pltpu.make_async_copy(items_ref.at[p], out_ref.at[p], sems.at[p]).start()

    @pl.loop(0, 16)
    def _(p):
        pltpu.make_async_copy(items_ref.at[p], out_ref.at[p], sems.at[p]).wait()


def column(pieces, wkv, first, received, wanted):
    shape = jax.ShapeDtypeStruct
    return call(
        column_kernel,
        (shape((16 * HEADS, 128, 128), BF16), shape((16, 1072, 128), BF16)),
        [pltpu.SemaphoreType.DMA, pltpu.SemaphoreType.DMA((16,))],
        (1_000_000_000, 12_000_000, 0),
        [*pieces, wkv, first, received],
        [wanted],
        by_hand=(1,),
    )


def partial_kernel(remote_ref, wq_ref, wkv_ref, kv_ref, out_ref, pair_ref, rows_ref, q_ref, s_ref):
    for p in range(16):
        for c in range(3):
            lanes = (p % 2) * 384 + c * 128
            rows_ref[p // 2 * 16 : p // 2 * 16 + 16, lanes : lanes + 128] = remote_ref[p, 1024 + 16 * c : 1040 + 16 * c, :]
    query = nn(rows_ref[...], wq_ref[...]).astype(BF16)
    pair = nn(rows_ref[...], wkv_ref[...]).astype(BF16)
    for h in range(HEADS):
        q_ref[h] = query[:, 128 * h : 128 * h + 128]
        pair_ref[h] = pair[:, 128 * h : 128 * h + 128]
    lane = lax.broadcasted_iota(jnp.int32, (128, 128), 1)
    highs = jnp.zeros((128, 128), F32)
    totals = jnp.zeros((128, 128), F32)
    for h in range(HEADS):
        keys = [kv_ref[4 * c : 4 * c + 4, h].reshape(512, 128) for c in range(4)]
        high = jnp.full((128, 1), NEGATIVE, F32)
        for c in range(4):
            s = nt(q_ref[h], keys[c])
            s_ref[h % 2, :, c * 512 : c * 512 + 512] = s
            high = jnp.maximum(high, jnp.max(s, axis=1, keepdims=True))
        total = jnp.zeros((128, 1), F32)
        acc = jnp.zeros((128, 128), F32)
        for c in range(4):
            p = jnp.exp(s_ref[h % 2, :, c * 512 : c * 512 + 512] - high)
            total = total + jnp.sum(p, axis=1, keepdims=True)
            head = p.astype(BF16)
            rest = (p - head.astype(F32)).astype(BF16)
            acc = acc + nn(head, keys[c]) + nn(rest, keys[c])
        out_ref[:, 64 * h : 64 * h + 64] = acc[:, 64:128]
        highs = jnp.where(lane == h, high, highs)
        totals = jnp.where(lane == h, total, totals)
    out_ref[:, 384:512] = highs
    out_ref[:, 512:640] = totals


def partial(remote, wq, wkv, kv):
    shape = jax.ShapeDtypeStruct
    return call(
        partial_kernel,
        (shape((128, 640), F32), shape((HEADS, 128, 128), BF16)),
        [
            pltpu.VMEM((128, 768), BF16),
            pltpu.VMEM((HEADS, 128, 128), BF16),
            pltpu.VMEM((2, 128, 2048), F32),
        ],
        (2_000_000_000, 10_000_000, 1_600_000),
        [remote, wq, wkv, kv],
    )


def merge_kernel(parts_ref, out_ref):
    highs = parts_ref[:, :, 384:512]
    factor = jnp.exp(highs - jnp.max(highs, axis=0, keepdims=True))
    total = jnp.sum(factor * parts_ref[:, :, 512:640], axis=0)
    outs = []
    for h in range(HEADS):
        acc = jnp.sum(parts_ref[:, :, 64 * h : 64 * h + 64] * factor[:, :, h : h + 1], axis=0)
        outs.append(acc / total[:, h : h + 1])
    rows = jnp.concatenate(outs, axis=1).astype(BF16)
    for p in range(32):
        out_ref[p] = rows


def merge(parts):
    return call(
        merge_kernel,
        jax.ShapeDtypeStruct((32, 8, 384), BF16),
        [],
        (2_000_000, 600_000, 10_000),
        [parts],
    )


def attend_kernel(q_ref, kv_ref, before_ref, after_ref, wkv_ref, remote_ref, pair_ref, slot_ref, edge_ref, out_ref, ext_ref, keys_ref):
    before = nn(before_ref[...], wkv_ref[...]).astype(BF16)
    after = nn(after_ref[...], wkv_ref[...]).astype(BF16)
    for h in range(HEADS):
        ext_ref[h, 0:64, :] = before[:, 128 * h : 128 * h + 128]
        ext_ref[h, 64:320, :] = kv_ref[h]
        ext_ref[h, 320:384, :] = after[:, 128 * h : 128 * h + 128]
    lane = lax.broadcasted_iota(jnp.int32, (64, 512), 1)

    @pl.loop(0, HEADS // 2)
    def _(pair):
        for b in range(4):
            outs = []
            for k in range(2):
                h = pair * 2 + k
                buf = keys_ref.at[b * 2 + k]
                buf[0:192, :] = ext_ref[h, b * 64 : b * 64 + 192, :]
                for r in range(3):
                    at = pl.multiple_of(slot_ref[0, (b * HEADS + h) * 3 + r], 16)
                    buf[192 + 64 * r : 256 + 64 * r, :] = remote_ref[pl.ds(at, 64), :]
                buf[384:512, :] = pair_ref[h]
                keys = buf[...]
                s = nt(q_ref[h, b * 64 : b * 64 + 64, :], keys)
                if b == 0:
                    s = jnp.where((lane < 64) & (edge_ref[0, 0] > 0), NEGATIVE, s)
                if b == 3:
                    s = jnp.where((lane >= 128) & (lane < 192) & (edge_ref[0, 1] > 0), NEGATIVE, s)
                p = jnp.exp(s - jnp.max(s, axis=1, keepdims=True))
                w = (p / jnp.sum(p, axis=1, keepdims=True)).astype(BF16)
                outs.append(nn(w, keys)[:, 64:128])
            lanes = pl.ds(pl.multiple_of(pair * 128, 128), 128)
            out_ref[b * 64 : b * 64 + 64, lanes] = jnp.concatenate(outs, axis=1).astype(BF16)


def attend(q, kv, before, after, wkv, remote, pair, slots, edges):
    return call(
        attend_kernel,
        jax.ShapeDtypeStruct((256, 384), BF16),
        [pltpu.VMEM((HEADS, 384, 128), BF16), pltpu.VMEM((8, 512, 128), BF16)],
        (600_000_000, 7_000_000, 800_000),
        [q, kv, before, after, wkv, remote, pair],
        [slots, edges],
    )


def norm(v, gain):
    shifted = v - jnp.mean(v, axis=1, keepdims=True)
    spread = jnp.mean(shifted * shifted, axis=1, keepdims=True)
    return shifted * lax.rsqrt(spread + EPSILON) * gain


CHUNK = 512


def finish_kernel(
    own_ref,
    other_ref,
    states_ref,
    wo_own,
    wo_other,
    gain_ref,
    gain2_ref,
    rows_ref,
    up_own,
    up_other,
    down_own,
    down_other,
    place_ref,
    out_ref,
    attended,
    states,
    wo,
    gains,
    rows,
    up,
    down,
    sums,
    result,
    sem,
    sems,
):
    copies = [
        pltpu.make_async_copy(source, target, sem.at[i])
        for i, (source, target) in enumerate(
            [
                (own_ref, attended.at[0]),
                (other_ref, attended.at[1]),
                (rows_ref, rows),
                (wo_own, wo.at[0]),
                (wo_other, wo.at[1]),
                (states_ref, states),
                (gain_ref, gains.at[0]),
                (gain2_ref, gains.at[1]),
            ]
        )
    ]
    chunks = []
    for half, (above, below) in enumerate(((up_own, down_own), (up_other, down_other))):
        for i in range(0, 1536, CHUNK):
            number = len(chunks)
            part = pl.ds(i, CHUNK)
            chunks.append(
                (
                    pltpu.make_async_copy(above.at[:, part], up.at[number], sems.at[2 * number]),
                    pltpu.make_async_copy(below.at[part, :], down.at[number], sems.at[2 * number + 1]),
                )
            )
    for copy in copies:
        copy.start()
    for chunk in chunks:
        chunk[0].start()
        chunk[1].start()
    for copy in copies:
        copy.wait()
    core = place_ref[0, 2]
    for g in range(2):

        @pl.when(place_ref[0, g] >= 0)
        def _():
            for k, side in ((0, core), (1, 1 - core)):
                for i in range(4):
                    first = (g * 8 + 2 * i) * 2 + side
                    at = pl.multiple_of(place_ref[0, g] * 64 + 16 * i, 16)
                    attended[k, pl.ds(at, 16), :] = jnp.concatenate([rows[first], rows[first + 2]], axis=0)

    projected = nn(attended[0], wo[0]) + nn(attended[1], wo[1])
    normed = norm(states[...].astype(F32) + projected, gains[0]).astype(BF16)
    for number, chunk in enumerate(chunks):
        chunk[0].wait()
        v = nn(normed, up[number])
        hidden = (v * (1.0 + lax.erf(v * 0.7071067811865476)) * 0.5).astype(BF16)
        chunk[1].wait()
        piece = nn(hidden, down[number])
        half = number // (1536 // CHUNK)
        if number % (1536 // CHUNK) == 0:
            sums[half] = piece
        else:
            sums[half] += piece
    result[...] = norm(normed.astype(F32) + (sums[0] + sums[1]), gains[1]).astype(BF16)
    pltpu.sync_copy(result, out_ref)


def finish(own, other, states, wo_own, wo_other, gain, gain2, rows, up_own, up_other, down_own, down_other, where):
    count = 2 * 1536 // CHUNK
    return pl.pallas_call(
        finish_kernel,
        out_shape=jax.ShapeDtypeStruct((256, 768), BF16),
        in_specs=[FAR] * 12 + [SMEM],
        out_specs=FAR,
        scratch_shapes=[
            pltpu.VMEM((2, 256, 384), BF16),
            pltpu.VMEM((256, 768), BF16),
            pltpu.VMEM((2, 384, 768), BF16),
            pltpu.VMEM((2, 1, 768), F32),
            pltpu.VMEM((32, 8, 384), BF16),
            pltpu.VMEM((count, 768, CHUNK), BF16),
            pltpu.VMEM((count, CHUNK, 768), BF16),
            pltpu.VMEM((2, 256, 768), F32),
            pltpu.VMEM((256, 768), BF16),
            pltpu.SemaphoreType.DMA((8,)),
            pltpu.SemaphoreType.DMA((2 * count,)),
        ],
        cost_estimate=pl.CostEstimate(flops=2_700_000_000, bytes_accessed=12_000_000, transcendentals=800_000),
        compiler_params=pltpu.CompilerParams(vmem_limit_bytes=LIMIT),
    )(own, other, states, wo_own, wo_other, gain, gain2, rows, up_own, up_other, down_own, down_other, where)


def turned(value, axis, shift):
    count = lax.axis_size(axis)
    return lax.ppermute(value, axis, [(i, (i + shift) % count) for i in range(count)])


def exchanged(value, axes):
    return lax.all_to_all(value, axes, split_axis=0, concat_axis=0, tiled=True)


def swapped(value):
    return lax.ppermute(value, "mp", [(0, 1), (1, 0)])


def shards(
    states, qkv_weight, out_weight, up_weight, down_weight, attn_gain, mlp_gain, global_ids, random_owner, random_local
):
    here = {axis: lax.axis_index(axis) for axis in ("x", "z", "y", "mp")}
    core = here["mp"]
    seq = (here["x"] * 8 + here["z"]) * 4 + here["y"]

    mine = lax.dynamic_slice_in_dim(states, core * 128, 128, 0)
    ups, downs = [mine], [mine]
    for _ in range(4):
        ups.append(turned(ups[-1], "z", 1))
    for _ in range(3):
        downs.append(turned(downs[-1], "z", -1))
    first = [ups[0], ups[1], ups[2], downs[1], downs[2]]
    last = [ups[3], ups[4], downs[3]]
    first = first + [swapped(piece) for piece in first]
    last = last + [swapped(piece) for piece in last]

    owner = random_owner.reshape(-1)
    local = random_local.reshape(-1)
    head = jnp.broadcast_to(jnp.arange(HEADS, dtype=jnp.int32)[None, :, None], (4, HEADS, 3)).reshape(-1)

    def piece_of(block_owner, block_local):
        away = (here["z"] - ((block_owner >> 2) & 7)) & 7
        far = ((block_local >> 1) != core).astype(jnp.int32)
        soon = far * 5 + jnp.where(away >= 6, 10 - away, away)
        return jnp.where((away >= 3) & (away <= 5), 10 + far * 3 + away - 3, soon)

    item = (piece_of(owner, local) * HEADS + head) * 2 + (local & 1)
    group = (owner >> 5) * 4 + (owner & 3)
    number = jnp.arange(owner.shape[0], dtype=jnp.int32)
    same = (group[:, None] == group[None, :]) & (number[None, :] < number[:, None])
    rank = jnp.sum(same.astype(jnp.int32), axis=1)
    slots = group * 1072 + rank * 64
    lanes = jnp.arange(2048, dtype=jnp.int32)
    chosen = (group * 128 + rank)[:, None] == lanes[None, :]
    wanted = jnp.sum(jnp.where(chosen, item[:, None], 0), axis=0).astype(F32).reshape(16, 128)

    root_owner, root_local = global_ids >> 2, global_ids & 3
    pieces = piece_of(root_owner, root_local)
    where = jnp.stack([pieces[0], root_local[0] & 1, pieces[1], root_local[1] & 1]).reshape(1, 4)
    spread = scatter(first + last, wanted, where)

    ends = [(i, i + 1) for i in range(127)]
    before = lax.ppermute(states[192:], SEQ, ends)
    after = lax.ppermute(states[:64], SEQ, [(j, i) for i, j in ends])
    weights = (swapped(out_weight), swapped(up_weight), swapped(down_weight))
    wq, wkv, q, kv = prepare(states, qkv_weight)
    soon = early(first, wkv).reshape(10 * HEADS, 128, 128)
    spread, soon, before, after, weights = lax.optimization_barrier((spread, soon, before, after, weights))
    wo_other, up_other, down_other = weights

    received = exchanged(spread, PLANE)
    root = (root_owner >> 5) * 4 + (root_owner & 3)
    source = jnp.where(here["x"] >= 2, root[1], root[0])
    wanted = jnp.concatenate([received[:, 48, :16].astype(jnp.int32).reshape(-1), source[None]]).reshape(1, 257)

    pairs, items = column(last, wkv, soon, received, wanted)
    remote = exchanged(items, PLANE)
    part, pair = partial(remote, wq, wkv, pairs.reshape(16, HEADS, 128, 128))
    rows = exchanged(merge(exchanged(part.reshape(16, 8, 640), PLANE)), PLANE + ("mp",))

    edges = jnp.stack([seq == 0, seq == 127]).astype(jnp.int32).reshape(1, 2)
    attended = attend(q, kv, before, after, wkv, remote.reshape(16 * 1072, 128), pair, slots.reshape(1, -1), edges)
    block = jnp.where(root_owner == seq, root_local, -1)
    where = jnp.concatenate([block, core[None]]).astype(jnp.int32).reshape(1, 3)
    return finish(
        attended,
        swapped(attended),
        states,
        out_weight,
        wo_other,
        attn_gain.reshape(1, -1),
        mlp_gain.reshape(1, -1),
        rows,
        up_weight,
        up_other,
        down_weight,
        down_other,
        where,
    )


def solution(mesh):
    split = Mesh(mesh.devices.reshape(4, 8, 4, mesh.shape["mp"]), ("x", "z", "y", "mp"))
    placed = (
        P(SEQ, None),
        P(None, None, "mp"),
        P("mp", None),
        P(None, "mp"),
        P("mp", None),
        P(),
        P(),
        P(),
        P("mp", SEQ, None, None),
        P("mp", SEQ, None, None),
    )
    return jax.shard_map(shards, mesh=split, in_specs=placed, out_specs=P(SEQ, None), check_vma=False)
```

```python
import functools

import jax
import jax.numpy as jnp
from jax import lax
from jax.experimental import pallas as pl
from jax.experimental.pallas import tpu as pltpu
from jax.sharding import Mesh
from jax.sharding import PartitionSpec as P

SEQ = ("x", "z", "y")
PLANE = ("x", "y")
EPSILON = 1e-05
NEGATIVE = -1e30
HEADS = 6
BF16 = jnp.bfloat16
F32 = jnp.float32
LIMIT = 56 * 1024 * 1024
SLOTS = 10
MORE = 16 - SLOTS
STRIDE = SLOTS * 64 + 48
FAR = pl.BlockSpec(memory_space=pltpu.HBM)
SMEM = pl.BlockSpec(memory_space=pltpu.SMEM)


def nt(a, b):
    return lax.dot_general(a, b, (((1,), (1,)), ((), ())), preferred_element_type=F32)


def nn(a, b):
    return jnp.dot(a, b, preferred_element_type=F32)


def call(kernel, outs, scratch, cost, arrays, raw=(), scalars=(), by_hand=(), tables=()):
    single = not isinstance(outs, tuple)
    results = (outs,) if single else outs
    count, total = len(arrays), len(arrays) + len(raw) + len(scalars)

    def body(*refs):
        inputs, others = refs[:count], refs[count:total]
        outputs = refs[total : total + len(results)]
        listed = refs[total + len(results) : total + len(results) + len(tables)]
        held = refs[total + len(results) + len(tables) :]
        near, made, (sem_in, sem_out), rest = (
            held[:count],
            held[count : count + len(results)],
            held[count + len(results) : count + len(results) + 2],
            held[count + len(results) + 2 :],
        )
        copies = [pltpu.make_async_copy(inputs[i], near[i], sem_in.at[i]) for i in range(count)]
        for copy in copies:
            copy.start()
        for copy in copies:
            copy.wait()
        kernel(*near, *others, *made, *[outputs[i] for i in by_hand], *listed, *rest)
        copies = [pltpu.make_async_copy(made[i], outputs[i], sem_out.at[i]) for i in range(len(results)) if i not in by_hand]
        for copy in copies:
            copy.start()
        for copy in copies:
            copy.wait()

    made = pl.pallas_call(
        body,
        out_shape=(*results, *tables),
        in_specs=[FAR] * (count + len(raw)) + [SMEM] * len(scalars),
        out_specs=(FAR,) * len(results) + (SMEM,) * len(tables),
        scratch_shapes=[pltpu.VMEM(v.shape, v.dtype) for v in (*arrays, *results)]
        + [pltpu.SemaphoreType.DMA((count,)), pltpu.SemaphoreType.DMA((len(results),))]
        + list(scratch),
        cost_estimate=pl.CostEstimate(flops=cost[0], bytes_accessed=cost[1], transcendentals=cost[2]),
        compiler_params=pltpu.CompilerParams(vmem_limit_bytes=LIMIT),
    )(*arrays, *raw, *scalars)
    return made[0] if single and not tables else made


def pick(condition, yes, no):
    return jnp.where(condition, yes, no)


def piece_of(owner, local, z, core):
    away = (z - ((owner >> 2) & 7)) & 7
    far = pick((local >> 1) == core, 0, 1)
    first = pick(away == 7, 2, away) + 3 * far
    second = pick(away == 6, 7, 6) + 2 * far
    last = 7 + away + 3 * far
    return pick((away <= 1) | (away == 7), first, pick((away == 2) | (away == 6), second, last))


def prepare_kernel(
    states_ref, weight_ref, owner_ref, local_ref, ids_ref, here_ref, wq_ref, wkv_ref, q_ref, kv_ref, spread_ref, slots_ref, count_ref, rows_ref
):
    z, core = here_ref[0, 1], here_ref[0, 3]
    for g in range(2):
        start = pl.multiple_of((ids_ref[0, g] & 3) * 64, 64)
        rows_ref[64 * g : 64 * g + 64, :] = states_ref[pl.ds(start, 64), :]
    for p in range(16):
        for c in range(3):
            lanes = (p % 2) * 384 + c * 128
            spread_ref[p, 16 * c : 16 * c + 16, :] = rows_ref[p // 2 * 16 : p // 2 * 16 + 16, lanes : lanes + 128]
        count_ref[p] = 0
    line = lax.broadcasted_iota(jnp.int32, (16, 128), 0)
    lane = lax.broadcasted_iota(jnp.int32, (16, 128), 1)
    place = line * 128 + lane
    wanted = jnp.zeros((16, 128), F32)
    most = jnp.int32(0)
    for b in range(4):
        for h in range(HEADS):
            for r in range(3):
                owner, local = owner_ref[0, b, h, r], local_ref[0, b, h, r]
                item = (piece_of(owner, local, z, core) * HEADS + h) * 2 + (local & 1)
                group = ((owner >> 5) << 2) + (owner & 3)
                rank = count_ref[group]
                count_ref[group] = rank + 1
                most = jnp.maximum(most, rank)
                near = group * STRIDE + rank * 64
                beyond = 16 * STRIDE + group * MORE * 64 + (rank - SLOTS) * 64
                slots_ref[0, (b * HEADS + h) * 3 + r] = pick(rank < SLOTS, near, beyond)
                wanted = jnp.where(place == group * 128 + rank, item.astype(F32), wanted)
    wanted = jnp.where(lane == 127, pick(most >= SLOTS, 1.0, 0.0), wanted)
    for p in range(16):
        spread_ref[p, 48:64, :] = jnp.broadcast_to(wanted[p : p + 1, :], (16, 128)).astype(BF16)
    wq_ref[...] = jnp.zeros_like(wq_ref)
    for h in range(HEADS):
        part = slice(64 * h, 64 * h + 64)
        wq_ref[:, 128 * h : 128 * h + 64] = weight_ref[0, :, part] * BF16(0.125)
        wkv_ref[:, 128 * h : 128 * h + 64] = weight_ref[1, :, part]
        wkv_ref[:, 128 * h + 64 : 128 * h + 128] = weight_ref[2, :, part]
    query = nn(states_ref[...], wq_ref[...]).astype(BF16)
    pair = nn(states_ref[...], wkv_ref[...]).astype(BF16)
    for h in range(HEADS):
        q_ref[h] = query[:, 128 * h : 128 * h + 128]
        kv_ref[h] = pair[:, 128 * h : 128 * h + 128]


def prepare(states, weight, owner, local, ids, here):
    shape = jax.ShapeDtypeStruct
    square, heads = shape((768, 768), BF16), shape((HEADS, 256, 128), BF16)
    return call(
        prepare_kernel,
        (square, square, heads, heads, shape((16, 64, 128), BF16)),
        [pltpu.SMEM((16,), jnp.int32), pltpu.VMEM((128, 768), BF16)],
        (600_000_000, 6_000_000, 0),
        [states, weight],
        scalars=[owner, local, ids, here],
        tables=(shape((1, 72), jnp.int32),),
    )


def early_kernel(*refs):
    wkv_ref, kv_ref = refs[-2:]
    for p in range(len(refs) - 2):
        pair = nn(refs[p][...], wkv_ref[...]).astype(BF16)
        for h in range(HEADS):
            kv_ref[p * HEADS + h] = pair[:, 128 * h : 128 * h + 128]


def early(pieces, wkv):
    count = len(pieces)
    return call(
        early_kernel,
        jax.ShapeDtypeStruct((count * HEADS, 128, 128), BF16),
        [],
        (count * 150_000_000, count * 500_000, 0),
        [*pieces, wkv],
    )


def column_kernel(*refs):
    (
        wkv_ref,
        received_ref,
        shares_ref,
        early_ref,
        second_ref,
        ids_ref,
        here_ref,
        kv_ref,
        items_ref,
        out_ref,
        wanted_ref,
        flag_ref,
        asked_ref,
        sem,
        sems,
    ) = refs[6:]
    copies = [
        pltpu.make_async_copy(early_ref, kv_ref.at[pl.ds(0, 6 * HEADS)], sem.at[0]),
        pltpu.make_async_copy(second_ref, kv_ref.at[pl.ds(6 * HEADS, 4 * HEADS)], sem.at[1]),
    ]
    for p in range(16):
        asked_ref[p : p + 1, :] = received_ref[p, 48:49, :].astype(F32).astype(jnp.int32)
    copies.append(pltpu.make_async_copy(asked_ref, wanted_ref, sem.at[2]))
    for copy in copies:
        copy.start()
    for p in range(6):
        pair = nn(refs[p][...], wkv_ref[...]).astype(BF16)
        for h in range(HEADS):
            kv_ref[(10 + p) * HEADS + h] = pair[:, 128 * h : 128 * h + 128]
    for copy in copies:
        copy.wait()
    flag = wanted_ref[0, 127]
    for p in range(1, 16):
        flag = jnp.maximum(flag, wanted_ref[p, 127])
    flag_ref[0, 0] = flag
    owner = pick(here_ref[0, 0] >= 2, ids_ref[0, 1], ids_ref[0, 0]) >> 2
    share = shares_ref[(owner >> 2) & 7]
    for p in range(16):
        items_ref[p, SLOTS * 64 : STRIDE, :] = share

    @pl.loop(0, 16)
    def _(p):
        for k in range(SLOTS):
            item = wanted_ref[p, k]
            at = pl.multiple_of((item & 1) * 64, 64)
            items_ref[p, 64 * k : 64 * k + 64, :] = kv_ref[item >> 1, pl.ds(at, 64), :]
        pltpu.make_async_copy(items_ref.at[p], out_ref.at[p], sems.at[p]).start()

    @pl.loop(0, 16)
    def _(p):
        pltpu.make_async_copy(items_ref.at[p], out_ref.at[p], sems.at[p]).wait()


def column(pieces, wkv, received, shares, first, second, ids, here):
    shape = jax.ShapeDtypeStruct
    return call(
        column_kernel,
        (shape((16 * HEADS, 128, 128), BF16), shape((16, STRIDE, 128), BF16)),
        [pltpu.VMEM((16, 128), jnp.int32), pltpu.SemaphoreType.DMA((3,)), pltpu.SemaphoreType.DMA((16,))],
        (1_000_000_000, 10_000_000, 0),
        [*pieces, wkv, received, shares],
        raw=[first, second],
        scalars=[ids, here],
        by_hand=(1,),
        tables=(shape((16, 128), jnp.int32), shape((1, 1), jnp.int32)),
    )


def extra_kernel(kv_ref, wanted_ref, items_ref):
    @pl.loop(0, 16)
    def _(p):
        for k in range(MORE):
            item = wanted_ref[p, SLOTS + k]
            at = pl.multiple_of((item & 1) * 64, 64)
            items_ref[p, 64 * k : 64 * k + 64, :] = kv_ref[item >> 1, pl.ds(at, 64), :]


def extra(kv, wanted):
    shape = jax.ShapeDtypeStruct((16, MORE * 64, 128), BF16)
    items = call(extra_kernel, shape, [], (0, 5_000_000, 0), [kv], scalars=[wanted])
    return exchanged(items, PLANE)


def unused_kernel(out_ref, row_ref):
    row_ref[...] = jnp.zeros_like(row_ref)
    pltpu.sync_copy(row_ref, out_ref.at[0, pl.ds(0, 16), :])


def unused():
    return pl.pallas_call(
        unused_kernel,
        out_shape=jax.ShapeDtypeStruct((16, MORE * 64, 128), BF16),
        out_specs=FAR,
        scratch_shapes=[pltpu.VMEM((16, 128), BF16)],
        compiler_params=pltpu.CompilerParams(vmem_limit_bytes=LIMIT),
    )()


def window_kernel(kv_ref, before_ref, after_ref, wkv_ref, ext_ref, rows_ref):
    rows_ref[0:64, :] = before_ref[...]
    rows_ref[64:128, :] = after_ref[...]
    pair = nn(rows_ref[...], wkv_ref[...]).astype(BF16)
    for h in range(HEADS):
        ext_ref[h, 0:64, :] = pair[0:64, 128 * h : 128 * h + 128]
        ext_ref[h, 64:320, :] = kv_ref[h]
        ext_ref[h, 320:384, :] = pair[64:128, 128 * h : 128 * h + 128]


def window(kv, before, after, wkv):
    return call(
        window_kernel,
        jax.ShapeDtypeStruct((HEADS, 384, 128), BF16),
        [pltpu.VMEM((128, 768), BF16)],
        (150_000_000, 3_000_000, 0),
        [kv, before, after, wkv],
    )


def partial_kernel(wq_ref, wkv_ref, remote_ref, kv_far, out_ref, pair_ref, share_ref, rows_ref, q_ref, s_ref, kv_ref, sem):
    copies = [pltpu.make_async_copy(remote_ref.at[p, pl.ds(SLOTS * 64, 48), :], share_ref.at[p], sem.at[p]) for p in range(16)]
    keep = pltpu.make_async_copy(kv_far, kv_ref, sem.at[16])
    for copy in copies:
        copy.start()
    keep.start()
    for p, copy in enumerate(copies):
        copy.wait()
        for c in range(3):
            lanes = (p % 2) * 384 + c * 128
            rows_ref[p // 2 * 16 : p // 2 * 16 + 16, lanes : lanes + 128] = share_ref[p, 16 * c : 16 * c + 16, :]
    query = nn(rows_ref[...], wq_ref[...]).astype(BF16)
    pair = nn(rows_ref[...], wkv_ref[...]).astype(BF16)
    for h in range(HEADS):
        q_ref[h] = query[:, 128 * h : 128 * h + 128]
        pair_ref[h] = pair[:, 128 * h : 128 * h + 128]
    keep.wait()
    lane = lax.broadcasted_iota(jnp.int32, (128, 128), 1)
    highs = jnp.zeros((128, 128), F32)
    totals = jnp.zeros((128, 128), F32)
    for h in range(HEADS):
        keys = [kv_ref[4 * c : 4 * c + 4, h].reshape(512, 128) for c in range(4)]
        high = jnp.full((128, 1), NEGATIVE, F32)
        for c in range(4):
            s = nt(q_ref[h], keys[c])
            s_ref[h % 2, :, c * 512 : c * 512 + 512] = s
            high = jnp.maximum(high, jnp.max(s, axis=1, keepdims=True))
        total = jnp.zeros((128, 1), F32)
        acc = jnp.zeros((128, 128), F32)
        for c in range(4):
            p = jnp.exp(s_ref[h % 2, :, c * 512 : c * 512 + 512] - high)
            total = total + jnp.sum(p, axis=1, keepdims=True)
            head = p.astype(BF16)
            rest = (p - head.astype(F32)).astype(BF16)
            acc = acc + nn(head, keys[c]) + nn(rest, keys[c])
        out_ref[:, 64 * h : 64 * h + 64] = acc[:, 64:128]
        highs = jnp.where(lane == h, high, highs)
        totals = jnp.where(lane == h, total, totals)
    out_ref[:, 384:512] = highs
    out_ref[:, 512:640] = totals


def partial(wq, wkv, remote, kv):
    shape = jax.ShapeDtypeStruct
    return call(
        partial_kernel,
        (shape((128, 640), F32), shape((HEADS, 128, 128), BF16)),
        [
            pltpu.VMEM((16, 48, 128), BF16),
            pltpu.VMEM((128, 768), BF16),
            pltpu.VMEM((HEADS, 128, 128), BF16),
            pltpu.VMEM((2, 128, 2048), F32),
            pltpu.VMEM((16, HEADS, 128, 128), BF16),
            pltpu.SemaphoreType.DMA((17,)),
        ],
        (2_000_000_000, 10_000_000, 1_600_000),
        [wq, wkv],
        raw=[remote, kv],
    )


def merge_kernel(parts_ref, out_ref):
    highs = parts_ref[:, :, 384:512]
    factor = jnp.exp(highs - jnp.max(highs, axis=0, keepdims=True))
    total = jnp.sum(factor * parts_ref[:, :, 512:640], axis=0)
    outs = []
    for h in range(HEADS):
        acc = jnp.sum(parts_ref[:, :, 64 * h : 64 * h + 64] * factor[:, :, h : h + 1], axis=0)
        outs.append(acc / total[:, h : h + 1])
    rows = jnp.concatenate(outs, axis=1).astype(BF16)
    for p in range(32):
        out_ref[p] = rows


def merge(parts):
    return call(
        merge_kernel,
        jax.ShapeDtypeStruct((32, 8, 384), BF16),
        [],
        (2_000_000, 600_000, 10_000),
        [parts],
    )


def attend_kernel(
    q_ref, ext_ref, pair_ref, remote_ref, more_ref, slot_ref, here_ref, flag_ref, out_ref, pool_ref, keys_ref, sem
):
    main = pltpu.make_async_copy(remote_ref, pool_ref.at[pl.ds(0, 16 * STRIDE), :], sem.at[0])
    main.start()

    @pl.when(flag_ref[0, 0] > 0)
    def _():
        pltpu.sync_copy(more_ref, pool_ref.at[pl.ds(16 * STRIDE, 16 * MORE * 64), :])

    main.wait()
    seq = (here_ref[0, 0] * 8 + here_ref[0, 1]) * 4 + here_ref[0, 2]
    lane = lax.broadcasted_iota(jnp.int32, (64, 512), 1)

    @pl.loop(0, HEADS // 2)
    def _(pair):
        for b in range(4):
            outs = []
            for k in range(2):
                h = pair * 2 + k
                buf = keys_ref.at[b * 2 + k]
                buf[0:192, :] = ext_ref[h, b * 64 : b * 64 + 192, :]
                for r in range(3):
                    at = pl.multiple_of(slot_ref[0, (b * HEADS + h) * 3 + r], 16)
                    buf[192 + 64 * r : 256 + 64 * r, :] = pool_ref[pl.ds(at, 64), :]
                buf[384:512, :] = pair_ref[h]
                keys = buf[...]
                s = nt(q_ref[h, b * 64 : b * 64 + 64, :], keys)
                if b == 0:
                    s = jnp.where((lane < 64) & (seq == 0), NEGATIVE, s)
                if b == 3:
                    s = jnp.where((lane >= 128) & (lane < 192) & (seq == 127), NEGATIVE, s)
                p = jnp.exp(s - jnp.max(s, axis=1, keepdims=True))
                w = (p * (1.0 / jnp.sum(p, axis=1, keepdims=True))).astype(BF16)
                outs.append(nn(w, keys)[:, 64:128])
            lanes = pl.ds(pl.multiple_of(pair * 128, 128), 128)
            out_ref[b * 64 : b * 64 + 64, lanes] = jnp.concatenate(outs, axis=1).astype(BF16)


def attend(q, ext, pair, remote, more, slots, here, flag):
    return call(
        attend_kernel,
        jax.ShapeDtypeStruct((256, 384), BF16),
        [
            pltpu.VMEM((16 * STRIDE + 16 * MORE * 64, 128), BF16),
            pltpu.VMEM((8, 512, 128), BF16),
            pltpu.SemaphoreType.DMA((1,)),
        ],
        (600_000_000, 7_000_000, 800_000),
        [q, ext, pair],
        raw=[remote, more],
        scalars=[slots, here, flag],
    )


def norm(v, gain):
    shifted = v - jnp.mean(v, axis=1, keepdims=True)
    spread = jnp.mean(shifted * shifted, axis=1, keepdims=True)
    return shifted * lax.rsqrt(spread + EPSILON) * gain


CHUNK = 512


def finish_kernel(
    own_ref,
    other_ref,
    states_ref,
    wo_own,
    wo_other,
    gain_ref,
    gain2_ref,
    rows_ref,
    up_own,
    up_other,
    down_own,
    down_other,
    ids_ref,
    here_ref,
    out_ref,
    attended,
    states,
    wo,
    gains,
    rows,
    up,
    down,
    sums,
    result,
    sem,
    sems,
):
    copies = [
        pltpu.make_async_copy(source, target, sem.at[i])
        for i, (source, target) in enumerate(
            [
                (own_ref, attended.at[0]),
                (other_ref, attended.at[1]),
                (rows_ref, rows),
                (wo_own, wo.at[0]),
                (wo_other, wo.at[1]),
                (states_ref, states),
                (gain_ref, gains.at[0]),
                (gain2_ref, gains.at[1]),
            ]
        )
    ]
    chunks = []
    for half, (above, below) in enumerate(((up_own, down_own), (up_other, down_other))):
        for i in range(0, 1536, CHUNK):
            number = len(chunks)
            part = pl.ds(i, CHUNK)
            chunks.append(
                (
                    pltpu.make_async_copy(above.at[:, part], up.at[number], sems.at[2 * number]),
                    pltpu.make_async_copy(below.at[part, :], down.at[number], sems.at[2 * number + 1]),
                )
            )
    for copy in copies:
        copy.start()
    for chunk in chunks:
        chunk[0].start()
        chunk[1].start()
    for copy in copies:
        copy.wait()
    core = here_ref[0, 3]
    seq = (here_ref[0, 0] * 8 + here_ref[0, 1]) * 4 + here_ref[0, 2]
    for g in range(2):

        @pl.when((ids_ref[0, g] >> 2) == seq)
        def _():
            for k, side in ((0, core), (1, 1 - core)):
                for i in range(4):
                    first = (g * 8 + 2 * i) * 2 + side
                    at = pl.multiple_of((ids_ref[0, g] & 3) * 64 + 16 * i, 16)
                    attended[k, pl.ds(at, 16), :] = jnp.concatenate([rows[first], rows[first + 2]], axis=0)

    projected = nn(attended[0], wo[0]) + nn(attended[1], wo[1])
    normed = norm(states[...].astype(F32) + projected, gains[0]).astype(BF16)
    for number, chunk in enumerate(chunks):
        chunk[0].wait()
        v = nn(normed, up[number])
        hidden = (v * (1.0 + lax.erf(v * 0.7071067811865476)) * 0.5).astype(BF16)
        chunk[1].wait()
        piece = nn(hidden, down[number])
        half = number // (1536 // CHUNK)
        if number % (1536 // CHUNK) == 0:
            sums[half] = piece
        else:
            sums[half] += piece
    result[...] = norm(normed.astype(F32) + (sums[0] + sums[1]), gains[1]).astype(BF16)
    pltpu.sync_copy(result, out_ref)


def finish(own, other, states, wo_own, wo_other, gain, gain2, rows, up_own, up_other, down_own, down_other, ids, here):
    count = 2 * 1536 // CHUNK
    return pl.pallas_call(
        finish_kernel,
        out_shape=jax.ShapeDtypeStruct((256, 768), BF16),
        in_specs=[FAR] * 12 + [SMEM] * 2,
        out_specs=FAR,
        scratch_shapes=[
            pltpu.VMEM((2, 256, 384), BF16),
            pltpu.VMEM((256, 768), BF16),
            pltpu.VMEM((2, 384, 768), BF16),
            pltpu.VMEM((2, 1, 768), F32),
            pltpu.VMEM((32, 8, 384), BF16),
            pltpu.VMEM((count, 768, CHUNK), BF16),
            pltpu.VMEM((count, CHUNK, 768), BF16),
            pltpu.VMEM((2, 256, 768), F32),
            pltpu.VMEM((256, 768), BF16),
            pltpu.SemaphoreType.DMA((8,)),
            pltpu.SemaphoreType.DMA((2 * count,)),
        ],
        cost_estimate=pl.CostEstimate(flops=2_700_000_000, bytes_accessed=12_000_000, transcendentals=800_000),
        compiler_params=pltpu.CompilerParams(vmem_limit_bytes=LIMIT),
    )(own, other, states, wo_own, wo_other, gain, gain2, rows, up_own, up_other, down_own, down_other, ids, here)


def turned(value, axis, shift):
    count = lax.axis_size(axis)
    return lax.ppermute(value, axis, [(i, (i + shift) % count) for i in range(count)])


def exchanged(value, axes):
    return lax.all_to_all(value, axes, split_axis=0, concat_axis=0, tiled=True)


def swapped(value):
    return lax.ppermute(value, "mp", [(0, 1), (1, 0)])


def shards(
    states, qkv_weight, out_weight, up_weight, down_weight, attn_gain, mlp_gain, global_ids, random_owner, random_local
):
    x, z, y, core = (lax.axis_index(axis) for axis in ("x", "z", "y", "mp"))
    here = jnp.stack([x, z, y, core]).astype(jnp.int32).reshape(1, 4)
    ids = global_ids.reshape(1, 2)
    tied = lax.optimization_barrier

    up0 = lax.dynamic_slice_in_dim(states, core * 128, 128, 0)
    up1, down1, far0 = turned(up0, "z", 1), turned(up0, "z", -1), swapped(up0)
    wq, wkv, q, kv, spread, slots = prepare(states, qkv_weight, random_owner, random_local, ids, here)
    up1, down1, far0, wkv, spread = tied((up1, down1, far0, wkv, spread))

    up2, down2 = turned(up1, "z", 1), turned(down1, "z", -1)
    far1, far7 = swapped(up1), swapped(down1)
    received = exchanged(spread, PLANE)
    up2, down2, far1, far7 = tied((up2, down2, far1, far7))

    up3, down3 = turned(up2, "z", 1), turned(down2, "z", -1)
    far2, far6 = swapped(up2), swapped(down2)
    first = early([up0, up1, down1, far0, far1, far7], wkv)
    up3, down3, far2, far6, first, received = tied((up3, down3, far2, far6, first, received))

    root_owner = pick(x >= 2, global_ids[1], global_ids[0]) >> 2
    root = (root_owner >> 5) * 4 + (root_owner & 3)
    share = lax.dynamic_slice(received, (root, 0, 0), (1, 48, 128))
    shares = exchanged(jnp.broadcast_to(share, (8, 48, 128)), "z")
    up4 = turned(up3, "z", 1)
    far3, far5 = swapped(up3), swapped(down3)
    second = early([up2, down2, far2, far6], wkv)
    ends = [(i, i + 1) for i in range(127)]
    before = lax.ppermute(states[192:], SEQ, ends)
    after = lax.ppermute(states[:64], SEQ, [(j, i) for i, j in ends])
    up4, far3, far5, second, shares, before, after = tied((up4, far3, far5, second, shares, before, after))

    pieces = [up3, up4, down3, far3, swapped(up4), far5]
    pairs, items, wanted, flag = column(pieces, wkv, received, shares, first, second, ids, here)
    more = lax.cond(flag[0, 0] > 0, lambda: extra(pairs, wanted), unused)
    items, more, weights = tied((items, more, (out_weight, up_weight, down_weight)))
    remote = exchanged(items, PLANE)
    wo_other, up_other, down_other = (swapped(weight) for weight in weights)
    ext = window(kv, before, after, wkv)
    remote, ext = tied((remote, ext))
    part, pair = partial(wq, wkv, remote, pairs.reshape(16, HEADS, 128, 128))
    rows = exchanged(merge(exchanged(part.reshape(16, 8, 640), PLANE)), PLANE + ("mp",))
    attended = attend(
        q, ext, pair, remote.reshape(16 * STRIDE, 128), more.reshape(16 * MORE * 64, 128), slots, here, flag
    )
    return finish(
        attended,
        swapped(attended),
        states,
        out_weight,
        wo_other,
        attn_gain.reshape(1, -1),
        mlp_gain.reshape(1, -1),
        rows,
        up_weight,
        up_other,
        down_weight,
        down_other,
        ids,
        here,
    )


def solution(mesh):
    split = Mesh(mesh.devices.reshape(4, 8, 4, mesh.shape["mp"]), ("x", "z", "y", "mp"))
    placed = (
        P(SEQ, None),
        P(None, None, "mp"),
        P("mp", None),
        P(None, "mp"),
        P("mp", None),
        P(),
        P(),
        P(),
        P("mp", SEQ, None, None),
        P("mp", SEQ, None, None),
    )
    return jax.shard_map(shards, mesh=split, in_specs=placed, out_specs=P(SEQ, None), check_vma=False)
```

```python
import functools

import jax
import jax.numpy as jnp
from jax import lax
from jax.experimental import pallas as pl
from jax.experimental.pallas import tpu as pltpu
from jax.sharding import Mesh
from jax.sharding import PartitionSpec as P

SEQ = ("x", "z", "y")
PLANE = ("x", "y")
EPSILON = 1e-05
NEGATIVE = -1e30
HEADS = 6
BF16 = jnp.bfloat16
F32 = jnp.float32
LIMIT = 51 * 1024 * 1024
SLOTS = 10
MORE = 16 - SLOTS
STRIDE = SLOTS * 64 + 48
FAR = pl.BlockSpec(memory_space=pltpu.HBM)
NEAR = pl.BlockSpec(memory_space=pltpu.VMEM)
SMEM = pl.BlockSpec(memory_space=pltpu.SMEM)


def nt(a, b):
    return lax.dot_general(a, b, (((1,), (1,)), ((), ())), preferred_element_type=F32)


def nn(a, b):
    return jnp.dot(a, b, preferred_element_type=F32)


def call(kernel, outs, scratch, cost, arrays, raw=(), near=(), scalars=(), by_hand=(), tables=()):
    single = not isinstance(outs, tuple)
    results = (outs,) if single else outs
    count, total = len(arrays), len(arrays) + len(raw) + len(near) + len(scalars)

    def body(*refs):
        inputs, others = refs[:count], refs[count:total]
        outputs = refs[total : total + len(results)]
        listed = refs[total + len(results) : total + len(results) + len(tables)]
        held = refs[total + len(results) + len(tables) :]
        copied, made, (sem_in, sem_out), rest = (
            held[:count],
            held[count : count + len(results)],
            held[count + len(results) : count + len(results) + 2],
            held[count + len(results) + 2 :],
        )
        copies = [pltpu.make_async_copy(inputs[i], copied[i], sem_in.at[i]) for i in range(count)]
        for copy in copies:
            copy.start()
        for copy in copies:
            copy.wait()
        kernel(*copied, *others, *made, *[outputs[i] for i in by_hand], *listed, *rest)
        copies = [pltpu.make_async_copy(made[i], outputs[i], sem_out.at[i]) for i in range(len(results)) if i not in by_hand]
        for copy in copies:
            copy.start()
        for copy in copies:
            copy.wait()

    made = pl.pallas_call(
        body,
        out_shape=(*results, *tables),
        in_specs=[FAR] * (count + len(raw)) + [NEAR] * len(near) + [SMEM] * len(scalars),
        out_specs=(FAR,) * len(results) + (SMEM,) * len(tables),
        scratch_shapes=[pltpu.VMEM(v.shape, v.dtype) for v in (*arrays, *results)]
        + [pltpu.SemaphoreType.DMA((max(count, 1),)), pltpu.SemaphoreType.DMA((len(results),))]
        + list(scratch),
        cost_estimate=pl.CostEstimate(flops=cost[0], bytes_accessed=cost[1], transcendentals=cost[2]),
        compiler_params=pltpu.CompilerParams(vmem_limit_bytes=LIMIT),
    )(*arrays, *raw, *near, *scalars)
    return made[0] if single and not tables else made


def pick(condition, yes, no):
    return jnp.where(condition, yes, no)


def piece_of(owner, local, z, core):
    return ((z - ((owner >> 2) & 7)) & 7) + pick((local >> 1) == core, 0, 8)


def plan_kernel(states_ref, owner_ref, local_ref, ids_ref, here_ref, spread_ref, slots_ref, count_ref, rows_ref, sem):
    z, core = here_ref[0, 1], here_ref[0, 3]
    copies = []
    for g in range(2):
        start = pl.multiple_of((ids_ref[0, g] & 3) * 64, 64)
        copies.append(pltpu.make_async_copy(states_ref.at[pl.ds(start, 64), :], rows_ref.at[pl.ds(64 * g, 64), :], sem.at[g]))
        copies[g].start()
    for p in range(16):
        count_ref[p] = 0
    line = lax.broadcasted_iota(jnp.int32, (16, 128), 0)
    lane = lax.broadcasted_iota(jnp.int32, (16, 128), 1)
    place = line * 128 + lane
    wanted = jnp.zeros((16, 128), F32)
    most = jnp.int32(0)
    for b in range(4):
        for h in range(HEADS):
            for r in range(3):
                owner, local = owner_ref[0, r, b, h], local_ref[0, r, b, h]
                item = (piece_of(owner, local, z, core) * HEADS + h) * 2 + (local & 1)
                group = ((owner >> 5) << 2) + (owner & 3)
                rank = count_ref[group]
                count_ref[group] = rank + 1
                most = jnp.maximum(most, rank)
                near = group * STRIDE + rank * 64
                beyond = 16 * STRIDE + group * MORE * 64 + (rank - SLOTS) * 64
                slots_ref[0, (b * HEADS + h) * 3 + r] = pick(rank < SLOTS, near, beyond)
                wanted = jnp.where(place == group * 128 + rank, item.astype(F32), wanted)
    wanted = jnp.where(lane == 127, pick(most >= SLOTS, 1.0, 0.0), wanted)
    for copy in copies:
        copy.wait()
    for p in range(16):
        spread_ref[p, 48:64, :] = jnp.broadcast_to(wanted[p : p + 1, :], (16, 128)).astype(BF16)
        for c in range(3):
            lanes = (p % 2) * 384 + c * 128
            spread_ref[p, 16 * c : 16 * c + 16, :] = rows_ref[p // 2 * 16 : p // 2 * 16 + 16, lanes : lanes + 128]


def plan(states, owner, local, ids, here):
    shape = jax.ShapeDtypeStruct
    return call(
        plan_kernel,
        shape((16, 64, 128), BF16),
        [pltpu.SMEM((16,), jnp.int32), pltpu.VMEM((128, 768), BF16), pltpu.SemaphoreType.DMA((2,))],
        (1_000_000, 600_000, 0),
        [],
        raw=[states],
        scalars=[owner, local, ids, here],
        tables=(shape((1, 72), jnp.int32),),
    )


def arrange_kernel(weight_ref, wq_ref, wkv_ref):
    wq_ref[...] = jnp.zeros_like(wq_ref)
    for h in range(HEADS):
        part = slice(64 * h, 64 * h + 64)
        wq_ref[:, 128 * h : 128 * h + 64] = weight_ref[0, :, part] * BF16(0.125)
        wkv_ref[:, 128 * h : 128 * h + 64] = weight_ref[1, :, part]
        wkv_ref[:, 128 * h + 64 : 128 * h + 128] = weight_ref[2, :, part]


def arrange(weight):
    square = jax.ShapeDtypeStruct((768, 768), BF16)
    return call(arrange_kernel, (square, square), [], (2_000_000, 4_000_000, 0), [weight])


def column_kernel(*refs):
    pieces = refs[1:17]
    wkv_ref = refs[0]
    (
        received_ref,
        shares_ref,
        ids_ref,
        here_ref,
        kv_ref,
        items_ref,
        out_ref,
        wanted_ref,
        flag_ref,
        asked_ref,
        rows_ref,
        sem,
        sems,
        sem_rows,
    ) = refs[17:]
    copies = [pltpu.make_async_copy(piece, rows_ref.at[pl.ds(128 * i, 128), :], sem_rows.at[i]) for i, piece in enumerate(pieces)]
    for copy in copies:
        copy.start()
    for p in range(16):
        asked_ref[p : p + 1, :] = received_ref[p, 48:49, :].astype(F32).astype(jnp.int32)
    asked = pltpu.make_async_copy(asked_ref, wanted_ref, sem.at[0])
    asked.start()
    owner = pick(here_ref[0, 0] >= 2, ids_ref[0, 1], ids_ref[0, 0]) >> 2
    share = shares_ref[(owner >> 2) & 7]
    for p in range(16):
        items_ref[p, SLOTS * 64 : STRIDE, :] = share
    for i in range(4):
        for copy in copies[4 * i : 4 * i + 4]:
            copy.wait()
        pair = nn(rows_ref[512 * i : 512 * i + 512, :], wkv_ref[...]).astype(BF16)
        for j in range(4):
            for h in range(HEADS):
                kv_ref[(4 * i + j) * HEADS + h] = pair[128 * j : 128 * j + 128, 128 * h : 128 * h + 128]
    asked.wait()
    flag = wanted_ref[0, 127]
    for p in range(1, 16):
        flag = jnp.maximum(flag, wanted_ref[p, 127])
    flag_ref[0, 0] = flag

    @pl.loop(0, 16)
    def _(p):
        for k in range(SLOTS):
            item = wanted_ref[p, k]
            at = pl.multiple_of((item & 1) * 64, 64)
            items_ref[p, 64 * k : 64 * k + 64, :] = kv_ref[item >> 1, pl.ds(at, 64), :]
        pltpu.make_async_copy(items_ref.at[p], out_ref.at[p], sems.at[p]).start()

    @pl.loop(0, 16)
    def _(p):
        pltpu.make_async_copy(items_ref.at[p], out_ref.at[p], sems.at[p]).wait()


def column(pieces, wkv, received, shares, ids, here):
    shape = jax.ShapeDtypeStruct
    return call(
        column_kernel,
        (shape((16 * HEADS, 128, 128), BF16), shape((16, STRIDE, 128), BF16)),
        [
            pltpu.VMEM((16, 128), jnp.int32),
            pltpu.VMEM((2048, 768), BF16),
            pltpu.SemaphoreType.DMA((1,)),
            pltpu.SemaphoreType.DMA((16,)),
            pltpu.SemaphoreType.DMA((16,)),
        ],
        (2_400_000_000, 10_000_000, 0),
        [wkv],
        raw=pieces,
        near=[received, shares],
        scalars=[ids, here],
        by_hand=(1,),
        tables=(shape((16, 128), jnp.int32), shape((1, 1), jnp.int32)),
    )


def extra_kernel(kv_ref, wanted_ref, items_ref):
    @pl.loop(0, 16)
    def _(p):
        for k in range(MORE):
            item = wanted_ref[p, SLOTS + k]
            at = pl.multiple_of((item & 1) * 64, 64)
            items_ref[p, 64 * k : 64 * k + 64, :] = kv_ref[item >> 1, pl.ds(at, 64), :]


def extra(kv, wanted):
    shape = jax.ShapeDtypeStruct((16, MORE * 64, 128), BF16)
    items = call(extra_kernel, shape, [], (0, 5_000_000, 0), [kv], scalars=[wanted])
    return exchanged(items, PLANE)


def unused_kernel(out_ref, row_ref):
    row_ref[...] = jnp.zeros_like(row_ref)
    pltpu.sync_copy(row_ref, out_ref.at[0, pl.ds(0, 16), :])


def unused():
    return pl.pallas_call(
        unused_kernel,
        out_shape=jax.ShapeDtypeStruct((16, MORE * 64, 128), BF16),
        out_specs=FAR,
        scratch_shapes=[pltpu.VMEM((16, 128), BF16)],
        compiler_params=pltpu.CompilerParams(vmem_limit_bytes=LIMIT),
    )()


def window_kernel(before_ref, states_ref, after_ref, wq_ref, wkv_ref, q_ref, ext_ref, rows_ref):
    rows_ref[0:64, :] = before_ref[...]
    rows_ref[64:320, :] = states_ref[...]
    rows_ref[320:384, :] = after_ref[...]
    pair = nn(rows_ref[...], wkv_ref[...]).astype(BF16)
    query = nn(states_ref[...], wq_ref[...]).astype(BF16)
    for h in range(HEADS):
        ext_ref[h] = pair[:, 128 * h : 128 * h + 128]
        q_ref[h] = query[:, 128 * h : 128 * h + 128]


def window(before, states, after, wq, wkv):
    shape = jax.ShapeDtypeStruct
    return call(
        window_kernel,
        (shape((HEADS, 256, 128), BF16), shape((HEADS, 384, 128), BF16)),
        [pltpu.VMEM((384, 768), BF16)],
        (800_000_000, 4_000_000, 0),
        [before, states, after, wq, wkv],
    )


def partial_kernel(wq_ref, wkv_ref, kv_far, remote_ref, out_ref, pair_ref, rows_ref, q_ref, s_ref, kv_ref, sem):
    keep = pltpu.make_async_copy(kv_far, kv_ref, sem.at[0])
    keep.start()
    for p in range(16):
        for c in range(3):
            lanes = (p % 2) * 384 + c * 128
            first = SLOTS * 64 + 16 * c
            rows_ref[p // 2 * 16 : p // 2 * 16 + 16, lanes : lanes + 128] = remote_ref[p, first : first + 16, :]
    query = nn(rows_ref[...], wq_ref[...]).astype(BF16)
    pair = nn(rows_ref[...], wkv_ref[...]).astype(BF16)
    for h in range(HEADS):
        q_ref[h] = query[:, 128 * h : 128 * h + 128]
        pair_ref[h] = pair[:, 128 * h : 128 * h + 128]
    keep.wait()
    lane = lax.broadcasted_iota(jnp.int32, (128, 128), 1)
    highs = jnp.zeros((128, 128), F32)
    totals = jnp.zeros((128, 128), F32)
    for h in range(HEADS):
        keys = [kv_ref[4 * c : 4 * c + 4, h].reshape(512, 128) for c in range(4)]
        high = jnp.full((128, 1), NEGATIVE, F32)
        for c in range(4):
            s = nt(q_ref[h], keys[c])
            s_ref[h % 2, :, c * 512 : c * 512 + 512] = s
            high = jnp.maximum(high, jnp.max(s, axis=1, keepdims=True))
        total = jnp.zeros((128, 1), F32)
        acc = jnp.zeros((128, 128), F32)
        for c in range(4):
            p = jnp.exp(s_ref[h % 2, :, c * 512 : c * 512 + 512] - high)
            total = total + jnp.sum(p, axis=1, keepdims=True)
            head = p.astype(BF16)
            rest = (p - head.astype(F32)).astype(BF16)
            acc = acc + nn(head, keys[c]) + nn(rest, keys[c])
        out_ref[:, 64 * h : 64 * h + 64] = acc[:, 64:128]
        highs = jnp.where(lane == h, high, highs)
        totals = jnp.where(lane == h, total, totals)
    out_ref[:, 384:512] = highs
    out_ref[:, 512:640] = totals


def partial(wq, wkv, remote, kv):
    shape = jax.ShapeDtypeStruct
    return call(
        partial_kernel,
        (shape((128, 640), F32), shape((HEADS, 128, 128), BF16)),
        [
            pltpu.VMEM((128, 768), BF16),
            pltpu.VMEM((HEADS, 128, 128), BF16),
            pltpu.VMEM((2, 128, 2048), F32),
            pltpu.VMEM((16, HEADS, 128, 128), BF16),
            pltpu.SemaphoreType.DMA((1,)),
        ],
        (2_000_000_000, 10_000_000, 1_600_000),
        [wq, wkv],
        raw=[kv],
        near=[remote],
    )


def merge_kernel(parts_ref, out_ref):
    highs = parts_ref[:, :, 384:512]
    factor = jnp.exp(highs - jnp.max(highs, axis=0, keepdims=True))
    total = jnp.sum(factor * parts_ref[:, :, 512:640], axis=0)
    outs = []
    for h in range(HEADS):
        acc = jnp.sum(parts_ref[:, :, 64 * h : 64 * h + 64] * factor[:, :, h : h + 1], axis=0)
        outs.append(acc / total[:, h : h + 1])
    rows = jnp.concatenate(outs, axis=1).astype(BF16)
    for p in range(32):
        out_ref[p] = rows


def merge(parts):
    return call(
        merge_kernel,
        jax.ShapeDtypeStruct((32, 8, 384), BF16),
        [],
        (2_000_000, 600_000, 10_000),
        [],
        near=[parts],
    )


def attend_kernel(first, count, q_ref, ext_ref, pair_ref, remote_ref, more_ref, slot_ref, here_ref, flag_ref, out_ref, items_ref, keys_ref):
    size = 16 * STRIDE

    def each(body):
        for b in range(4):
            for h in range(2 * count):
                for r in range(3):
                    body((b * 2 * count + h) * 3 + r, slot_ref[0, (b * HEADS + 2 * first + h) * 3 + r])

    def main(i, slot):
        at = pl.multiple_of(jnp.minimum(slot, size - 64), 16)
        items_ref[i] = remote_ref[pl.ds(at, 64), :]

    def beyond(i, slot):
        @pl.when(slot >= size)
        def _():
            items_ref[i] = more_ref[pl.ds(pl.multiple_of(slot - size, 64), 64), :]

    each(main)

    @pl.when(flag_ref[0, 0] > 0)
    def _():
        each(beyond)

    seq = (here_ref[0, 0] * 8 + here_ref[0, 1]) * 4 + here_ref[0, 2]
    lane = lax.broadcasted_iota(jnp.int32, (64, 512), 1)
    for pair in range(count):
        for b in range(4):
            outs = []
            for k in range(2):
                h = 2 * (first + pair) + k
                i = (b * 2 * count + 2 * pair + k) * 3
                buf = keys_ref.at[b * 2 + k]
                buf[0:192, :] = ext_ref[h, b * 64 : b * 64 + 192, :]
                for r in range(3):
                    buf[192 + 64 * r : 256 + 64 * r, :] = items_ref[i + r]
                buf[384:512, :] = pair_ref[h]
                keys = buf[...]
                s = nt(q_ref[h, b * 64 : b * 64 + 64, :], keys)
                if b == 0:
                    s = jnp.where((lane < 64) & (seq == 0), NEGATIVE, s)
                if b == 3:
                    s = jnp.where((lane >= 128) & (lane < 192) & (seq == 127), NEGATIVE, s)
                p = jnp.exp(s - jnp.max(s, axis=1, keepdims=True))
                w = (p * (1.0 / jnp.sum(p, axis=1, keepdims=True))).astype(BF16)
                outs.append(nn(w, keys)[:, 64:128])
            out_ref[b * 64 : b * 64 + 64, 128 * pair : 128 * pair + 128] = jnp.concatenate(outs, axis=1).astype(BF16)


def attend(first, count, q, ext, pair, remote, more, slots, here, flag):
    return call(
        functools.partial(attend_kernel, first, count),
        jax.ShapeDtypeStruct((256, 128 * count), BF16),
        [pltpu.VMEM((24 * count, 64, 128), BF16), pltpu.VMEM((8, 512, 128), BF16)],
        (200_000_000 * count, 1_500_000 * count, 270_000 * count),
        [q, ext, pair],
        near=[remote, more],
        scalars=[slots, here, flag],
    )


def norm(v, gain):
    shifted = v - jnp.mean(v, axis=1, keepdims=True)
    spread = jnp.mean(shifted * shifted, axis=1, keepdims=True)
    return shifted * lax.rsqrt(spread + EPSILON) * gain


CHUNK = 512


def finish_kernel(
    own_ref,
    other_ref,
    own2_ref,
    other2_ref,
    states_ref,
    wo_own,
    wo_other,
    gain_ref,
    gain2_ref,
    up_own,
    up_other,
    down_own,
    down_other,
    rows,
    ids_ref,
    here_ref,
    out_ref,
    attended,
    states,
    wo,
    gains,
    up,
    down,
    sums,
    result,
    sem,
    sems,
):
    copies = [
        pltpu.make_async_copy(source, target, sem.at[i])
        for i, (source, target) in enumerate(
            [
                (own_ref, attended.at[0, :, pl.ds(0, 256)]),
                (other_ref, attended.at[1, :, pl.ds(0, 256)]),
                (own2_ref, attended.at[0, :, pl.ds(256, 128)]),
                (other2_ref, attended.at[1, :, pl.ds(256, 128)]),
                (wo_own, wo.at[0]),
                (wo_other, wo.at[1]),
                (states_ref, states),
                (gain_ref, gains.at[0]),
                (gain2_ref, gains.at[1]),
            ]
        )
    ]
    chunks = []
    for half, (above, below) in enumerate(((up_own, down_own), (up_other, down_other))):
        for i in range(0, 1536, CHUNK):
            number = len(chunks)
            part = pl.ds(i, CHUNK)
            chunks.append(
                (
                    pltpu.make_async_copy(above.at[:, part], up.at[number], sems.at[2 * number]),
                    pltpu.make_async_copy(below.at[part, :], down.at[number], sems.at[2 * number + 1]),
                )
            )
    for copy in copies:
        copy.start()
    for chunk in chunks:
        chunk[0].start()
        chunk[1].start()
    for copy in copies:
        copy.wait()
    core = here_ref[0, 3]
    seq = (here_ref[0, 0] * 8 + here_ref[0, 1]) * 4 + here_ref[0, 2]
    for g in range(2):

        @pl.when((ids_ref[0, g] >> 2) == seq)
        def _():
            for k, side in ((0, core), (1, 1 - core)):
                for i in range(4):
                    first = (g * 8 + 2 * i) * 2 + side
                    at = pl.multiple_of((ids_ref[0, g] & 3) * 64 + 16 * i, 16)
                    attended[k, pl.ds(at, 16), :] = jnp.concatenate([rows[first], rows[first + 2]], axis=0)

    projected = nn(attended[0], wo[0]) + nn(attended[1], wo[1])
    normed = norm(states[...].astype(F32) + projected, gains[0]).astype(BF16)
    for number, chunk in enumerate(chunks):
        chunk[0].wait()
        v = nn(normed, up[number])
        hidden = (v * (1.0 + lax.erf(v * 0.7071067811865476)) * 0.5).astype(BF16)
        chunk[1].wait()
        piece = nn(hidden, down[number])
        half = number // (1536 // CHUNK)
        if number % (1536 // CHUNK) == 0:
            sums[half] = piece
        else:
            sums[half] += piece
    result[...] = norm(normed.astype(F32) + (sums[0] + sums[1]), gains[1]).astype(BF16)
    pltpu.sync_copy(result, out_ref)


def finish(*operands):
    count = 2 * 1536 // CHUNK
    return pl.pallas_call(
        finish_kernel,
        out_shape=jax.ShapeDtypeStruct((256, 768), BF16),
        in_specs=[FAR] * 13 + [NEAR] + [SMEM] * 2,
        out_specs=FAR,
        scratch_shapes=[
            pltpu.VMEM((2, 256, 384), BF16),
            pltpu.VMEM((256, 768), BF16),
            pltpu.VMEM((2, 384, 768), BF16),
            pltpu.VMEM((2, 1, 768), F32),
            pltpu.VMEM((count, 768, CHUNK), BF16),
            pltpu.VMEM((count, CHUNK, 768), BF16),
            pltpu.VMEM((2, 256, 768), F32),
            pltpu.VMEM((256, 768), BF16),
            pltpu.SemaphoreType.DMA((9,)),
            pltpu.SemaphoreType.DMA((2 * count,)),
        ],
        cost_estimate=pl.CostEstimate(flops=2_700_000_000, bytes_accessed=12_000_000, transcendentals=800_000),
        compiler_params=pltpu.CompilerParams(vmem_limit_bytes=LIMIT),
    )(*operands)


def turned(value, axis, shift):
    count = lax.axis_size(axis)
    return lax.ppermute(value, axis, [(i, (i + shift) % count) for i in range(count)])


def exchanged(value, axes):
    return lax.all_to_all(value, axes, split_axis=0, concat_axis=0, tiled=True)


def swapped(value):
    return lax.ppermute(value, "mp", [(0, 1), (1, 0)])


def shards(
    states, qkv_weight, out_weight, up_weight, down_weight, attn_gain, mlp_gain, global_ids, random_owner, random_local
):
    x, z, y, core = (lax.axis_index(axis) for axis in ("x", "z", "y", "mp"))
    here = jnp.stack([x, z, y, core]).astype(jnp.int32).reshape(1, 4)
    ids = global_ids.reshape(1, 2)
    tied = lax.optimization_barrier

    up0 = lax.dynamic_slice_in_dim(states, core * 128, 128, 0)
    up1, down1, far0 = turned(up0, "z", 1), turned(up0, "z", -1), swapped(up0)
    order = (0, 3, 1, 2)
    spread, slots = plan(states, random_owner.transpose(order), random_local.transpose(order), ids, here)
    up1, down1, far0, spread = tied((up1, down1, far0, spread))

    up2, down2 = turned(up1, "z", 1), turned(down1, "z", -1)
    far1, far7 = swapped(up1), swapped(down1)
    received = exchanged(spread, PLANE)
    wq, wkv = arrange(qkv_weight)
    up2, down2, far1, far7, wkv = tied((up2, down2, far1, far7, wkv))

    up3, down3 = turned(up2, "z", 1), turned(down2, "z", -1)
    far2, far6 = swapped(up2), swapped(down2)
    up3, down3, far2, far6, received = tied((up3, down3, far2, far6, received))

    root_owner = pick(x >= 2, global_ids[1], global_ids[0]) >> 2
    root = (root_owner >> 5) * 4 + (root_owner & 3)
    share = lax.dynamic_slice(received, (root, 0, 0), (1, 48, 128))
    up4 = turned(up3, "z", 1)
    shares = exchanged(jnp.broadcast_to(share, (8, 48, 128)), "z")
    far3, far5 = swapped(up3), swapped(down3)
    ends = [(i, i + 1) for i in range(127)]
    before = lax.ppermute(states[192:], SEQ, ends)
    after = lax.ppermute(states[:64], SEQ, [(j, i) for i, j in ends])
    up4, far3, far5, shares, before, after = tied((up4, far3, far5, shares, before, after))

    pieces = [up0, up1, up2, up3, up4, down3, down2, down1, far0, far1, far2, far3, swapped(up4), far5, far6, far7]
    pairs, items, wanted, flag = column(pieces, wkv, received, shares, ids, here)
    more = lax.cond(flag[0, 0] > 0, lambda: extra(pairs, wanted), unused)
    items, more, weights = tied((items, more, (out_weight, up_weight, down_weight)))
    remote = exchanged(items, PLANE)
    wo_other, up_other, down_other = (swapped(weight) for weight in weights)
    q, ext = window(before, states, after, wq, wkv)
    remote, ext = tied((remote, ext))
    part, pair = partial(wq, wkv, remote, pairs.reshape(16, HEADS, 128, 128))
    parts = exchanged(part.reshape(16, 8, 640), PLANE)
    rest = (q, ext, pair, remote.reshape(16 * STRIDE, 128), more.reshape(16 * MORE * 64, 128), slots, here, flag)
    attended = attend(0, 2, *rest)
    parts, attended = tied((parts, attended))
    rows = exchanged(merge(parts), PLANE + ("mp",))
    attended2 = attend(2, 1, *rest)
    return finish(
        attended,
        swapped(attended),
        attended2,
        swapped(attended2),
        states,
        out_weight,
        wo_other,
        attn_gain.reshape(1, -1),
        mlp_gain.reshape(1, -1),
        up_weight,
        up_other,
        down_weight,
        down_other,
        rows,
        ids,
        here,
    )


def solution(mesh):
    split = Mesh(mesh.devices.reshape(4, 8, 4, mesh.shape["mp"]), ("x", "z", "y", "mp"))
    placed = (
        P(SEQ, None),
        P(None, None, "mp"),
        P("mp", None),
        P(None, "mp"),
        P("mp", None),
        P(),
        P(),
        P(),
        P("mp", SEQ, None, None),
        P("mp", SEQ, None, None),
    )
    return jax.shard_map(shards, mesh=split, in_specs=placed, out_specs=P(SEQ, None), check_vma=False)
```

```python
import functools

import jax
import jax.numpy as jnp
from jax import lax
from jax.experimental import pallas as pl
from jax.experimental.pallas import tpu as pltpu
from jax.sharding import Mesh
from jax.sharding import PartitionSpec as P

SEQ = ("x", "z", "y")
PLANE = ("x", "y")
EPSILON = 1e-05
NEGATIVE = -1e30
HEADS = 6
BF16 = jnp.bfloat16
F32 = jnp.float32
LIMIT = 51 * 1024 * 1024
HIGH = 60 * 1024 * 1024
SLOTS = 10
MORE = 16 - SLOTS
STRIDE = SLOTS * 64 + 48
FAR = pl.BlockSpec(memory_space=pltpu.HBM)
NEAR = pl.BlockSpec(memory_space=pltpu.VMEM)
SMEM = pl.BlockSpec(memory_space=pltpu.SMEM)


def nt(a, b):
    return lax.dot_general(a, b, (((1,), (1,)), ((), ())), preferred_element_type=F32)


def nn(a, b):
    return jnp.dot(a, b, preferred_element_type=F32)


def call(kernel, outs, scratch, cost, arrays, raw=(), near=(), scalars=(), by_hand=(), held=(), tables=(), limit=LIMIT):
    single = not isinstance(outs, tuple)
    results = (outs,) if single else outs
    away = [i for i in range(len(results)) if i not in held]
    count, total = len(arrays), len(arrays) + len(raw) + len(near) + len(scalars)

    def body(*refs):
        inputs, others = refs[:count], refs[count:total]
        outputs = refs[total : total + len(results)]
        listed = refs[total + len(results) : total + len(results) + len(tables)]
        left = refs[total + len(results) + len(tables) :]
        copied, made, (sem_in, sem_out), rest = (
            left[:count],
            left[count : count + len(away)],
            left[count + len(away) : count + len(away) + 2],
            left[count + len(away) + 2 :],
        )
        copies = [pltpu.make_async_copy(inputs[i], copied[i], sem_in.at[i]) for i in range(count)]
        for copy in copies:
            copy.start()
        for copy in copies:
            copy.wait()
        places = [made[away.index(i)] if i in away else outputs[i] for i in range(len(results))]
        kernel(*copied, *others, *places, *[outputs[i] for i in by_hand], *listed, *rest)
        copies = [pltpu.make_async_copy(places[i], outputs[i], sem_out.at[i]) for i in away if i not in by_hand]
        for copy in copies:
            copy.start()
        for copy in copies:
            copy.wait()

    made = pl.pallas_call(
        body,
        out_shape=(*results, *tables),
        in_specs=[FAR] * (count + len(raw)) + [NEAR] * len(near) + [SMEM] * len(scalars),
        out_specs=tuple(FAR if i in away else NEAR for i in range(len(results))) + (SMEM,) * len(tables),
        scratch_shapes=[pltpu.VMEM(v.shape, v.dtype) for v in (*arrays, *[results[i] for i in away])]
        + [pltpu.SemaphoreType.DMA((max(count, 1),)), pltpu.SemaphoreType.DMA((len(results),))]
        + list(scratch),
        cost_estimate=pl.CostEstimate(flops=cost[0], bytes_accessed=cost[1], transcendentals=cost[2]),
        compiler_params=pltpu.CompilerParams(vmem_limit_bytes=limit),
    )(*arrays, *raw, *near, *scalars)
    return made[0] if single and not tables else made


def pick(condition, yes, no):
    return jnp.where(condition, yes, no)


def piece_of(owner, local, z, core):
    return ((z - ((owner >> 2) & 7)) & 7) + pick((local >> 1) == core, 0, 8)


def plan_kernel(states_ref, owner_ref, local_ref, ids_ref, here_ref, spread_ref, slots_ref, count_ref, rows_ref, sem):
    z, core = here_ref[0, 1], here_ref[0, 3]
    copies = []
    for g in range(2):
        start = pl.multiple_of((ids_ref[0, g] & 3) * 64, 64)
        copies.append(pltpu.make_async_copy(states_ref.at[pl.ds(start, 64), :], rows_ref.at[pl.ds(64 * g, 64), :], sem.at[g]))
        copies[g].start()
    for p in range(16):
        count_ref[p] = 0
    line = lax.broadcasted_iota(jnp.int32, (16, 128), 0)
    lane = lax.broadcasted_iota(jnp.int32, (16, 128), 1)
    place = line * 128 + lane
    wanted = jnp.zeros((16, 128), F32)
    most = jnp.int32(0)
    for b in range(4):
        for h in range(HEADS):
            for r in range(3):
                owner, local = owner_ref[0, r, b, h], local_ref[0, r, b, h]
                item = (piece_of(owner, local, z, core) * HEADS + h) * 2 + (local & 1)
                group = ((owner >> 5) << 2) + (owner & 3)
                rank = count_ref[group]
                count_ref[group] = rank + 1
                most = jnp.maximum(most, rank)
                near = group * STRIDE + rank * 64
                beyond = 16 * STRIDE + group * MORE * 64 + (rank - SLOTS) * 64
                slots_ref[0, (b * HEADS + h) * 3 + r] = pick(rank < SLOTS, near, beyond)
                wanted = jnp.where(place == group * 128 + rank, item.astype(F32), wanted)
    wanted = jnp.where(lane == 127, pick(most >= SLOTS, 1.0, 0.0), wanted)
    for copy in copies:
        copy.wait()
    for p in range(16):
        spread_ref[p, 48:64, :] = jnp.broadcast_to(wanted[p : p + 1, :], (16, 128)).astype(BF16)
        for c in range(3):
            lanes = (p % 2) * 384 + c * 128
            spread_ref[p, 16 * c : 16 * c + 16, :] = rows_ref[p // 2 * 16 : p // 2 * 16 + 16, lanes : lanes + 128]


def plan(states, owner, local, ids, here):
    shape = jax.ShapeDtypeStruct
    return call(
        plan_kernel,
        shape((16, 64, 128), BF16),
        [pltpu.SMEM((16,), jnp.int32), pltpu.VMEM((128, 768), BF16), pltpu.SemaphoreType.DMA((2,))],
        (1_000_000, 600_000, 0),
        [],
        raw=[states],
        scalars=[owner, local, ids, here],
        tables=(shape((1, 72), jnp.int32),),
        limit=HIGH,
    )


def interleave(weight_ref, first, wkv_ref):
    for h in range(HEADS):
        part = slice(64 * h, 64 * h + 64)
        wkv_ref[:, 128 * h : 128 * h + 64] = weight_ref[first, :, part]
        wkv_ref[:, 128 * h + 64 : 128 * h + 128] = weight_ref[first + 1, :, part]


def column_kernel(*refs):
    pieces = refs[1:17]
    weight_far = refs[0]
    (
        received_ref,
        shares_ref,
        ids_ref,
        here_ref,
        kv_ref,
        items_ref,
        out_ref,
        wanted_ref,
        flag_ref,
        asked_ref,
        rows_ref,
        weight_ref,
        wkv_ref,
        sem,
        sems,
    ) = refs[17:]
    weight = pltpu.make_async_copy(weight_far.at[pl.ds(1, 2)], weight_ref, sem.at[1])
    weight.start()
    for i, piece in enumerate(pieces):
        rows_ref[128 * i : 128 * i + 128, :] = piece[...]
    for p in range(16):
        asked_ref[p : p + 1, :] = received_ref[p, 48:49, :].astype(F32).astype(jnp.int32)
    asked = pltpu.make_async_copy(asked_ref, wanted_ref, sem.at[0])
    asked.start()
    owner = pick(here_ref[0, 0] >= 2, ids_ref[0, 1], ids_ref[0, 0]) >> 2
    share = shares_ref[(owner >> 2) & 7]
    for p in range(16):
        items_ref[p, SLOTS * 64 : STRIDE, :] = share
    weight.wait()
    interleave(weight_ref, 0, wkv_ref)

    @pl.loop(0, 4)
    def _(i):
        pair = nn(rows_ref[pl.ds(pl.multiple_of(i * 512, 512), 512), :], wkv_ref[...]).astype(BF16)
        for j in range(4):
            for h in range(HEADS):
                kv_ref[(4 * i + j) * HEADS + h] = pair[128 * j : 128 * j + 128, 128 * h : 128 * h + 128]

    asked.wait()
    flag = wanted_ref[0, 127]
    for p in range(1, 16):
        flag = jnp.maximum(flag, wanted_ref[p, 127])
    flag_ref[0, 0] = flag

    @pl.loop(0, 16)
    def _(p):
        for k in range(SLOTS):
            item = wanted_ref[p, k]
            at = pl.multiple_of((item & 1) * 64, 64)
            items_ref[p, 64 * k : 64 * k + 64, :] = kv_ref[item >> 1, pl.ds(at, 64), :]
        pltpu.make_async_copy(items_ref.at[p], out_ref.at[p], sems.at[p]).start()

    @pl.loop(0, 16)
    def _(p):
        pltpu.make_async_copy(items_ref.at[p], out_ref.at[p], sems.at[p]).wait()


def column(pieces, weight, received, shares, ids, here):
    shape = jax.ShapeDtypeStruct
    return call(
        column_kernel,
        (shape((16 * HEADS, 128, 128), BF16), shape((16, STRIDE, 128), BF16)),
        [
            pltpu.VMEM((16, 128), jnp.int32),
            pltpu.VMEM((2048, 768), BF16),
            pltpu.VMEM((2, 768, 384), BF16),
            pltpu.VMEM((768, 768), BF16),
            pltpu.SemaphoreType.DMA((2,)),
            pltpu.SemaphoreType.DMA((16,)),
        ],
        (2_400_000_000, 10_000_000, 0),
        [],
        raw=[weight],
        near=[*pieces, received, shares],
        scalars=[ids, here],
        by_hand=(1,),
        held=(0,),
        tables=(shape((16, 128), jnp.int32), shape((1, 1), jnp.int32)),
    )


def extra_kernel(kv_ref, wanted_ref, items_ref):
    @pl.loop(0, 16)
    def _(p):
        for k in range(MORE):
            item = wanted_ref[p, SLOTS + k]
            at = pl.multiple_of((item & 1) * 64, 64)
            items_ref[p, 64 * k : 64 * k + 64, :] = kv_ref[item >> 1, pl.ds(at, 64), :]


def extra(kv, wanted):
    shape = jax.ShapeDtypeStruct((16, MORE * 64, 128), BF16)
    items = call(extra_kernel, shape, [], (0, 5_000_000, 0), [], near=[kv], scalars=[wanted])
    return exchanged(items, PLANE)


def unused_kernel(out_ref, row_ref):
    row_ref[...] = jnp.zeros_like(row_ref)
    pltpu.sync_copy(row_ref, out_ref.at[0, pl.ds(0, 16), :])


def unused():
    return pl.pallas_call(
        unused_kernel,
        out_shape=jax.ShapeDtypeStruct((16, MORE * 64, 128), BF16),
        out_specs=FAR,
        scratch_shapes=[pltpu.VMEM((16, 128), BF16)],
        compiler_params=pltpu.CompilerParams(vmem_limit_bytes=LIMIT),
    )()


def window_kernel(before_ref, states_ref, after_ref, weight_ref, q_ref, ext_ref, wq_ref, wkv_ref, rows_ref):
    wq_ref[...] = jnp.zeros_like(wq_ref)
    for h in range(HEADS):
        wq_ref[:, 128 * h : 128 * h + 64] = weight_ref[0, :, 64 * h : 64 * h + 64] * BF16(0.125)
    interleave(weight_ref, 1, wkv_ref)
    rows_ref[0:64, :] = before_ref[...]
    rows_ref[64:320, :] = states_ref[...]
    rows_ref[320:384, :] = after_ref[...]
    pair = nn(rows_ref[...], wkv_ref[...]).astype(BF16)
    query = nn(states_ref[...], wq_ref[...]).astype(BF16)
    for h in range(HEADS):
        ext_ref[h] = pair[:, 128 * h : 128 * h + 128]
        q_ref[h] = query[:, 128 * h : 128 * h + 128]


def window(before, states, after, weight):
    shape = jax.ShapeDtypeStruct
    square = shape((768, 768), BF16)
    return call(
        window_kernel,
        (shape((HEADS, 256, 128), BF16), shape((HEADS, 384, 128), BF16), square, square),
        [pltpu.VMEM((384, 768), BF16)],
        (800_000_000, 4_000_000, 0),
        [before, states, after, weight],
        held=(0, 1, 2, 3),
    )


def partial_kernel(wq_ref, wkv_ref, kv_ref, remote_ref, out_ref, pair_ref, rows_ref, q_ref, s_ref):
    for p in range(16):
        for c in range(3):
            lanes = (p % 2) * 384 + c * 128
            first = SLOTS * 64 + 16 * c
            rows_ref[p // 2 * 16 : p // 2 * 16 + 16, lanes : lanes + 128] = remote_ref[p, first : first + 16, :]
    query = nn(rows_ref[...], wq_ref[...]).astype(BF16)
    pair = nn(rows_ref[...], wkv_ref[...]).astype(BF16)
    for h in range(HEADS):
        q_ref[h] = query[:, 128 * h : 128 * h + 128]
        pair_ref[h] = pair[:, 128 * h : 128 * h + 128]
    lane = lax.broadcasted_iota(jnp.int32, (128, 128), 1)
    highs = jnp.zeros((128, 128), F32)
    totals = jnp.zeros((128, 128), F32)
    for h in range(HEADS):
        keys = [kv_ref[4 * c : 4 * c + 4, h].reshape(512, 128) for c in range(4)]
        high = jnp.full((128, 1), NEGATIVE, F32)
        for c in range(4):
            s = nt(q_ref[h], keys[c])
            s_ref[h % 2, :, c * 512 : c * 512 + 512] = s
            high = jnp.maximum(high, jnp.max(s, axis=1, keepdims=True))
        total = jnp.zeros((128, 1), F32)
        acc = jnp.zeros((128, 128), F32)
        for c in range(4):
            p = jnp.exp(s_ref[h % 2, :, c * 512 : c * 512 + 512] - high)
            total = total + jnp.sum(p, axis=1, keepdims=True)
            acc = acc + nn(p.astype(BF16), keys[c])
        out_ref[:, 64 * h : 64 * h + 64] = acc[:, 64:128]
        highs = jnp.where(lane == h, high, highs)
        totals = jnp.where(lane == h, total, totals)
    out_ref[:, 384:512] = highs
    out_ref[:, 512:640] = totals


def partial(wq, wkv, remote, kv):
    shape = jax.ShapeDtypeStruct
    return call(
        partial_kernel,
        (shape((128, 640), F32), shape((HEADS, 128, 128), BF16)),
        [
            pltpu.VMEM((128, 768), BF16),
            pltpu.VMEM((HEADS, 128, 128), BF16),
            pltpu.VMEM((2, 128, 2048), F32),
        ],
        (2_000_000_000, 10_000_000, 1_600_000),
        [],
        near=[wq, wkv, kv, remote],
        held=(1,),
    )


def merge_kernel(parts_ref, out_ref):
    highs = parts_ref[:, :, 384:512]
    factor = jnp.exp(highs - jnp.max(highs, axis=0, keepdims=True))
    total = jnp.sum(factor * parts_ref[:, :, 512:640], axis=0)
    outs = []
    for h in range(HEADS):
        acc = jnp.sum(parts_ref[:, :, 64 * h : 64 * h + 64] * factor[:, :, h : h + 1], axis=0)
        outs.append(acc / total[:, h : h + 1])
    rows = jnp.concatenate(outs, axis=1).astype(BF16)
    for p in range(32):
        out_ref[p] = rows


def merge(parts):
    return call(
        merge_kernel,
        jax.ShapeDtypeStruct((32, 8, 384), BF16),
        [],
        (2_000_000, 600_000, 10_000),
        [],
        near=[parts],
    )


def attend_kernel(first, count, q_ref, ext_ref, pair_ref, remote_ref, more_ref, slot_ref, here_ref, flag_ref, out_ref, items_ref, keys_ref):
    size = 16 * STRIDE

    def each(body):
        for b in range(4):
            for h in range(2 * count):
                for r in range(3):
                    body((b * 2 * count + h) * 3 + r, slot_ref[0, (b * HEADS + 2 * first + h) * 3 + r])

    def main(i, slot):
        at = pl.multiple_of(jnp.minimum(slot, size - 64), 16)
        items_ref[i] = remote_ref[pl.ds(at, 64), :]

    def beyond(i, slot):
        @pl.when(slot >= size)
        def _():
            items_ref[i] = more_ref[pl.ds(pl.multiple_of(slot - size, 64), 64), :]

    each(main)

    @pl.when(flag_ref[0, 0] > 0)
    def _():
        each(beyond)

    seq = (here_ref[0, 0] * 8 + here_ref[0, 1]) * 4 + here_ref[0, 2]
    lane = lax.broadcasted_iota(jnp.int32, (64, 512), 1)
    for pair in range(count):
        for b in range(4):
            outs = []
            for k in range(2):
                h = 2 * (first + pair) + k
                i = (b * 2 * count + 2 * pair + k) * 3
                buf = keys_ref.at[b * 2 + k]
                buf[0:192, :] = ext_ref[h, b * 64 : b * 64 + 192, :]
                for r in range(3):
                    buf[192 + 64 * r : 256 + 64 * r, :] = items_ref[i + r]
                buf[384:512, :] = pair_ref[h]
                keys = buf[...]
                s = nt(q_ref[h, b * 64 : b * 64 + 64, :], keys)
                if b == 0:
                    s = jnp.where((lane < 64) & (seq == 0), NEGATIVE, s)
                if b == 3:
                    s = jnp.where((lane >= 128) & (lane < 192) & (seq == 127), NEGATIVE, s)
                p = jnp.exp(s - jnp.max(s, axis=1, keepdims=True))
                w = (p * (1.0 / jnp.sum(p, axis=1, keepdims=True))).astype(BF16)
                outs.append(nn(w, keys)[:, 64:128])
            out_ref[b * 64 : b * 64 + 64, 128 * pair : 128 * pair + 128] = jnp.concatenate(outs, axis=1).astype(BF16)


def attend(first, count, q, ext, pair, remote, more, slots, here, flag):
    return call(
        functools.partial(attend_kernel, first, count),
        jax.ShapeDtypeStruct((256, 128 * count), BF16),
        [pltpu.VMEM((24 * count, 64, 128), BF16), pltpu.VMEM((8, 512, 128), BF16)],
        (200_000_000 * count, 1_500_000 * count, 270_000 * count),
        [],
        near=[q, ext, pair, remote, more],
        scalars=[slots, here, flag],
    )


def norm(v, gain):
    shifted = v - jnp.mean(v, axis=1, keepdims=True)
    spread = jnp.mean(shifted * shifted, axis=1, keepdims=True)
    return shifted * lax.rsqrt(spread + EPSILON) * gain


CHUNK = 512


def finish_kernel(
    own_ref,
    other_ref,
    own2_ref,
    other2_ref,
    states_ref,
    wo_own,
    wo_other,
    gain_ref,
    gain2_ref,
    up_own,
    up_other,
    down_own,
    down_other,
    rows,
    ids_ref,
    here_ref,
    out_ref,
    attended,
    states,
    wo,
    gains,
    up,
    down,
    sums,
    result,
    sem,
    sems,
):
    copies = [
        pltpu.make_async_copy(source, target, sem.at[i])
        for i, (source, target) in enumerate(
            [
                (own_ref, attended.at[0, :, pl.ds(0, 256)]),
                (other_ref, attended.at[1, :, pl.ds(0, 256)]),
                (own2_ref, attended.at[0, :, pl.ds(256, 128)]),
                (other2_ref, attended.at[1, :, pl.ds(256, 128)]),
                (wo_own, wo.at[0]),
                (wo_other, wo.at[1]),
                (states_ref, states),
                (gain_ref, gains.at[0]),
                (gain2_ref, gains.at[1]),
            ]
        )
    ]
    chunks = []
    for half, (above, below) in enumerate(((up_own, down_own), (up_other, down_other))):
        for i in range(0, 1536, CHUNK):
            number = len(chunks)
            part = pl.ds(i, CHUNK)
            chunks.append(
                (
                    pltpu.make_async_copy(above.at[:, part], up.at[number], sems.at[2 * number]),
                    pltpu.make_async_copy(below.at[part, :], down.at[number], sems.at[2 * number + 1]),
                )
            )
    for copy in copies:
        copy.start()
    for chunk in chunks:
        chunk[0].start()
        chunk[1].start()
    for copy in copies:
        copy.wait()
    core = here_ref[0, 3]
    seq = (here_ref[0, 0] * 8 + here_ref[0, 1]) * 4 + here_ref[0, 2]
    for g in range(2):

        @pl.when((ids_ref[0, g] >> 2) == seq)
        def _():
            for k, side in ((0, core), (1, 1 - core)):
                for i in range(4):
                    first = (g * 8 + 2 * i) * 2 + side
                    at = pl.multiple_of((ids_ref[0, g] & 3) * 64 + 16 * i, 16)
                    attended[k, pl.ds(at, 16), :] = jnp.concatenate([rows[first], rows[first + 2]], axis=0)

    projected = nn(attended[0], wo[0]) + nn(attended[1], wo[1])
    normed = norm(states[...].astype(F32) + projected, gains[0]).astype(BF16)
    for number, chunk in enumerate(chunks):
        chunk[0].wait()
        v = nn(normed, up[number])
        hidden = (v * (1.0 + lax.erf(v * 0.7071067811865476)) * 0.5).astype(BF16)
        chunk[1].wait()
        piece = nn(hidden, down[number])
        half = number // (1536 // CHUNK)
        if number % (1536 // CHUNK) == 0:
            sums[half] = piece
        else:
            sums[half] += piece
    result[...] = norm(normed.astype(F32) + (sums[0] + sums[1]), gains[1]).astype(BF16)
    pltpu.sync_copy(result, out_ref)


def finish(*operands):
    count = 2 * 1536 // CHUNK
    return pl.pallas_call(
        finish_kernel,
        out_shape=jax.ShapeDtypeStruct((256, 768), BF16),
        in_specs=[FAR] * 13 + [NEAR] + [SMEM] * 2,
        out_specs=FAR,
        scratch_shapes=[
            pltpu.VMEM((2, 256, 384), BF16),
            pltpu.VMEM((256, 768), BF16),
            pltpu.VMEM((2, 384, 768), BF16),
            pltpu.VMEM((2, 1, 768), F32),
            pltpu.VMEM((count, 768, CHUNK), BF16),
            pltpu.VMEM((count, CHUNK, 768), BF16),
            pltpu.VMEM((2, 256, 768), F32),
            pltpu.VMEM((256, 768), BF16),
            pltpu.SemaphoreType.DMA((9,)),
            pltpu.SemaphoreType.DMA((2 * count,)),
        ],
        cost_estimate=pl.CostEstimate(flops=2_700_000_000, bytes_accessed=12_000_000, transcendentals=800_000),
        compiler_params=pltpu.CompilerParams(vmem_limit_bytes=LIMIT),
    )(*operands)


def turned(value, axis, shift):
    count = lax.axis_size(axis)
    return lax.ppermute(value, axis, [(i, (i + shift) % count) for i in range(count)])


def exchanged(value, axes):
    return lax.all_to_all(value, axes, split_axis=0, concat_axis=0, tiled=True)


def swapped(value):
    return lax.ppermute(value, "mp", [(0, 1), (1, 0)])


def shards(
    states, qkv_weight, out_weight, up_weight, down_weight, attn_gain, mlp_gain, global_ids, random_owner, random_local
):
    x, z, y, core = (lax.axis_index(axis) for axis in ("x", "z", "y", "mp"))
    here = jnp.stack([x, z, y, core]).astype(jnp.int32).reshape(1, 4)
    ids = global_ids.reshape(1, 2)
    tied = lax.optimization_barrier

    up0 = lax.dynamic_slice_in_dim(states, core * 128, 128, 0)
    ends = [(i, i + 1) for i in range(127)]
    before = lax.ppermute(states[192:], SEQ, ends)
    after = lax.ppermute(states[:64], SEQ, [(j, i) for i, j in ends])
    up1, down1, far0 = turned(up0, "z", 1), turned(up0, "z", -1), swapped(up0)
    order = (0, 3, 1, 2)
    spread, slots = plan(states, random_owner.transpose(order), random_local.transpose(order), ids, here)
    up1, down1, far0, spread, before, after = tied((up1, down1, far0, spread, before, after))

    up2, down2 = turned(up1, "z", 1), turned(down1, "z", -1)
    far1, far7 = swapped(up1), swapped(down1)
    received = exchanged(spread, PLANE)
    up2, down2, far1, far7 = tied((up2, down2, far1, far7))

    up3, down3 = turned(up2, "z", 1), turned(down2, "z", -1)
    far2, far6 = swapped(up2), swapped(down2)
    up3, down3, far2, far6, received = tied((up3, down3, far2, far6, received))

    root_owner = pick(x >= 2, global_ids[1], global_ids[0]) >> 2
    root = (root_owner >> 5) * 4 + (root_owner & 3)
    share = lax.dynamic_slice(received, (root, 0, 0), (1, 48, 128))
    up4 = turned(up3, "z", 1)
    shares = exchanged(jnp.broadcast_to(share, (8, 48, 128)), "z")
    far3, far5 = swapped(up3), swapped(down3)
    up4, far3, far5, shares = tied((up4, far3, far5, shares))

    pieces = [up0, up1, up2, up3, up4, down3, down2, down1, far0, far1, far2, far3, swapped(up4), far5, far6, far7]
    pairs, items, wanted, flag = column(pieces, qkv_weight, received, shares, ids, here)
    more = lax.cond(flag[0, 0] > 0, lambda: extra(pairs, wanted), unused)
    items, more, weights = tied((items, more, (out_weight, up_weight, down_weight)))
    remote = exchanged(items, PLANE)
    wo_other, up_other, down_other = (swapped(weight) for weight in weights)
    q, ext, wq, wkv = window(before, states, after, qkv_weight)
    remote, ext = tied((remote, ext))
    part, pair = partial(wq, wkv, remote, pairs.reshape(16, HEADS, 128, 128))
    parts = exchanged(part.reshape(16, 8, 640), PLANE)
    rest = (q, ext, pair, remote.reshape(16 * STRIDE, 128), more.reshape(16 * MORE * 64, 128), slots, here, flag)
    attended = attend(0, 2, *rest)
    parts, attended = tied((parts, attended))
    rows = exchanged(merge(parts), PLANE + ("mp",))
    attended2 = attend(2, 1, *rest)
    return finish(
        attended,
        swapped(attended),
        attended2,
        swapped(attended2),
        states,
        out_weight,
        wo_other,
        attn_gain.reshape(1, -1),
        mlp_gain.reshape(1, -1),
        up_weight,
        up_other,
        down_weight,
        down_other,
        rows,
        ids,
        here,
    )


def solution(mesh):
    split = Mesh(mesh.devices.reshape(4, 8, 4, mesh.shape["mp"]), ("x", "z", "y", "mp"))
    placed = (
        P(SEQ, None),
        P(None, None, "mp"),
        P("mp", None),
        P(None, "mp"),
        P("mp", None),
        P(),
        P(),
        P(),
        P("mp", SEQ, None, None),
        P("mp", SEQ, None, None),
    )
    return jax.shard_map(shards, mesh=split, in_specs=placed, out_specs=P(SEQ, None), check_vma=False)
```

```python
import functools

import jax
import jax.numpy as jnp
from jax import lax
from jax.experimental import pallas as pl
from jax.experimental.pallas import tpu as pltpu
from jax.sharding import Mesh
from jax.sharding import PartitionSpec as P

SEQ = ("x", "z", "y")
PLANE = ("x", "y")
EPSILON = 1e-05
NEGATIVE = -1e30
HEADS = 6
BF16 = jnp.bfloat16
F32 = jnp.float32
LIMIT = 51 * 1024 * 1024
HIGH = 60 * 1024 * 1024
SLOTS = 10
MORE = 16 - SLOTS
STRIDE = SLOTS * 64 + 48
FAR = pl.BlockSpec(memory_space=pltpu.HBM)
NEAR = pl.BlockSpec(memory_space=pltpu.VMEM)
SMEM = pl.BlockSpec(memory_space=pltpu.SMEM)


def nt(a, b):
    return lax.dot_general(a, b, (((1,), (1,)), ((), ())), preferred_element_type=F32)


def nn(a, b):
    return jnp.dot(a, b, preferred_element_type=F32)


def call(kernel, outs, scratch, cost, arrays, raw=(), near=(), scalars=(), by_hand=(), held=(), tables=(), limit=LIMIT):
    single = not isinstance(outs, tuple)
    results = (outs,) if single else outs
    away = [i for i in range(len(results)) if i not in held]
    count, total = len(arrays), len(arrays) + len(raw) + len(near) + len(scalars)

    def body(*refs):
        inputs, others = refs[:count], refs[count:total]
        outputs = refs[total : total + len(results)]
        listed = refs[total + len(results) : total + len(results) + len(tables)]
        left = refs[total + len(results) + len(tables) :]
        copied, made, (sem_in, sem_out), rest = (
            left[:count],
            left[count : count + len(away)],
            left[count + len(away) : count + len(away) + 2],
            left[count + len(away) + 2 :],
        )
        copies = [pltpu.make_async_copy(inputs[i], copied[i], sem_in.at[i]) for i in range(count)]
        for copy in copies:
            copy.start()
        for copy in copies:
            copy.wait()
        places = [made[away.index(i)] if i in away else outputs[i] for i in range(len(results))]
        kernel(*copied, *others, *places, *[outputs[i] for i in by_hand], *listed, *rest)
        copies = [pltpu.make_async_copy(places[i], outputs[i], sem_out.at[i]) for i in away if i not in by_hand]
        for copy in copies:
            copy.start()
        for copy in copies:
            copy.wait()

    made = pl.pallas_call(
        body,
        out_shape=(*results, *tables),
        in_specs=[FAR] * (count + len(raw)) + [NEAR] * len(near) + [SMEM] * len(scalars),
        out_specs=tuple(FAR if i in away else NEAR for i in range(len(results))) + (SMEM,) * len(tables),
        scratch_shapes=[pltpu.VMEM(v.shape, v.dtype) for v in (*arrays, *[results[i] for i in away])]
        + [pltpu.SemaphoreType.DMA((max(count, 1),)), pltpu.SemaphoreType.DMA((len(results),))]
        + list(scratch),
        cost_estimate=pl.CostEstimate(flops=cost[0], bytes_accessed=cost[1], transcendentals=cost[2]),
        compiler_params=pltpu.CompilerParams(vmem_limit_bytes=limit),
    )(*arrays, *raw, *near, *scalars)
    return made[0] if single and not tables else made


def pick(condition, yes, no):
    return jnp.where(condition, yes, no)


def piece_of(owner, local, z, core):
    return ((z - ((owner >> 2) & 7)) & 7) + pick((local >> 1) == core, 0, 8)


def plan_kernel(states_ref, owner_ref, local_ref, ids_ref, here_ref, spread_ref, slots_ref, count_ref, rows_ref, sem):
    z, core = here_ref[0, 1], here_ref[0, 3]
    copies = []
    for g in range(2):
        start = pl.multiple_of((ids_ref[0, g] & 3) * 64, 64)
        copies.append(pltpu.make_async_copy(states_ref.at[pl.ds(start, 64), :], rows_ref.at[pl.ds(64 * g, 64), :], sem.at[g]))
        copies[g].start()
    for p in range(16):
        count_ref[p] = 0
    line = lax.broadcasted_iota(jnp.int32, (16, 128), 0)
    lane = lax.broadcasted_iota(jnp.int32, (16, 128), 1)
    place = line * 128 + lane
    wanted = jnp.zeros((16, 128), F32)
    most = jnp.int32(0)
    for b in range(4):
        for h in range(HEADS):
            for r in range(3):
                owner, local = owner_ref[0, r, b, h], local_ref[0, r, b, h]
                item = (piece_of(owner, local, z, core) * HEADS + h) * 2 + (local & 1)
                group = ((owner >> 5) << 2) + (owner & 3)
                rank = count_ref[group]
                count_ref[group] = rank + 1
                most = jnp.maximum(most, rank)
                near = group * STRIDE + rank * 64
                beyond = 16 * STRIDE + group * MORE * 64 + (rank - SLOTS) * 64
                slots_ref[0, (b * HEADS + h) * 3 + r] = pick(rank < SLOTS, near, beyond)
                wanted = jnp.where(place == group * 128 + rank, item.astype(F32), wanted)
    wanted = jnp.where(lane == 127, pick(most >= SLOTS, 1.0, 0.0), wanted)
    for copy in copies:
        copy.wait()
    for p in range(16):
        spread_ref[p, 48:64, :] = jnp.broadcast_to(wanted[p : p + 1, :], (16, 128)).astype(BF16)
        for c in range(3):
            lanes = (p % 2) * 384 + c * 128
            spread_ref[p, 16 * c : 16 * c + 16, :] = rows_ref[p // 2 * 16 : p // 2 * 16 + 16, lanes : lanes + 128]


def plan(states, owner, local, ids, here):
    shape = jax.ShapeDtypeStruct
    return call(
        plan_kernel,
        shape((16, 64, 128), BF16),
        [pltpu.SMEM((16,), jnp.int32), pltpu.VMEM((128, 768), BF16), pltpu.SemaphoreType.DMA((2,))],
        (1_000_000, 600_000, 0),
        [],
        raw=[states],
        scalars=[owner, local, ids, here],
        tables=(shape((1, 72), jnp.int32),),
        limit=HIGH,
    )


def interleave(weight_ref, first, wkv_ref):
    for h in range(HEADS):
        part = slice(64 * h, 64 * h + 64)
        wkv_ref[:, 128 * h : 128 * h + 64] = weight_ref[first, :, part]
        wkv_ref[:, 128 * h + 64 : 128 * h + 128] = weight_ref[first + 1, :, part]


def column_kernel(*refs):
    pieces = refs[1:17]
    weight_far = refs[0]
    (
        received_ref,
        shares_ref,
        ids_ref,
        here_ref,
        kv_ref,
        items_ref,
        out_ref,
        wanted_ref,
        flag_ref,
        asked_ref,
        rows_ref,
        weight_ref,
        wkv_ref,
        sem,
        sems,
    ) = refs[17:]
    weight = pltpu.make_async_copy(weight_far.at[pl.ds(1, 2)], weight_ref, sem.at[1])
    weight.start()
    for i, piece in enumerate(pieces):
        rows_ref[128 * i : 128 * i + 128, :] = piece[...]
    for p in range(16):
        asked_ref[p : p + 1, :] = received_ref[p, 48:49, :].astype(F32).astype(jnp.int32)
    asked = pltpu.make_async_copy(asked_ref, wanted_ref, sem.at[0])
    asked.start()
    owner = pick(here_ref[0, 0] >= 2, ids_ref[0, 1], ids_ref[0, 0]) >> 2
    share = shares_ref[(owner >> 2) & 7]
    for p in range(16):
        items_ref[p, SLOTS * 64 : STRIDE, :] = share
    weight.wait()
    interleave(weight_ref, 0, wkv_ref)

    @pl.loop(0, 4)
    def _(i):
        pair = nn(rows_ref[pl.ds(pl.multiple_of(i * 512, 512), 512), :], wkv_ref[...]).astype(BF16)
        for j in range(4):
            for h in range(HEADS):
                kv_ref[(4 * i + j) * HEADS + h] = pair[128 * j : 128 * j + 128, 128 * h : 128 * h + 128]

    asked.wait()
    flag = wanted_ref[0, 127]
    for p in range(1, 16):
        flag = jnp.maximum(flag, wanted_ref[p, 127])
    flag_ref[0, 0] = flag

    @pl.loop(0, 16)
    def _(p):
        for k in range(SLOTS):
            item = wanted_ref[p, k]
            at = pl.multiple_of((item & 1) * 64, 64)
            items_ref[p, 64 * k : 64 * k + 64, :] = kv_ref[item >> 1, pl.ds(at, 64), :]
        pltpu.make_async_copy(items_ref.at[p], out_ref.at[p], sems.at[p]).start()

    @pl.loop(0, 16)
    def _(p):
        pltpu.make_async_copy(items_ref.at[p], out_ref.at[p], sems.at[p]).wait()


def column(pieces, weight, received, shares, ids, here):
    shape = jax.ShapeDtypeStruct
    return call(
        column_kernel,
        (shape((16 * HEADS, 128, 128), BF16), shape((16, STRIDE, 128), BF16)),
        [
            pltpu.VMEM((16, 128), jnp.int32),
            pltpu.VMEM((2048, 768), BF16),
            pltpu.VMEM((2, 768, 384), BF16),
            pltpu.VMEM((768, 768), BF16),
            pltpu.SemaphoreType.DMA((2,)),
            pltpu.SemaphoreType.DMA((16,)),
        ],
        (2_400_000_000, 10_000_000, 0),
        [],
        raw=[weight],
        near=[*pieces, received, shares],
        scalars=[ids, here],
        by_hand=(1,),
        held=(0,),
        tables=(shape((16, 128), jnp.int32), shape((1, 1), jnp.int32)),
    )


def extra_kernel(kv_ref, wanted_ref, items_ref):
    @pl.loop(0, 16)
    def _(p):
        for k in range(MORE):
            item = wanted_ref[p, SLOTS + k]
            at = pl.multiple_of((item & 1) * 64, 64)
            items_ref[p, 64 * k : 64 * k + 64, :] = kv_ref[item >> 1, pl.ds(at, 64), :]


def extra(kv, wanted):
    shape = jax.ShapeDtypeStruct((16, MORE * 64, 128), BF16)
    items = call(extra_kernel, shape, [], (0, 5_000_000, 0), [], near=[kv], scalars=[wanted])
    return exchanged(items, PLANE)


def unused_kernel(out_ref, row_ref):
    row_ref[...] = jnp.zeros_like(row_ref)
    pltpu.sync_copy(row_ref, out_ref.at[0, pl.ds(0, 16), :])


def unused():
    return pl.pallas_call(
        unused_kernel,
        out_shape=jax.ShapeDtypeStruct((16, MORE * 64, 128), BF16),
        out_specs=FAR,
        scratch_shapes=[pltpu.VMEM((16, 128), BF16)],
        compiler_params=pltpu.CompilerParams(vmem_limit_bytes=LIMIT),
    )()


def window_kernel(before_ref, states_ref, after_ref, weight_ref, q_ref, ext_ref, wq_ref, wkv_ref, rows_ref):
    wq_ref[...] = jnp.zeros_like(wq_ref)
    for h in range(HEADS):
        wq_ref[:, 128 * h : 128 * h + 64] = weight_ref[0, :, 64 * h : 64 * h + 64] * BF16(0.125)
    interleave(weight_ref, 1, wkv_ref)
    rows_ref[0:64, :] = before_ref[...]
    rows_ref[64:320, :] = states_ref[...]
    rows_ref[320:384, :] = after_ref[...]
    pair = nn(rows_ref[...], wkv_ref[...]).astype(BF16)
    query = nn(states_ref[...], wq_ref[...]).astype(BF16)
    for h in range(HEADS):
        ext_ref[h] = pair[:, 128 * h : 128 * h + 128]
        q_ref[h] = query[:, 128 * h : 128 * h + 128]


def window(before, states, after, weight):
    shape = jax.ShapeDtypeStruct
    square = shape((768, 768), BF16)
    return call(
        window_kernel,
        (shape((HEADS, 256, 128), BF16), shape((HEADS, 384, 128), BF16), square, square),
        [pltpu.VMEM((384, 768), BF16)],
        (800_000_000, 4_000_000, 0),
        [before, states, after, weight],
        held=(0, 1, 2, 3),
    )


def partial_kernel(wq_ref, wkv_ref, kv_ref, remote_ref, out_ref, pair_ref, rows_ref, q_ref, s_ref):
    for p in range(16):
        for c in range(3):
            lanes = (p % 2) * 384 + c * 128
            first = SLOTS * 64 + 16 * c
            rows_ref[p // 2 * 16 : p // 2 * 16 + 16, lanes : lanes + 128] = remote_ref[p, first : first + 16, :]
    query = nn(rows_ref[...], wq_ref[...]).astype(BF16)
    pair = nn(rows_ref[...], wkv_ref[...]).astype(BF16)
    for h in range(HEADS):
        q_ref[h] = query[:, 128 * h : 128 * h + 128]
        pair_ref[h] = pair[:, 128 * h : 128 * h + 128]
    lane = lax.broadcasted_iota(jnp.int32, (128, 128), 1)
    highs = jnp.zeros((128, 128), F32)
    totals = jnp.zeros((128, 128), F32)
    for h in range(HEADS):
        keys = [kv_ref[4 * c : 4 * c + 4, h].reshape(512, 128) for c in range(4)]
        high = jnp.full((128, 1), NEGATIVE, F32)
        for c in range(4):
            s = nt(q_ref[h], keys[c])
            s_ref[h % 2, :, c * 512 : c * 512 + 512] = s
            high = jnp.maximum(high, jnp.max(s, axis=1, keepdims=True))
        total = jnp.zeros((128, 1), F32)
        acc = jnp.zeros((128, 128), F32)
        for c in range(4):
            p = jnp.exp(s_ref[h % 2, :, c * 512 : c * 512 + 512] - high)
            total = total + jnp.sum(p, axis=1, keepdims=True)
            acc = acc + nn(p.astype(BF16), keys[c])
        out_ref[:, 64 * h : 64 * h + 64] = acc[:, 64:128]
        highs = jnp.where(lane == h, high, highs)
        totals = jnp.where(lane == h, total, totals)
    out_ref[:, 384:512] = highs
    out_ref[:, 512:640] = totals


def partial(wq, wkv, remote, kv):
    shape = jax.ShapeDtypeStruct
    return call(
        partial_kernel,
        (shape((128, 640), F32), shape((HEADS, 128, 128), BF16)),
        [
            pltpu.VMEM((128, 768), BF16),
            pltpu.VMEM((HEADS, 128, 128), BF16),
            pltpu.VMEM((2, 128, 2048), F32),
        ],
        (2_000_000_000, 10_000_000, 1_600_000),
        [],
        near=[wq, wkv, kv, remote],
        held=(1,),
    )


def merge_kernel(parts_ref, out_ref):
    highs = parts_ref[:, :, 384:512]
    factor = jnp.exp(highs - jnp.max(highs, axis=0, keepdims=True))
    total = jnp.sum(factor * parts_ref[:, :, 512:640], axis=0)
    outs = []
    for h in range(HEADS):
        acc = jnp.sum(parts_ref[:, :, 64 * h : 64 * h + 64] * factor[:, :, h : h + 1], axis=0)
        outs.append(acc / total[:, h : h + 1])
    rows = jnp.concatenate(outs, axis=1).astype(BF16)
    for p in range(32):
        out_ref[p] = rows


def merge(parts):
    return call(
        merge_kernel,
        jax.ShapeDtypeStruct((32, 8, 384), BF16),
        [],
        (2_000_000, 600_000, 10_000),
        [],
        near=[parts],
    )


def attend_kernel(first, count, q_ref, ext_ref, pair_ref, remote_ref, more_ref, slot_ref, here_ref, flag_ref, out_ref, items_ref, keys_ref):
    size = 16 * STRIDE

    def each(body):
        for b in range(4):
            for h in range(2 * count):
                for r in range(3):
                    body((b * 2 * count + h) * 3 + r, slot_ref[0, (b * HEADS + 2 * first + h) * 3 + r])

    def main(i, slot):
        at = pl.multiple_of(jnp.minimum(slot, size - 64), 16)
        items_ref[i] = remote_ref[pl.ds(at, 64), :]

    def beyond(i, slot):
        @pl.when(slot >= size)
        def _():
            items_ref[i] = more_ref[pl.ds(pl.multiple_of(slot - size, 64), 64), :]

    each(main)

    @pl.when(flag_ref[0, 0] > 0)
    def _():
        each(beyond)

    seq = (here_ref[0, 0] * 8 + here_ref[0, 1]) * 4 + here_ref[0, 2]
    lane = lax.broadcasted_iota(jnp.int32, (64, 512), 1)
    for pair in range(count):
        for b in range(4):
            outs = []
            for k in range(2):
                h = 2 * (first + pair) + k
                i = (b * 2 * count + 2 * pair + k) * 3
                buf = keys_ref.at[b * 2 + k]
                buf[0:192, :] = ext_ref[h, b * 64 : b * 64 + 192, :]
                for r in range(3):
                    buf[192 + 64 * r : 256 + 64 * r, :] = items_ref[i + r]
                buf[384:512, :] = pair_ref[h]
                keys = buf[...]
                s = nt(q_ref[h, b * 64 : b * 64 + 64, :], keys)
                if b == 0:
                    s = jnp.where((lane < 64) & (seq == 0), NEGATIVE, s)
                if b == 3:
                    s = jnp.where((lane >= 128) & (lane < 192) & (seq == 127), NEGATIVE, s)
                p = jnp.exp(s - jnp.max(s, axis=1, keepdims=True))
                w = (p * (1.0 / jnp.sum(p, axis=1, keepdims=True))).astype(BF16)
                outs.append(nn(w, keys)[:, 64:128])
            out_ref[b * 64 : b * 64 + 64, 128 * pair : 128 * pair + 128] = jnp.concatenate(outs, axis=1).astype(BF16)


def attend(first, count, q, ext, pair, remote, more, slots, here, flag):
    return call(
        functools.partial(attend_kernel, first, count),
        jax.ShapeDtypeStruct((256, 128 * count), BF16),
        [pltpu.VMEM((24 * count, 64, 128), BF16), pltpu.VMEM((8, 512, 128), BF16)],
        (200_000_000 * count, 1_500_000 * count, 270_000 * count),
        [],
        near=[q, ext, pair, remote, more],
        held=(0,),
        scalars=[slots, here, flag],
    )


def norm(v, gain):
    shifted = v - jnp.mean(v, axis=1, keepdims=True)
    spread = jnp.mean(shifted * shifted, axis=1, keepdims=True)
    return shifted * lax.rsqrt(spread + EPSILON) * gain


CHUNK = 512


def finish_kernel(
    own_ref,
    other_ref,
    own2_ref,
    other2_ref,
    states_ref,
    wo_own,
    wo_other,
    gain_ref,
    gain2_ref,
    up_own,
    up_other,
    down_own,
    down_other,
    rows,
    ids_ref,
    here_ref,
    out_ref,
    attended,
    states,
    wo,
    gains,
    up,
    down,
    sums,
    result,
    sem,
    sems,
):
    copies = [
        pltpu.make_async_copy(source, target, sem.at[i])
        for i, (source, target) in enumerate(
            [
                (own_ref, attended.at[0, :, pl.ds(0, 256)]),
                (other_ref, attended.at[1, :, pl.ds(0, 256)]),
                (own2_ref, attended.at[0, :, pl.ds(256, 128)]),
                (other2_ref, attended.at[1, :, pl.ds(256, 128)]),
                (wo_own, wo.at[0]),
                (wo_other, wo.at[1]),
                (states_ref, states),
                (gain_ref, gains.at[0]),
                (gain2_ref, gains.at[1]),
            ]
        )
    ]
    chunks = []
    for half, (above, below) in enumerate(((up_own, down_own), (up_other, down_other))):
        for i in range(0, 1536, CHUNK):
            number = len(chunks)
            part = pl.ds(i, CHUNK)
            chunks.append(
                (
                    pltpu.make_async_copy(above.at[:, part], up.at[number], sems.at[2 * number]),
                    pltpu.make_async_copy(below.at[part, :], down.at[number], sems.at[2 * number + 1]),
                )
            )
    for copy in copies:
        copy.start()
    for chunk in chunks:
        chunk[0].start()
        chunk[1].start()
    for copy in copies:
        copy.wait()
    core = here_ref[0, 3]
    seq = (here_ref[0, 0] * 8 + here_ref[0, 1]) * 4 + here_ref[0, 2]
    for g in range(2):

        @pl.when((ids_ref[0, g] >> 2) == seq)
        def _():
            for k, side in ((0, core), (1, 1 - core)):
                for i in range(4):
                    first = (g * 8 + 2 * i) * 2 + side
                    at = pl.multiple_of((ids_ref[0, g] & 3) * 64 + 16 * i, 16)
                    attended[k, pl.ds(at, 16), :] = jnp.concatenate([rows[first], rows[first + 2]], axis=0)

    projected = nn(attended[0], wo[0]) + nn(attended[1], wo[1])
    normed = norm(states[...].astype(F32) + projected, gains[0]).astype(BF16)
    for number, chunk in enumerate(chunks):
        chunk[0].wait()
        v = nn(normed, up[number])
        hidden = (v * (1.0 + lax.erf(v * 0.7071067811865476)) * 0.5).astype(BF16)
        chunk[1].wait()
        piece = nn(hidden, down[number])
        half = number // (1536 // CHUNK)
        if number % (1536 // CHUNK) == 0:
            sums[half] = piece
        else:
            sums[half] += piece
    result[...] = norm(normed.astype(F32) + (sums[0] + sums[1]), gains[1]).astype(BF16)
    pltpu.sync_copy(result, out_ref)


def finish(*operands):
    count = 2 * 1536 // CHUNK
    return pl.pallas_call(
        finish_kernel,
        out_shape=jax.ShapeDtypeStruct((256, 768), BF16),
        in_specs=[FAR] * 13 + [NEAR] + [SMEM] * 2,
        out_specs=FAR,
        scratch_shapes=[
            pltpu.VMEM((2, 256, 384), BF16),
            pltpu.VMEM((256, 768), BF16),
            pltpu.VMEM((2, 384, 768), BF16),
            pltpu.VMEM((2, 1, 768), F32),
            pltpu.VMEM((count, 768, CHUNK), BF16),
            pltpu.VMEM((count, CHUNK, 768), BF16),
            pltpu.VMEM((2, 256, 768), F32),
            pltpu.VMEM((256, 768), BF16),
            pltpu.SemaphoreType.DMA((9,)),
            pltpu.SemaphoreType.DMA((2 * count,)),
        ],
        cost_estimate=pl.CostEstimate(flops=2_700_000_000, bytes_accessed=12_000_000, transcendentals=800_000),
        compiler_params=pltpu.CompilerParams(vmem_limit_bytes=LIMIT),
    )(*operands)


def turned(value, axis, shift):
    count = lax.axis_size(axis)
    return lax.ppermute(value, axis, [(i, (i + shift) % count) for i in range(count)])


def exchanged(value, axes):
    return lax.all_to_all(value, axes, split_axis=0, concat_axis=0, tiled=True)


def swapped(value):
    return lax.ppermute(value, "mp", [(0, 1), (1, 0)])


def shards(
    states, qkv_weight, out_weight, up_weight, down_weight, attn_gain, mlp_gain, global_ids, random_owner, random_local
):
    x, z, y, core = (lax.axis_index(axis) for axis in ("x", "z", "y", "mp"))
    here = jnp.stack([x, z, y, core]).astype(jnp.int32).reshape(1, 4)
    ids = global_ids.reshape(1, 2)
    tied = lax.optimization_barrier

    up0 = lax.dynamic_slice_in_dim(states, core * 128, 128, 0)
    ends = [(i, i + 1) for i in range(127)]
    before = lax.ppermute(states[192:], SEQ, ends)
    after = lax.ppermute(states[:64], SEQ, [(j, i) for i, j in ends])
    up1, down1, far0 = turned(up0, "z", 1), turned(up0, "z", -1), swapped(up0)
    order = (0, 3, 1, 2)
    spread, slots = plan(states, random_owner.transpose(order), random_local.transpose(order), ids, here)
    received = exchanged(spread, PLANE)
    up1, down1, far0 = tied((up1, down1, far0))

    up2, down2 = turned(up1, "z", 1), turned(down1, "z", -1)
    far1, far7 = swapped(up1), swapped(down1)
    up2, down2, far1, far7, received = tied((up2, down2, far1, far7, received))

    up3, down3 = turned(up2, "z", 1), turned(down2, "z", -1)
    far2, far6 = swapped(up2), swapped(down2)
    up3, down3, far2, far6, before, after = tied((up3, down3, far2, far6, before, after))

    root_owner = pick(x >= 2, global_ids[1], global_ids[0]) >> 2
    root = (root_owner >> 5) * 4 + (root_owner & 3)
    share = lax.dynamic_slice(received, (root, 0, 0), (1, 48, 128))
    up4 = turned(up3, "z", 1)
    shares = exchanged(jnp.broadcast_to(share, (8, 48, 128)), "z")
    far3, far5 = swapped(up3), swapped(down3)

    pieces = [up0, up1, up2, up3, up4, down3, down2, down1, far0, far1, far2, far3, swapped(up4), far5, far6, far7]
    pairs, items, wanted, flag = column(pieces, qkv_weight, received, shares, ids, here)
    more = lax.cond(flag[0, 0] > 0, lambda: extra(pairs, wanted), unused)
    items, more, weights = tied((items, more, (out_weight, up_weight, down_weight)))
    remote = exchanged(items, PLANE)
    wo_other, up_other, down_other = (swapped(weight) for weight in weights)
    q, ext, wq, wkv = window(before, states, after, qkv_weight)
    remote, ext = tied((remote, ext))
    part, pair = partial(wq, wkv, remote, pairs.reshape(16, HEADS, 128, 128))
    parts = exchanged(part.reshape(16, 8, 640), PLANE)
    rest = (q, ext, pair, remote.reshape(16 * STRIDE, 128), more.reshape(16 * MORE * 64, 128), slots, here, flag)
    attended = attend(0, 2, *rest)
    parts, attended = tied((parts, attended))
    rows = exchanged(merge(parts), PLANE + ("mp",))
    attended2 = attend(2, 1, *rest)
    return finish(
        attended,
        swapped(attended),
        attended2,
        swapped(attended2),
        states,
        out_weight,
        wo_other,
        attn_gain.reshape(1, -1),
        mlp_gain.reshape(1, -1),
        up_weight,
        up_other,
        down_weight,
        down_other,
        rows,
        ids,
        here,
    )


def solution(mesh):
    split = Mesh(mesh.devices.reshape(4, 8, 4, mesh.shape["mp"]), ("x", "z", "y", "mp"))
    placed = (
        P(SEQ, None),
        P(None, None, "mp"),
        P("mp", None),
        P(None, "mp"),
        P("mp", None),
        P(),
        P(),
        P(),
        P("mp", SEQ, None, None),
        P("mp", SEQ, None, None),
    )
    return jax.shard_map(shards, mesh=split, in_specs=placed, out_specs=P(SEQ, None), check_vma=False)
```

```python
import functools

import jax
import jax.numpy as jnp
from jax import lax
from jax.experimental import pallas as pl
from jax.experimental.pallas import tpu as pltpu
from jax.sharding import Mesh
from jax.sharding import PartitionSpec as P

SEQ = ("x", "z", "y")
PLANE = ("x", "y")
EPSILON = 1e-05
NEGATIVE = -1e30
HEADS = 6
BF16 = jnp.bfloat16
F32 = jnp.float32
LIMIT = 51 * 1024 * 1024
HIGH = 60 * 1024 * 1024
SLOTS = 10
MORE = 16 - SLOTS
STRIDE = SLOTS * 64 + 48
FAR = pl.BlockSpec(memory_space=pltpu.HBM)
NEAR = pl.BlockSpec(memory_space=pltpu.VMEM)
SMEM = pl.BlockSpec(memory_space=pltpu.SMEM)


def nt(a, b):
    return lax.dot_general(a, b, (((1,), (1,)), ((), ())), preferred_element_type=F32)


def nn(a, b):
    return jnp.dot(a, b, preferred_element_type=F32)


def call(kernel, outs, scratch, cost, arrays, raw=(), near=(), scalars=(), by_hand=(), held=(), tables=(), limit=LIMIT):
    single = not isinstance(outs, tuple)
    results = (outs,) if single else outs
    away = [i for i in range(len(results)) if i not in held]
    count, total = len(arrays), len(arrays) + len(raw) + len(near) + len(scalars)

    def body(*refs):
        inputs, others = refs[:count], refs[count:total]
        outputs = refs[total : total + len(results)]
        listed = refs[total + len(results) : total + len(results) + len(tables)]
        left = refs[total + len(results) + len(tables) :]
        copied, made, (sem_in, sem_out), rest = (
            left[:count],
            left[count : count + len(away)],
            left[count + len(away) : count + len(away) + 2],
            left[count + len(away) + 2 :],
        )
        copies = [pltpu.make_async_copy(inputs[i], copied[i], sem_in.at[i]) for i in range(count)]
        for copy in copies:
            copy.start()
        for copy in copies:
            copy.wait()
        places = [made[away.index(i)] if i in away else outputs[i] for i in range(len(results))]
        kernel(*copied, *others, *places, *[outputs[i] for i in by_hand], *listed, *rest)
        copies = [pltpu.make_async_copy(places[i], outputs[i], sem_out.at[i]) for i in away if i not in by_hand]
        for copy in copies:
            copy.start()
        for copy in copies:
            copy.wait()

    made = pl.pallas_call(
        body,
        out_shape=(*results, *tables),
        in_specs=[FAR] * (count + len(raw)) + [NEAR] * len(near) + [SMEM] * len(scalars),
        out_specs=tuple(FAR if i in away else NEAR for i in range(len(results))) + (SMEM,) * len(tables),
        scratch_shapes=[pltpu.VMEM(v.shape, v.dtype) for v in (*arrays, *[results[i] for i in away])]
        + [pltpu.SemaphoreType.DMA((max(count, 1),)), pltpu.SemaphoreType.DMA((len(results),))]
        + list(scratch),
        cost_estimate=pl.CostEstimate(flops=cost[0], bytes_accessed=cost[1], transcendentals=cost[2]),
        compiler_params=pltpu.CompilerParams(vmem_limit_bytes=limit),
    )(*arrays, *raw, *near, *scalars)
    return made[0] if single and not tables else made


def pick(condition, yes, no):
    return jnp.where(condition, yes, no)


def piece_of(owner, local, z, core):
    return ((z - ((owner >> 2) & 7)) & 7) + pick((local >> 1) == core, 0, 8)


def plan_kernel(states_ref, owner_ref, local_ref, ids_ref, here_ref, spread_ref, slots_ref, count_ref, rows_ref, sem):
    z, core = here_ref[0, 1], here_ref[0, 3]
    copies = []
    for g in range(2):
        start = pl.multiple_of((ids_ref[0, g] & 3) * 64, 64)
        copies.append(pltpu.make_async_copy(states_ref.at[pl.ds(start, 64), :], rows_ref.at[pl.ds(64 * g, 64), :], sem.at[g]))
        copies[g].start()
    for p in range(16):
        count_ref[p] = 0
    line = lax.broadcasted_iota(jnp.int32, (16, 128), 0)
    lane = lax.broadcasted_iota(jnp.int32, (16, 128), 1)
    place = line * 128 + lane
    wanted = jnp.zeros((16, 128), F32)
    most = jnp.int32(0)
    for b in range(4):
        for h in range(HEADS):
            for r in range(3):
                owner, local = owner_ref[0, r, b, h], local_ref[0, r, b, h]
                item = (piece_of(owner, local, z, core) * HEADS + h) * 2 + (local & 1)
                group = ((owner >> 5) << 2) + (owner & 3)
                rank = count_ref[group]
                count_ref[group] = rank + 1
                most = jnp.maximum(most, rank)
                near = group * STRIDE + rank * 64
                beyond = 16 * STRIDE + group * MORE * 64 + (rank - SLOTS) * 64
                slots_ref[0, (b * HEADS + h) * 3 + r] = pick(rank < SLOTS, near, beyond)
                wanted = jnp.where(place == group * 128 + rank, item.astype(F32), wanted)
    roots = [((ids_ref[0, g] >> 4) & 7).astype(F32) for g in range(2)]
    wanted = jnp.where(lane == 126, jnp.where(line >= 8, roots[1], roots[0]), wanted)
    wanted = jnp.where(lane == 127, pick(most >= SLOTS, 1.0, 0.0), wanted)
    for copy in copies:
        copy.wait()
    for p in range(16):
        spread_ref[p, 48:64, :] = jnp.broadcast_to(wanted[p : p + 1, :], (16, 128)).astype(BF16)
        for c in range(3):
            lanes = (p % 2) * 384 + c * 128
            spread_ref[p, 16 * c : 16 * c + 16, :] = rows_ref[p // 2 * 16 : p // 2 * 16 + 16, lanes : lanes + 128]


def plan(states, owner, local, ids, here):
    shape = jax.ShapeDtypeStruct
    return call(
        plan_kernel,
        shape((16, 64, 128), BF16),
        [pltpu.SMEM((16,), jnp.int32), pltpu.VMEM((128, 768), BF16), pltpu.SemaphoreType.DMA((2,))],
        (1_000_000, 600_000, 0),
        [],
        raw=[states],
        scalars=[owner, local, ids, here],
        tables=(shape((1, 72), jnp.int32),),
        limit=HIGH,
    )


def interleave(weight_ref, first, wkv_ref):
    for h in range(HEADS):
        part = slice(64 * h, 64 * h + 64)
        wkv_ref[:, 128 * h : 128 * h + 64] = weight_ref[first, :, part]
        wkv_ref[:, 128 * h + 64 : 128 * h + 128] = weight_ref[first + 1, :, part]


def column_kernel(*refs):
    pieces = refs[1:17]
    weight_far = refs[0]
    (
        received_ref,
        shares_ref,
        kv_ref,
        items_ref,
        out_ref,
        wanted_ref,
        flag_ref,
        asked_ref,
        rows_ref,
        weight_ref,
        wkv_ref,
        sem,
        sems,
    ) = refs[17:]
    weight = pltpu.make_async_copy(weight_far.at[pl.ds(1, 2)], weight_ref, sem.at[1])
    weight.start()
    for i, piece in enumerate(pieces):
        rows_ref[128 * i : 128 * i + 128, :] = piece[...]
    for p in range(16):
        asked_ref[p : p + 1, :] = received_ref[p, 48:49, :].astype(F32).astype(jnp.int32)
    asked = pltpu.make_async_copy(asked_ref, wanted_ref, sem.at[0])
    asked.start()
    weight.wait()
    interleave(weight_ref, 0, wkv_ref)

    @pl.loop(0, 4)
    def _(i):
        pair = nn(rows_ref[pl.ds(pl.multiple_of(i * 512, 512), 512), :], wkv_ref[...]).astype(BF16)
        for j in range(4):
            for h in range(HEADS):
                kv_ref[(4 * i + j) * HEADS + h] = pair[128 * j : 128 * j + 128, 128 * h : 128 * h + 128]

    asked.wait()
    flag = wanted_ref[0, 127]
    for p in range(1, 16):
        flag = jnp.maximum(flag, wanted_ref[p, 127])
    flag_ref[0, 0] = flag
    share = shares_ref[wanted_ref[0, 126]]
    for p in range(16):
        items_ref[p, SLOTS * 64 : STRIDE, :] = share

    @pl.loop(0, 16)
    def _(p):
        for k in range(SLOTS):
            item = wanted_ref[p, k]
            at = pl.multiple_of((item & 1) * 64, 64)
            items_ref[p, 64 * k : 64 * k + 64, :] = kv_ref[item >> 1, pl.ds(at, 64), :]
        pltpu.make_async_copy(items_ref.at[p], out_ref.at[p], sems.at[p]).start()

    @pl.loop(0, 16)
    def _(p):
        pltpu.make_async_copy(items_ref.at[p], out_ref.at[p], sems.at[p]).wait()


def column(pieces, weight, received, shares):
    shape = jax.ShapeDtypeStruct
    return call(
        column_kernel,
        (shape((16 * HEADS, 128, 128), BF16), shape((16, STRIDE, 128), BF16)),
        [
            pltpu.VMEM((16, 128), jnp.int32),
            pltpu.VMEM((2048, 768), BF16),
            pltpu.VMEM((2, 768, 384), BF16),
            pltpu.VMEM((768, 768), BF16),
            pltpu.SemaphoreType.DMA((2,)),
            pltpu.SemaphoreType.DMA((16,)),
        ],
        (2_400_000_000, 10_000_000, 0),
        [],
        raw=[weight],
        near=[*pieces, received, shares],
        by_hand=(1,),
        held=(0,),
        tables=(shape((16, 128), jnp.int32), shape((1, 1), jnp.int32)),
    )


def extra_kernel(kv_ref, wanted_ref, items_ref):
    @pl.loop(0, 16)
    def _(p):
        for k in range(MORE):
            item = wanted_ref[p, SLOTS + k]
            at = pl.multiple_of((item & 1) * 64, 64)
            items_ref[p, 64 * k : 64 * k + 64, :] = kv_ref[item >> 1, pl.ds(at, 64), :]


def extra(kv, wanted):
    shape = jax.ShapeDtypeStruct((16, MORE * 64, 128), BF16)
    items = call(extra_kernel, shape, [], (0, 5_000_000, 0), [], near=[kv], scalars=[wanted])
    return exchanged(items, PLANE)


def unused_kernel(out_ref, row_ref):
    row_ref[...] = jnp.zeros_like(row_ref)
    pltpu.sync_copy(row_ref, out_ref.at[0, pl.ds(0, 16), :])


def unused():
    return pl.pallas_call(
        unused_kernel,
        out_shape=jax.ShapeDtypeStruct((16, MORE * 64, 128), BF16),
        out_specs=FAR,
        scratch_shapes=[pltpu.VMEM((16, 128), BF16)],
        compiler_params=pltpu.CompilerParams(vmem_limit_bytes=LIMIT),
    )()


def window_kernel(before_ref, states_ref, after_ref, weight_ref, q_ref, ext_ref, wq_ref, wkv_ref, rows_ref):
    wq_ref[...] = jnp.zeros_like(wq_ref)
    for h in range(HEADS):
        wq_ref[:, 128 * h : 128 * h + 64] = weight_ref[0, :, 64 * h : 64 * h + 64] * BF16(0.125)
    interleave(weight_ref, 1, wkv_ref)
    rows_ref[0:64, :] = before_ref[...]
    rows_ref[64:320, :] = states_ref[...]
    rows_ref[320:384, :] = after_ref[...]
    pair = nn(rows_ref[...], wkv_ref[...]).astype(BF16)
    query = nn(states_ref[...], wq_ref[...]).astype(BF16)
    for h in range(HEADS):
        ext_ref[h] = pair[:, 128 * h : 128 * h + 128]
        q_ref[h] = query[:, 128 * h : 128 * h + 128]


def window(before, states, after, weight):
    shape = jax.ShapeDtypeStruct
    square = shape((768, 768), BF16)
    return call(
        window_kernel,
        (shape((HEADS, 256, 128), BF16), shape((HEADS, 384, 128), BF16), square, square),
        [pltpu.VMEM((384, 768), BF16)],
        (800_000_000, 4_000_000, 0),
        [before, states, after, weight],
        held=(0, 1, 2, 3),
    )


def partial_kernel(wq_ref, wkv_ref, kv_ref, remote_ref, out_ref, pair_ref, rows_ref, q_ref, s_ref):
    for p in range(16):
        for c in range(3):
            lanes = (p % 2) * 384 + c * 128
            first = SLOTS * 64 + 16 * c
            rows_ref[p // 2 * 16 : p // 2 * 16 + 16, lanes : lanes + 128] = remote_ref[p, first : first + 16, :]
    query = nn(rows_ref[...], wq_ref[...]).astype(BF16)
    pair = nn(rows_ref[...], wkv_ref[...]).astype(BF16)
    for h in range(HEADS):
        q_ref[h] = query[:, 128 * h : 128 * h + 128]
        pair_ref[h] = pair[:, 128 * h : 128 * h + 128]
    lane = lax.broadcasted_iota(jnp.int32, (128, 128), 1)
    highs = jnp.zeros((128, 128), F32)
    totals = jnp.zeros((128, 128), F32)
    for h in range(HEADS):
        keys = [kv_ref[4 * c : 4 * c + 4, h].reshape(512, 128) for c in range(4)]
        high = jnp.full((128, 1), NEGATIVE, F32)
        for c in range(4):
            s = nt(q_ref[h], keys[c])
            s_ref[h % 2, :, c * 512 : c * 512 + 512] = s
            high = jnp.maximum(high, jnp.max(s, axis=1, keepdims=True))
        total = jnp.zeros((128, 1), F32)
        acc = jnp.zeros((128, 128), F32)
        for c in range(4):
            p = jnp.exp(s_ref[h % 2, :, c * 512 : c * 512 + 512] - high)
            total = total + jnp.sum(p, axis=1, keepdims=True)
            acc = acc + nn(p.astype(BF16), keys[c])
        out_ref[:, 64 * h : 64 * h + 64] = acc[:, 64:128]
        highs = jnp.where(lane == h, high, highs)
        totals = jnp.where(lane == h, total, totals)
    out_ref[:, 384:512] = highs
    out_ref[:, 512:640] = totals


def partial(wq, wkv, remote, kv):
    shape = jax.ShapeDtypeStruct
    return call(
        partial_kernel,
        (shape((128, 640), F32), shape((HEADS, 128, 128), BF16)),
        [
            pltpu.VMEM((128, 768), BF16),
            pltpu.VMEM((HEADS, 128, 128), BF16),
            pltpu.VMEM((2, 128, 2048), F32),
        ],
        (2_000_000_000, 10_000_000, 1_600_000),
        [],
        near=[wq, wkv, kv, remote],
        held=(1,),
    )


def merge_kernel(parts_ref, out_ref):
    highs = parts_ref[:, :, 384:512]
    factor = jnp.exp(highs - jnp.max(highs, axis=0, keepdims=True))
    total = jnp.sum(factor * parts_ref[:, :, 512:640], axis=0)
    outs = []
    for h in range(HEADS):
        acc = jnp.sum(parts_ref[:, :, 64 * h : 64 * h + 64] * factor[:, :, h : h + 1], axis=0)
        outs.append(acc / total[:, h : h + 1])
    rows = jnp.concatenate(outs, axis=1).astype(BF16)
    for p in range(32):
        out_ref[p] = rows


def merge(parts):
    return call(
        merge_kernel,
        jax.ShapeDtypeStruct((32, 8, 384), BF16),
        [],
        (2_000_000, 600_000, 10_000),
        [],
        near=[parts],
    )


def attend_kernel(first, count, q_ref, ext_ref, pair_ref, remote_ref, more_ref, slot_ref, here_ref, flag_ref, out_ref, items_ref, keys_ref):
    size = 16 * STRIDE

    def each(body):
        for b in range(4):
            for h in range(2 * count):
                for r in range(3):
                    body((b * 2 * count + h) * 3 + r, slot_ref[0, (b * HEADS + 2 * first + h) * 3 + r])

    def main(i, slot):
        at = pl.multiple_of(jnp.minimum(slot, size - 64), 16)
        items_ref[i] = remote_ref[pl.ds(at, 64), :]

    def beyond(i, slot):
        @pl.when(slot >= size)
        def _():
            items_ref[i] = more_ref[pl.ds(pl.multiple_of(slot - size, 64), 64), :]

    each(main)

    @pl.when(flag_ref[0, 0] > 0)
    def _():
        each(beyond)

    seq = (here_ref[0, 0] * 8 + here_ref[0, 1]) * 4 + here_ref[0, 2]
    lane = lax.broadcasted_iota(jnp.int32, (64, 512), 1)
    for pair in range(count):
        for b in range(4):
            outs = []
            for k in range(2):
                h = 2 * (first + pair) + k
                i = (b * 2 * count + 2 * pair + k) * 3
                buf = keys_ref.at[b * 2 + k]
                buf[0:192, :] = ext_ref[h, b * 64 : b * 64 + 192, :]
                for r in range(3):
                    buf[192 + 64 * r : 256 + 64 * r, :] = items_ref[i + r]
                buf[384:512, :] = pair_ref[h]
                keys = buf[...]
                s = nt(q_ref[h, b * 64 : b * 64 + 64, :], keys)
                if b == 0:
                    s = jnp.where((lane < 64) & (seq == 0), NEGATIVE, s)
                if b == 3:
                    s = jnp.where((lane >= 128) & (lane < 192) & (seq == 127), NEGATIVE, s)
                p = jnp.exp(s - jnp.max(s, axis=1, keepdims=True))
                w = (p * (1.0 / jnp.sum(p, axis=1, keepdims=True))).astype(BF16)
                outs.append(nn(w, keys)[:, 64:128])
            out_ref[b * 64 : b * 64 + 64, 128 * pair : 128 * pair + 128] = jnp.concatenate(outs, axis=1).astype(BF16)


def attend(first, count, q, ext, pair, remote, more, slots, here, flag):
    return call(
        functools.partial(attend_kernel, first, count),
        jax.ShapeDtypeStruct((256, 128 * count), BF16),
        [pltpu.VMEM((24 * count, 64, 128), BF16), pltpu.VMEM((8, 512, 128), BF16)],
        (200_000_000 * count, 1_500_000 * count, 270_000 * count),
        [],
        near=[q, ext, pair, remote, more],
        held=(0,),
        scalars=[slots, here, flag],
    )


def norm(v, gain):
    shifted = v - jnp.mean(v, axis=1, keepdims=True)
    spread = jnp.mean(shifted * shifted, axis=1, keepdims=True)
    return shifted * lax.rsqrt(spread + EPSILON) * gain


CHUNK = 512


def finish_kernel(
    own_ref,
    other_ref,
    own2_ref,
    other2_ref,
    states_ref,
    wo_own,
    wo_other,
    gain_ref,
    gain2_ref,
    up_own,
    up_other,
    down_own,
    down_other,
    rows,
    ids_ref,
    here_ref,
    out_ref,
    attended,
    states,
    wo,
    gains,
    up,
    down,
    sums,
    result,
    sem,
    sems,
):
    copies = [
        pltpu.make_async_copy(source, target, sem.at[i])
        for i, (source, target) in enumerate(
            [
                (own_ref, attended.at[0, :, pl.ds(0, 256)]),
                (other_ref, attended.at[1, :, pl.ds(0, 256)]),
                (own2_ref, attended.at[0, :, pl.ds(256, 128)]),
                (other2_ref, attended.at[1, :, pl.ds(256, 128)]),
                (wo_own, wo.at[0]),
                (wo_other, wo.at[1]),
                (states_ref, states),
                (gain_ref, gains.at[0]),
                (gain2_ref, gains.at[1]),
            ]
        )
    ]
    chunks = []
    for half, (above, below) in enumerate(((up_own, down_own), (up_other, down_other))):
        for i in range(0, 1536, CHUNK):
            number = len(chunks)
            part = pl.ds(i, CHUNK)
            chunks.append(
                (
                    pltpu.make_async_copy(above.at[:, part], up.at[number], sems.at[2 * number]),
                    pltpu.make_async_copy(below.at[part, :], down.at[number], sems.at[2 * number + 1]),
                )
            )
    for copy in copies:
        copy.start()
    for chunk in chunks:
        chunk[0].start()
        chunk[1].start()
    for copy in copies:
        copy.wait()
    core = here_ref[0, 3]
    seq = (here_ref[0, 0] * 8 + here_ref[0, 1]) * 4 + here_ref[0, 2]
    for g in range(2):

        @pl.when((ids_ref[0, g] >> 2) == seq)
        def _():
            for k, side in ((0, core), (1, 1 - core)):
                for i in range(4):
                    first = (g * 8 + 2 * i) * 2 + side
                    at = pl.multiple_of((ids_ref[0, g] & 3) * 64 + 16 * i, 16)
                    attended[k, pl.ds(at, 16), :] = jnp.concatenate([rows[first], rows[first + 2]], axis=0)

    projected = nn(attended[0], wo[0]) + nn(attended[1], wo[1])
    normed = norm(states[...].astype(F32) + projected, gains[0]).astype(BF16)
    for number, chunk in enumerate(chunks):
        chunk[0].wait()
        v = nn(normed, up[number])
        hidden = (v * (1.0 + lax.erf(v * 0.7071067811865476)) * 0.5).astype(BF16)
        chunk[1].wait()
        piece = nn(hidden, down[number])
        half = number // (1536 // CHUNK)
        if number % (1536 // CHUNK) == 0:
            sums[half] = piece
        else:
            sums[half] += piece
    result[...] = norm(normed.astype(F32) + (sums[0] + sums[1]), gains[1]).astype(BF16)
    pltpu.sync_copy(result, out_ref)


def finish(*operands):
    count = 2 * 1536 // CHUNK
    return pl.pallas_call(
        finish_kernel,
        out_shape=jax.ShapeDtypeStruct((256, 768), BF16),
        in_specs=[FAR] * 13 + [NEAR] + [SMEM] * 2,
        out_specs=FAR,
        scratch_shapes=[
            pltpu.VMEM((2, 256, 384), BF16),
            pltpu.VMEM((256, 768), BF16),
            pltpu.VMEM((2, 384, 768), BF16),
            pltpu.VMEM((2, 1, 768), F32),
            pltpu.VMEM((count, 768, CHUNK), BF16),
            pltpu.VMEM((count, CHUNK, 768), BF16),
            pltpu.VMEM((2, 256, 768), F32),
            pltpu.VMEM((256, 768), BF16),
            pltpu.SemaphoreType.DMA((9,)),
            pltpu.SemaphoreType.DMA((2 * count,)),
        ],
        cost_estimate=pl.CostEstimate(flops=2_700_000_000, bytes_accessed=12_000_000, transcendentals=800_000),
        compiler_params=pltpu.CompilerParams(vmem_limit_bytes=LIMIT),
    )(*operands)


def turned(value, axis, shift):
    count = lax.axis_size(axis)
    return lax.ppermute(value, axis, [(i, (i + shift) % count) for i in range(count)])


def exchanged(value, axes):
    return lax.all_to_all(value, axes, split_axis=0, concat_axis=0, tiled=True)


def swapped(value):
    return lax.ppermute(value, "mp", [(0, 1), (1, 0)])


def shards(
    states, qkv_weight, out_weight, up_weight, down_weight, attn_gain, mlp_gain, global_ids, random_owner, random_local
):
    x, z, y, core = (lax.axis_index(axis) for axis in ("x", "z", "y", "mp"))
    here = jnp.stack([x, z, y, core]).astype(jnp.int32).reshape(1, 4)
    ids = global_ids.reshape(1, 2)
    tied = lax.optimization_barrier

    up0 = lax.dynamic_slice_in_dim(states, core * 128, 128, 0)
    ends = [(i, i + 1) for i in range(127)]
    before = lax.ppermute(states[192:], SEQ, ends)
    after = lax.ppermute(states[:64], SEQ, [(j, i) for i, j in ends])
    up1, down1, far0 = turned(up0, "z", 1), turned(up0, "z", -1), swapped(up0)
    order = (0, 3, 1, 2)
    spread, slots = plan(states, random_owner.transpose(order), random_local.transpose(order), ids, here)
    received = exchanged(spread, PLANE)
    up1, down1, far0 = tied((up1, down1, far0))

    up2, down2 = turned(up1, "z", 1), turned(down1, "z", -1)
    far1, far7 = swapped(up1), swapped(down1)
    up2, down2, far1, far7, received = tied((up2, down2, far1, far7, received))

    root_owner = pick(x >= 2, global_ids[1], global_ids[0]) >> 2
    root = (root_owner >> 5) * 4 + (root_owner & 3)
    share = lax.dynamic_slice(received, (root, 0, 0), (1, 48, 128))
    shares = exchanged(jnp.broadcast_to(share, (8, 48, 128)), "z")
    up3, down3 = turned(up2, "z", 1), turned(down2, "z", -1)
    far2, far6 = swapped(up2), swapped(down2)
    up3, down3, far2, far6, shares, before, after = tied((up3, down3, far2, far6, shares, before, after))

    up4 = turned(up3, "z", 1)
    far3, far5 = swapped(up3), swapped(down3)
    pieces = [up0, up1, up2, up3, up4, down3, down2, down1, far0, far1, far2, far3, swapped(up4), far5, far6, far7]
    pairs, items, wanted, flag = column(pieces, qkv_weight, received, shares)
    more = lax.cond(flag[0, 0] > 0, lambda: extra(pairs, wanted), unused)
    items, more, weights = tied((items, more, (out_weight, up_weight, down_weight)))
    remote = exchanged(items, PLANE)
    wo_other, up_other, down_other = (swapped(weight) for weight in weights)
    q, ext, wq, wkv = window(before, states, after, qkv_weight)
    remote, ext = tied((remote, ext))
    part, pair = partial(wq, wkv, remote, pairs.reshape(16, HEADS, 128, 128))
    parts = exchanged(part.reshape(16, 8, 640), PLANE)
    rest = (q, ext, pair, remote.reshape(16 * STRIDE, 128), more.reshape(16 * MORE * 64, 128), slots, here, flag)
    attended = attend(0, 2, *rest)
    parts, attended = tied((parts, attended))
    rows = exchanged(merge(parts), PLANE + ("mp",))
    attended2 = attend(2, 1, *rest)
    return finish(
        attended,
        swapped(attended),
        attended2,
        swapped(attended2),
        states,
        out_weight,
        wo_other,
        attn_gain.reshape(1, -1),
        mlp_gain.reshape(1, -1),
        up_weight,
        up_other,
        down_weight,
        down_other,
        rows,
        ids,
        here,
    )


def solution(mesh):
    split = Mesh(mesh.devices.reshape(4, 8, 4, mesh.shape["mp"]), ("x", "z", "y", "mp"))
    placed = (
        P(SEQ, None),
        P(None, None, "mp"),
        P("mp", None),
        P(None, "mp"),
        P("mp", None),
        P(),
        P(),
        P(),
        P("mp", SEQ, None, None),
        P("mp", SEQ, None, None),
    )
    return jax.shard_map(shards, mesh=split, in_specs=placed, out_specs=P(SEQ, None), check_vma=False)
```

```python
import functools

import jax
import jax.numpy as jnp
from jax import lax
from jax.experimental import pallas as pl
from jax.experimental.pallas import tpu as pltpu
from jax.sharding import Mesh
from jax.sharding import PartitionSpec as P

SEQ = ("x", "z", "y")
PLANE = ("x", "y")
EPSILON = 1e-05
NEGATIVE = -1e30
HEADS = 6
BF16 = jnp.bfloat16
F32 = jnp.float32
LIMIT = 51 * 1024 * 1024
HIGH = 60 * 1024 * 1024
SLOTS = 10
MORE = 16 - SLOTS
STRIDE = SLOTS * 64 + 48
FAR = pl.BlockSpec(memory_space=pltpu.HBM)
NEAR = pl.BlockSpec(memory_space=pltpu.VMEM)
SMEM = pl.BlockSpec(memory_space=pltpu.SMEM)


def nt(a, b):
    return lax.dot_general(a, b, (((1,), (1,)), ((), ())), preferred_element_type=F32)


def nn(a, b):
    return jnp.dot(a, b, preferred_element_type=F32)


def call(kernel, outs, scratch, cost, arrays, raw=(), near=(), scalars=(), by_hand=(), held=(), tables=(), limit=LIMIT):
    single = not isinstance(outs, tuple)
    results = (outs,) if single else outs
    away = [i for i in range(len(results)) if i not in held]
    count, total = len(arrays), len(arrays) + len(raw) + len(near) + len(scalars)

    def body(*refs):
        inputs, others = refs[:count], refs[count:total]
        outputs = refs[total : total + len(results)]
        listed = refs[total + len(results) : total + len(results) + len(tables)]
        left = refs[total + len(results) + len(tables) :]
        copied, made, (sem_in, sem_out), rest = (
            left[:count],
            left[count : count + len(away)],
            left[count + len(away) : count + len(away) + 2],
            left[count + len(away) + 2 :],
        )
        copies = [pltpu.make_async_copy(inputs[i], copied[i], sem_in.at[i]) for i in range(count)]
        for copy in copies:
            copy.start()
        for copy in copies:
            copy.wait()
        places = [made[away.index(i)] if i in away else outputs[i] for i in range(len(results))]
        kernel(*copied, *others, *places, *[outputs[i] for i in by_hand], *listed, *rest)
        copies = [pltpu.make_async_copy(places[i], outputs[i], sem_out.at[i]) for i in away if i not in by_hand]
        for copy in copies:
            copy.start()
        for copy in copies:
            copy.wait()

    made = pl.pallas_call(
        body,
        out_shape=(*results, *tables),
        in_specs=[FAR] * (count + len(raw)) + [NEAR] * len(near) + [SMEM] * len(scalars),
        out_specs=tuple(FAR if i in away else NEAR for i in range(len(results))) + (SMEM,) * len(tables),
        scratch_shapes=[pltpu.VMEM(v.shape, v.dtype) for v in (*arrays, *[results[i] for i in away])]
        + [pltpu.SemaphoreType.DMA((max(count, 1),)), pltpu.SemaphoreType.DMA((len(results),))]
        + list(scratch),
        cost_estimate=pl.CostEstimate(flops=cost[0], bytes_accessed=cost[1], transcendentals=cost[2]),
        compiler_params=pltpu.CompilerParams(vmem_limit_bytes=limit),
    )(*arrays, *raw, *near, *scalars)
    return made[0] if single and not tables else made


def pick(condition, yes, no):
    return jnp.where(condition, yes, no)


def piece_of(owner, local, z, core):
    return ((z - ((owner >> 2) & 7)) & 7) + pick((local >> 1) == core, 0, 8)


def plan_kernel(states_ref, owner_ref, local_ref, ids_ref, here_ref, spread_ref, slots_ref, count_ref, rows_ref, sem):
    z, core = here_ref[0, 1], here_ref[0, 3]
    copies = []
    for g in range(2):
        start = pl.multiple_of((ids_ref[0, g] & 3) * 64, 64)
        copies.append(pltpu.make_async_copy(states_ref.at[pl.ds(start, 64), :], rows_ref.at[pl.ds(64 * g, 64), :], sem.at[g]))
        copies[g].start()
    for p in range(16):
        count_ref[p] = 0
    line = lax.broadcasted_iota(jnp.int32, (16, 128), 0)
    lane = lax.broadcasted_iota(jnp.int32, (16, 128), 1)
    place = line * 128 + lane
    wanted = jnp.zeros((16, 128), F32)
    most = jnp.int32(0)
    for b in range(4):
        for h in range(HEADS):
            for r in range(3):
                owner, local = owner_ref[0, r, b, h], local_ref[0, r, b, h]
                item = (piece_of(owner, local, z, core) * HEADS + h) * 2 + (local & 1)
                group = ((owner >> 5) << 2) + (owner & 3)
                rank = count_ref[group]
                count_ref[group] = rank + 1
                most = jnp.maximum(most, rank)
                near = group * STRIDE + rank * 64
                beyond = 16 * STRIDE + group * MORE * 64 + (rank - SLOTS) * 64
                slots_ref[0, (b * HEADS + h) * 3 + r] = pick(rank < SLOTS, near, beyond)
                wanted = jnp.where(place == group * 128 + rank, item.astype(F32), wanted)
    roots = [((ids_ref[0, g] >> 4) & 7).astype(F32) for g in range(2)]
    wanted = jnp.where(lane == 126, jnp.where(line >= 8, roots[1], roots[0]), wanted)
    wanted = jnp.where(lane == 127, pick(most >= SLOTS, 1.0, 0.0), wanted)
    for copy in copies:
        copy.wait()
    for p in range(16):
        spread_ref[p, 48:64, :] = jnp.broadcast_to(wanted[p : p + 1, :], (16, 128)).astype(BF16)
        for c in range(3):
            lanes = (p % 2) * 384 + c * 128
            spread_ref[p, 16 * c : 16 * c + 16, :] = rows_ref[p // 2 * 16 : p // 2 * 16 + 16, lanes : lanes + 128]


def plan(states, owner, local, ids, here):
    shape = jax.ShapeDtypeStruct
    return call(
        plan_kernel,
        shape((16, 64, 128), BF16),
        [pltpu.SMEM((16,), jnp.int32), pltpu.VMEM((128, 768), BF16), pltpu.SemaphoreType.DMA((2,))],
        (1_000_000, 600_000, 0),
        [],
        raw=[states],
        scalars=[owner, local, ids, here],
        tables=(shape((1, 72), jnp.int32),),
        limit=HIGH,
    )


def interleave(weight_ref, first, wkv_ref):
    for h in range(HEADS):
        part = slice(64 * h, 64 * h + 64)
        wkv_ref[:, 128 * h : 128 * h + 64] = weight_ref[first, :, part]
        wkv_ref[:, 128 * h + 64 : 128 * h + 128] = weight_ref[first + 1, :, part]


def column_kernel(*refs):
    pieces = refs[1:17]
    weight_far = refs[0]
    (
        received_ref,
        shares_ref,
        kv_ref,
        items_ref,
        out_ref,
        wanted_ref,
        flag_ref,
        asked_ref,
        rows_ref,
        weight_ref,
        wkv_ref,
        sem,
        sems,
    ) = refs[17:]
    weight = pltpu.make_async_copy(weight_far.at[pl.ds(1, 2)], weight_ref, sem.at[1])
    weight.start()
    for i, piece in enumerate(pieces):
        rows_ref[128 * i : 128 * i + 128, :] = piece[...]
    for p in range(16):
        asked_ref[p : p + 1, :] = received_ref[p, 48:49, :].astype(F32).astype(jnp.int32)
    asked = pltpu.make_async_copy(asked_ref, wanted_ref, sem.at[0])
    asked.start()
    weight.wait()
    interleave(weight_ref, 0, wkv_ref)

    @pl.loop(0, 4)
    def _(i):
        pair = nn(rows_ref[pl.ds(pl.multiple_of(i * 512, 512), 512), :], wkv_ref[...]).astype(BF16)
        for j in range(4):
            for h in range(HEADS):
                kv_ref[(4 * i + j) * HEADS + h] = pair[128 * j : 128 * j + 128, 128 * h : 128 * h + 128]

    asked.wait()
    flag = wanted_ref[0, 127]
    for p in range(1, 16):
        flag = jnp.maximum(flag, wanted_ref[p, 127])
    flag_ref[0, 0] = flag
    share = shares_ref[wanted_ref[0, 126]]
    for p in range(16):
        items_ref[p, SLOTS * 64 : STRIDE, :] = share

    @pl.loop(0, 16)
    def _(p):
        for k in range(SLOTS):
            item = wanted_ref[p, k]
            at = pl.multiple_of((item & 1) * 64, 64)
            items_ref[p, 64 * k : 64 * k + 64, :] = kv_ref[item >> 1, pl.ds(at, 64), :]
        pltpu.make_async_copy(items_ref.at[p], out_ref.at[p], sems.at[p]).start()

    @pl.loop(0, 16)
    def _(p):
        pltpu.make_async_copy(items_ref.at[p], out_ref.at[p], sems.at[p]).wait()


def column(pieces, weight, received, shares):
    shape = jax.ShapeDtypeStruct
    return call(
        column_kernel,
        (shape((16 * HEADS, 128, 128), BF16), shape((16, STRIDE, 128), BF16)),
        [
            pltpu.VMEM((16, 128), jnp.int32),
            pltpu.VMEM((2048, 768), BF16),
            pltpu.VMEM((2, 768, 384), BF16),
            pltpu.VMEM((768, 768), BF16),
            pltpu.SemaphoreType.DMA((2,)),
            pltpu.SemaphoreType.DMA((16,)),
        ],
        (2_400_000_000, 10_000_000, 0),
        [],
        raw=[weight],
        near=[*pieces, received, shares],
        by_hand=(1,),
        held=(0,),
        tables=(shape((16, 128), jnp.int32), shape((1, 1), jnp.int32)),
    )


def extra_kernel(kv_ref, wanted_ref, items_ref):
    @pl.loop(0, 16)
    def _(p):
        for k in range(MORE):
            item = wanted_ref[p, SLOTS + k]
            at = pl.multiple_of((item & 1) * 64, 64)
            items_ref[p, 64 * k : 64 * k + 64, :] = kv_ref[item >> 1, pl.ds(at, 64), :]


def extra(kv, wanted):
    shape = jax.ShapeDtypeStruct((16, MORE * 64, 128), BF16)
    items = call(extra_kernel, shape, [], (0, 5_000_000, 0), [], near=[kv], scalars=[wanted])
    return exchanged(items, PLANE)


def unused_kernel(out_ref, row_ref):
    row_ref[...] = jnp.zeros_like(row_ref)
    pltpu.sync_copy(row_ref, out_ref.at[0, pl.ds(0, 16), :])


def unused():
    return pl.pallas_call(
        unused_kernel,
        out_shape=jax.ShapeDtypeStruct((16, MORE * 64, 128), BF16),
        out_specs=FAR,
        scratch_shapes=[pltpu.VMEM((16, 128), BF16)],
        compiler_params=pltpu.CompilerParams(vmem_limit_bytes=LIMIT),
    )()


def window_kernel(before_ref, states_ref, after_ref, weight_ref, q_ref, ext_ref, wq_ref, wkv_ref, rows_ref):
    wq_ref[...] = jnp.zeros_like(wq_ref)
    for h in range(HEADS):
        wq_ref[:, 128 * h : 128 * h + 64] = weight_ref[0, :, 64 * h : 64 * h + 64] * BF16(0.125)
    interleave(weight_ref, 1, wkv_ref)
    rows_ref[0:64, :] = before_ref[...]
    rows_ref[64:320, :] = states_ref[...]
    rows_ref[320:384, :] = after_ref[...]
    pair = nn(rows_ref[...], wkv_ref[...]).astype(BF16)
    query = nn(states_ref[...], wq_ref[...]).astype(BF16)
    for h in range(HEADS):
        ext_ref[h] = pair[:, 128 * h : 128 * h + 128]
        q_ref[h] = query[:, 128 * h : 128 * h + 128]


def window(before, states, after, weight):
    shape = jax.ShapeDtypeStruct
    square = shape((768, 768), BF16)
    return call(
        window_kernel,
        (shape((HEADS, 256, 128), BF16), shape((HEADS, 384, 128), BF16), square, square),
        [pltpu.VMEM((384, 768), BF16)],
        (800_000_000, 4_000_000, 0),
        [before, states, after, weight],
        held=(0, 1, 2, 3),
    )


def partial_kernel(wq_ref, wkv_ref, kv_ref, remote_ref, out_ref, pair_ref, rows_ref, q_ref, s_ref):
    for p in range(16):
        for c in range(3):
            lanes = (p % 2) * 384 + c * 128
            first = SLOTS * 64 + 16 * c
            rows_ref[p // 2 * 16 : p // 2 * 16 + 16, lanes : lanes + 128] = remote_ref[p, first : first + 16, :]
    query = nn(rows_ref[...], wq_ref[...]).astype(BF16)
    pair = nn(rows_ref[...], wkv_ref[...]).astype(BF16)
    for h in range(HEADS):
        q_ref[h] = query[:, 128 * h : 128 * h + 128]
        pair_ref[h] = pair[:, 128 * h : 128 * h + 128]
    lane = lax.broadcasted_iota(jnp.int32, (128, 128), 1)
    highs = jnp.zeros((128, 128), F32)
    totals = jnp.zeros((128, 128), F32)
    for h in range(HEADS):
        keys = [kv_ref[4 * c : 4 * c + 4, h].reshape(512, 128) for c in range(4)]
        high = jnp.full((128, 1), NEGATIVE, F32)
        for c in range(4):
            s = nt(q_ref[h], keys[c])
            s_ref[h % 2, :, c * 512 : c * 512 + 512] = s
            high = jnp.maximum(high, jnp.max(s, axis=1, keepdims=True))
        total = jnp.zeros((128, 1), F32)
        acc = jnp.zeros((128, 128), F32)
        for c in range(4):
            p = jnp.exp(s_ref[h % 2, :, c * 512 : c * 512 + 512] - high)
            total = total + jnp.sum(p, axis=1, keepdims=True)
            acc = acc + nn(p.astype(BF16), keys[c])
        out_ref[:, 64 * h : 64 * h + 64] = acc[:, 64:128]
        highs = jnp.where(lane == h, high, highs)
        totals = jnp.where(lane == h, total, totals)
    out_ref[:, 384:512] = highs
    out_ref[:, 512:640] = totals


def partial(wq, wkv, remote, kv):
    shape = jax.ShapeDtypeStruct
    return call(
        partial_kernel,
        (shape((128, 640), F32), shape((HEADS, 128, 128), BF16)),
        [
            pltpu.VMEM((128, 768), BF16),
            pltpu.VMEM((HEADS, 128, 128), BF16),
            pltpu.VMEM((2, 128, 2048), F32),
        ],
        (2_000_000_000, 10_000_000, 1_600_000),
        [],
        near=[wq, wkv, kv, remote],
        held=(1,),
    )


def merge_kernel(parts_ref, out_ref):
    highs = parts_ref[:, :, 384:512]
    factor = jnp.exp(highs - jnp.max(highs, axis=0, keepdims=True))
    total = jnp.sum(factor * parts_ref[:, :, 512:640], axis=0)
    outs = []
    for h in range(HEADS):
        acc = jnp.sum(parts_ref[:, :, 64 * h : 64 * h + 64] * factor[:, :, h : h + 1], axis=0)
        outs.append(acc / total[:, h : h + 1])
    rows = jnp.concatenate(outs, axis=1).astype(BF16)
    for p in range(32):
        out_ref[p] = rows


def merge(parts):
    return call(
        merge_kernel,
        jax.ShapeDtypeStruct((32, 8, 384), BF16),
        [],
        (2_000_000, 600_000, 10_000),
        [],
        near=[parts],
    )


def attend_kernel(first, count, q_ref, ext_ref, pair_ref, remote_ref, more_ref, slot_ref, here_ref, flag_ref, out_ref, items_ref, keys_ref):
    size = 16 * STRIDE

    def each(body):
        for b in range(4):
            for h in range(2 * count):
                for r in range(3):
                    body((b * 2 * count + h) * 3 + r, slot_ref[0, (b * HEADS + 2 * first + h) * 3 + r])

    def main(i, slot):
        at = pl.multiple_of(jnp.minimum(slot, size - 64), 16)
        items_ref[i] = remote_ref[pl.ds(at, 64), :]

    def beyond(i, slot):
        @pl.when(slot >= size)
        def _():
            items_ref[i] = more_ref[pl.ds(pl.multiple_of(slot - size, 64), 64), :]

    each(main)

    @pl.when(flag_ref[0, 0] > 0)
    def _():
        each(beyond)

    seq = (here_ref[0, 0] * 8 + here_ref[0, 1]) * 4 + here_ref[0, 2]
    lane = lax.broadcasted_iota(jnp.int32, (64, 512), 1)
    for pair in range(count):
        for b in range(4):
            outs = []
            for k in range(2):
                h = 2 * (first + pair) + k
                i = (b * 2 * count + 2 * pair + k) * 3
                buf = keys_ref.at[b * 2 + k]
                buf[0:192, :] = ext_ref[h, b * 64 : b * 64 + 192, :]
                for r in range(3):
                    buf[192 + 64 * r : 256 + 64 * r, :] = items_ref[i + r]
                buf[384:512, :] = pair_ref[h]
                keys = buf[...]
                s = nt(q_ref[h, b * 64 : b * 64 + 64, :], keys)
                if b == 0:
                    s = jnp.where((lane < 64) & (seq == 0), NEGATIVE, s)
                if b == 3:
                    s = jnp.where((lane >= 128) & (lane < 192) & (seq == 127), NEGATIVE, s)
                p = jnp.exp(s - jnp.max(s, axis=1, keepdims=True))
                w = (p * (1.0 / jnp.sum(p, axis=1, keepdims=True))).astype(BF16)
                outs.append(nn(w, keys)[:, 64:128])
            out_ref[b * 64 : b * 64 + 64, 128 * pair : 128 * pair + 128] = jnp.concatenate(outs, axis=1).astype(BF16)


def attend(first, count, q, ext, pair, remote, more, slots, here, flag):
    return call(
        functools.partial(attend_kernel, first, count),
        jax.ShapeDtypeStruct((256, 128 * count), BF16),
        [pltpu.VMEM((24 * count, 64, 128), BF16), pltpu.VMEM((8, 512, 128), BF16)],
        (200_000_000 * count, 1_500_000 * count, 270_000 * count),
        [],
        near=[q, ext, pair, remote, more],
        held=(0,),
        scalars=[slots, here, flag],
    )


def norm(v, gain):
    shifted = v - jnp.mean(v, axis=1, keepdims=True)
    spread = jnp.mean(shifted * shifted, axis=1, keepdims=True)
    return shifted * lax.rsqrt(spread + EPSILON) * gain


CHUNK = 512


def finish_kernel(
    own_ref,
    other_ref,
    own2_ref,
    other2_ref,
    states_ref,
    wo_own,
    wo_other,
    gain_ref,
    gain2_ref,
    up_own,
    up_other,
    down_own,
    down_other,
    rows,
    ids_ref,
    here_ref,
    out_ref,
    attended,
    states,
    wo,
    gains,
    up,
    down,
    sums,
    result,
    sem,
    sems,
):
    copies = [
        pltpu.make_async_copy(source, target, sem.at[i])
        for i, (source, target) in enumerate(
            [
                (own_ref, attended.at[0, :, pl.ds(0, 256)]),
                (other_ref, attended.at[1, :, pl.ds(0, 256)]),
                (own2_ref, attended.at[0, :, pl.ds(256, 128)]),
                (other2_ref, attended.at[1, :, pl.ds(256, 128)]),
                (wo_own, wo.at[0]),
                (wo_other, wo.at[1]),
                (states_ref, states),
                (gain_ref, gains.at[0]),
                (gain2_ref, gains.at[1]),
            ]
        )
    ]
    chunks = []
    for half, (above, below) in enumerate(((up_own, down_own), (up_other, down_other))):
        for i in range(0, 1536, CHUNK):
            number = len(chunks)
            part = pl.ds(i, CHUNK)
            chunks.append(
                (
                    pltpu.make_async_copy(above.at[:, part], up.at[number], sems.at[2 * number]),
                    pltpu.make_async_copy(below.at[part, :], down.at[number], sems.at[2 * number + 1]),
                )
            )
    for copy in copies:
        copy.start()
    for chunk in chunks:
        chunk[0].start()
        chunk[1].start()
    for copy in copies:
        copy.wait()
    core = here_ref[0, 3]
    seq = (here_ref[0, 0] * 8 + here_ref[0, 1]) * 4 + here_ref[0, 2]
    for g in range(2):

        @pl.when((ids_ref[0, g] >> 2) == seq)
        def _():
            for k, side in ((0, core), (1, 1 - core)):
                for i in range(4):
                    first = (g * 8 + 2 * i) * 2 + side
                    at = pl.multiple_of((ids_ref[0, g] & 3) * 64 + 16 * i, 16)
                    attended[k, pl.ds(at, 16), :] = jnp.concatenate([rows[first], rows[first + 2]], axis=0)

    projected = nn(attended[0], wo[0]) + nn(attended[1], wo[1])
    normed = norm(states[...].astype(F32) + projected, gains[0]).astype(BF16)
    for number, chunk in enumerate(chunks):
        chunk[0].wait()
        v = nn(normed, up[number])
        hidden = (v * (1.0 + lax.erf(v * 0.7071067811865476)) * 0.5).astype(BF16)
        chunk[1].wait()
        piece = nn(hidden, down[number])
        half = number // (1536 // CHUNK)
        if number % (1536 // CHUNK) == 0:
            sums[half] = piece
        else:
            sums[half] += piece
    result[...] = norm(normed.astype(F32) + (sums[0] + sums[1]), gains[1]).astype(BF16)
    pltpu.sync_copy(result, out_ref)


def finish(*operands):
    count = 2 * 1536 // CHUNK
    return pl.pallas_call(
        finish_kernel,
        out_shape=jax.ShapeDtypeStruct((256, 768), BF16),
        in_specs=[FAR] * 13 + [NEAR] + [SMEM] * 2,
        out_specs=FAR,
        scratch_shapes=[
            pltpu.VMEM((2, 256, 384), BF16),
            pltpu.VMEM((256, 768), BF16),
            pltpu.VMEM((2, 384, 768), BF16),
            pltpu.VMEM((2, 1, 768), F32),
            pltpu.VMEM((count, 768, CHUNK), BF16),
            pltpu.VMEM((count, CHUNK, 768), BF16),
            pltpu.VMEM((2, 256, 768), F32),
            pltpu.VMEM((256, 768), BF16),
            pltpu.SemaphoreType.DMA((9,)),
            pltpu.SemaphoreType.DMA((2 * count,)),
        ],
        cost_estimate=pl.CostEstimate(flops=2_700_000_000, bytes_accessed=12_000_000, transcendentals=800_000),
        compiler_params=pltpu.CompilerParams(vmem_limit_bytes=LIMIT),
    )(*operands)


def turned(value, axis, shift):
    count = lax.axis_size(axis)
    return lax.ppermute(value, axis, [(i, (i + shift) % count) for i in range(count)])


def exchanged(value, axes):
    return lax.all_to_all(value, axes, split_axis=0, concat_axis=0, tiled=True)


def swapped(value):
    return lax.ppermute(value, "mp", [(0, 1), (1, 0)])


def shards(
    states, qkv_weight, out_weight, up_weight, down_weight, attn_gain, mlp_gain, global_ids, random_owner, random_local
):
    x, z, y, core = (lax.axis_index(axis) for axis in ("x", "z", "y", "mp"))
    here = jnp.stack([x, z, y, core]).astype(jnp.int32).reshape(1, 4)
    ids = global_ids.reshape(1, 2)
    tied = lax.optimization_barrier

    up0 = lax.dynamic_slice_in_dim(states, core * 128, 128, 0)
    ends = [(i, i + 1) for i in range(127)]
    before = lax.ppermute(states[192:], SEQ, ends)
    after = lax.ppermute(states[:64], SEQ, [(j, i) for i, j in ends])
    up1, down1, far0 = turned(up0, "z", 1), turned(up0, "z", -1), swapped(up0)
    order = (0, 3, 1, 2)
    spread, slots = plan(states, random_owner.transpose(order), random_local.transpose(order), ids, here)
    received = exchanged(spread, PLANE)
    up1, down1, far0 = tied((up1, down1, far0))

    up2, down2 = turned(up1, "z", 1), turned(down1, "z", -1)
    far1, far7 = swapped(up1), swapped(down1)
    up2, down2, far1, far7, received = tied((up2, down2, far1, far7, received))

    root_owner = pick(x >= 2, global_ids[1], global_ids[0]) >> 2
    root = (root_owner >> 5) * 4 + (root_owner & 3)
    share = lax.dynamic_slice(received, (root, 0, 0), (1, 48, 128))
    shares = exchanged(jnp.broadcast_to(share, (8, 48, 128)), "z")
    up3, down3 = turned(up2, "z", 1), turned(down2, "z", -1)
    far2, far6 = swapped(up2), swapped(down2)
    up3, down3, far2, far6 = tied((up3, down3, far2, far6))

    up4 = turned(up3, "z", 1)
    up3, down3, shares, before, after = tied((up3, down3, shares, before, after))
    far3, far5 = swapped(up3), swapped(down3)
    pieces = [up0, up1, up2, up3, up4, down3, down2, down1, far0, far1, far2, far3, swapped(up4), far5, far6, far7]
    pairs, items, wanted, flag = column(pieces, qkv_weight, received, shares)
    more = lax.cond(flag[0, 0] > 0, lambda: extra(pairs, wanted), unused)
    items, more, weights = tied((items, more, (out_weight, up_weight, down_weight)))
    remote = exchanged(items, PLANE)
    wo_other, up_other, down_other = (swapped(weight) for weight in weights)
    q, ext, wq, wkv = window(before, states, after, qkv_weight)
    remote, ext = tied((remote, ext))
    part, pair = partial(wq, wkv, remote, pairs.reshape(16, HEADS, 128, 128))
    parts = exchanged(part.reshape(16, 8, 640), PLANE)
    rest = (q, ext, pair, remote.reshape(16 * STRIDE, 128), more.reshape(16 * MORE * 64, 128), slots, here, flag)
    attended = attend(0, 2, *rest)
    parts, attended = tied((parts, attended))
    rows = exchanged(merge(parts), PLANE + ("mp",))
    attended2 = attend(2, 1, *rest)
    return finish(
        attended,
        swapped(attended),
        attended2,
        swapped(attended2),
        states,
        out_weight,
        wo_other,
        attn_gain.reshape(1, -1),
        mlp_gain.reshape(1, -1),
        up_weight,
        up_other,
        down_weight,
        down_other,
        rows,
        ids,
        here,
    )


def solution(mesh):
    split = Mesh(mesh.devices.reshape(4, 8, 4, mesh.shape["mp"]), ("x", "z", "y", "mp"))
    placed = (
        P(SEQ, None),
        P(None, None, "mp"),
        P("mp", None),
        P(None, "mp"),
        P("mp", None),
        P(),
        P(),
        P(),
        P("mp", SEQ, None, None),
        P("mp", SEQ, None, None),
    )
    return jax.shard_map(shards, mesh=split, in_specs=placed, out_specs=P(SEQ, None), check_vma=False)
```

```python
import functools

import jax
import jax.numpy as jnp
from jax import lax
from jax.experimental import pallas as pl
from jax.experimental.pallas import tpu as pltpu
from jax.sharding import Mesh
from jax.sharding import PartitionSpec as P

SEQ = ("x", "z", "y")
PLANE = ("x", "y")
EPSILON = 1e-05
NEGATIVE = -1e30
HEADS = 6
BF16 = jnp.bfloat16
F32 = jnp.float32
LIMIT = 51 * 1024 * 1024
HIGH = 60 * 1024 * 1024
SLOTS = 9
MORE = 16 - SLOTS
STRIDE = SLOTS * 64 + 48
FAR = pl.BlockSpec(memory_space=pltpu.HBM)
NEAR = pl.BlockSpec(memory_space=pltpu.VMEM)
SMEM = pl.BlockSpec(memory_space=pltpu.SMEM)


def nt(a, b):
    return lax.dot_general(a, b, (((1,), (1,)), ((), ())), preferred_element_type=F32)


def nn(a, b):
    return jnp.dot(a, b, preferred_element_type=F32)


def call(kernel, outs, scratch, cost, arrays, raw=(), near=(), scalars=(), by_hand=(), held=(), tables=(), limit=LIMIT):
    single = not isinstance(outs, tuple)
    results = (outs,) if single else outs
    away = [i for i in range(len(results)) if i not in held]
    count, total = len(arrays), len(arrays) + len(raw) + len(near) + len(scalars)

    def body(*refs):
        inputs, others = refs[:count], refs[count:total]
        outputs = refs[total : total + len(results)]
        listed = refs[total + len(results) : total + len(results) + len(tables)]
        left = refs[total + len(results) + len(tables) :]
        copied, made, (sem_in, sem_out), rest = (
            left[:count],
            left[count : count + len(away)],
            left[count + len(away) : count + len(away) + 2],
            left[count + len(away) + 2 :],
        )
        copies = [pltpu.make_async_copy(inputs[i], copied[i], sem_in.at[i]) for i in range(count)]
        for copy in copies:
            copy.start()
        for copy in copies:
            copy.wait()
        places = [made[away.index(i)] if i in away else outputs[i] for i in range(len(results))]
        kernel(*copied, *others, *places, *[outputs[i] for i in by_hand], *listed, *rest)
        copies = [pltpu.make_async_copy(places[i], outputs[i], sem_out.at[i]) for i in away if i not in by_hand]
        for copy in copies:
            copy.start()
        for copy in copies:
            copy.wait()

    made = pl.pallas_call(
        body,
        out_shape=(*results, *tables),
        in_specs=[FAR] * (count + len(raw)) + [NEAR] * len(near) + [SMEM] * len(scalars),
        out_specs=tuple(FAR if i in away else NEAR for i in range(len(results))) + (SMEM,) * len(tables),
        scratch_shapes=[pltpu.VMEM(v.shape, v.dtype) for v in (*arrays, *[results[i] for i in away])]
        + [pltpu.SemaphoreType.DMA((max(count, 1),)), pltpu.SemaphoreType.DMA((len(results),))]
        + list(scratch),
        cost_estimate=pl.CostEstimate(flops=cost[0], bytes_accessed=cost[1], transcendentals=cost[2]),
        compiler_params=pltpu.CompilerParams(vmem_limit_bytes=limit),
    )(*arrays, *raw, *near, *scalars)
    return made[0] if single and not tables else made


def pick(condition, yes, no):
    return jnp.where(condition, yes, no)


def piece_of(owner, local, z, core):
    return ((z - ((owner >> 2) & 7)) & 7) + pick((local >> 1) == core, 0, 8)


def plan_kernel(states_ref, owner_ref, local_ref, ids_ref, here_ref, spread_ref, slots_ref, count_ref, rows_ref, sem):
    z, core = here_ref[0, 1], here_ref[0, 3]
    copies = []
    for g in range(2):
        start = pl.multiple_of((ids_ref[0, g] & 3) * 64, 64)
        copies.append(pltpu.make_async_copy(states_ref.at[pl.ds(start, 64), :], rows_ref.at[pl.ds(64 * g, 64), :], sem.at[g]))
        copies[g].start()
    for p in range(16):
        count_ref[p] = 0
    line = lax.broadcasted_iota(jnp.int32, (16, 128), 0)
    lane = lax.broadcasted_iota(jnp.int32, (16, 128), 1)
    place = line * 128 + lane
    wanted = jnp.zeros((16, 128), F32)
    most = jnp.int32(0)
    for b in range(4):
        for h in range(HEADS):
            for r in range(3):
                owner, local = owner_ref[0, r, b, h], local_ref[0, r, b, h]
                item = (piece_of(owner, local, z, core) * HEADS + h) * 2 + (local & 1)
                group = ((owner >> 5) << 2) + (owner & 3)
                rank = count_ref[group]
                count_ref[group] = rank + 1
                most = jnp.maximum(most, rank)
                near = group * STRIDE + rank * 64
                beyond = 16 * STRIDE + group * MORE * 64 + (rank - SLOTS) * 64
                slots_ref[0, (b * HEADS + h) * 3 + r] = pick(rank < SLOTS, near, beyond)
                wanted = jnp.where(place == group * 128 + rank, item.astype(F32), wanted)
    roots = [((ids_ref[0, g] >> 4) & 7).astype(F32) for g in range(2)]
    wanted = jnp.where(lane == 126, jnp.where(line >= 8, roots[1], roots[0]), wanted)
    wanted = jnp.where(lane == 127, pick(most >= SLOTS, 1.0, 0.0), wanted)
    for copy in copies:
        copy.wait()
    for p in range(16):
        spread_ref[p, 48:64, :] = jnp.broadcast_to(wanted[p : p + 1, :], (16, 128)).astype(BF16)
        for c in range(3):
            lanes = (p % 2) * 384 + c * 128
            spread_ref[p, 16 * c : 16 * c + 16, :] = rows_ref[p // 2 * 16 : p // 2 * 16 + 16, lanes : lanes + 128]


def plan(states, owner, local, ids, here):
    shape = jax.ShapeDtypeStruct
    return call(
        plan_kernel,
        shape((16, 64, 128), BF16),
        [pltpu.SMEM((16,), jnp.int32), pltpu.VMEM((128, 768), BF16), pltpu.SemaphoreType.DMA((2,))],
        (1_000_000, 600_000, 0),
        [],
        raw=[states],
        scalars=[owner, local, ids, here],
        tables=(shape((1, 72), jnp.int32),),
        limit=HIGH,
    )


def interleave(weight_ref, first, wkv_ref):
    for h in range(HEADS):
        part = slice(64 * h, 64 * h + 64)
        wkv_ref[:, 128 * h : 128 * h + 64] = weight_ref[first, :, part]
        wkv_ref[:, 128 * h + 64 : 128 * h + 128] = weight_ref[first + 1, :, part]


def column_kernel(*refs):
    pieces = refs[1:17]
    weight_far = refs[0]
    (
        received_ref,
        shares_ref,
        kv_ref,
        items_ref,
        out_ref,
        wanted_ref,
        flag_ref,
        asked_ref,
        rows_ref,
        weight_ref,
        wkv_ref,
        sem,
        sems,
    ) = refs[17:]
    weight = pltpu.make_async_copy(weight_far.at[pl.ds(1, 2)], weight_ref, sem.at[1])
    weight.start()
    for i, piece in enumerate(pieces):
        rows_ref[128 * i : 128 * i + 128, :] = piece[...]
    for p in range(16):
        asked_ref[p : p + 1, :] = received_ref[p, 48:49, :].astype(F32).astype(jnp.int32)
    asked = pltpu.make_async_copy(asked_ref, wanted_ref, sem.at[0])
    asked.start()
    weight.wait()
    interleave(weight_ref, 0, wkv_ref)

    @pl.loop(0, 4)
    def _(i):
        pair = nn(rows_ref[pl.ds(pl.multiple_of(i * 512, 512), 512), :], wkv_ref[...]).astype(BF16)
        for j in range(4):
            for h in range(HEADS):
                kv_ref[(4 * i + j) * HEADS + h] = pair[128 * j : 128 * j + 128, 128 * h : 128 * h + 128]

    asked.wait()
    flag = wanted_ref[0, 127]
    for p in range(1, 16):
        flag = jnp.maximum(flag, wanted_ref[p, 127])
    flag_ref[0, 0] = flag
    share = shares_ref[wanted_ref[0, 126]]
    for p in range(16):
        items_ref[p, SLOTS * 64 : STRIDE, :] = share

    @pl.loop(0, 16)
    def _(p):
        for k in range(SLOTS):
            item = wanted_ref[p, k]
            at = pl.multiple_of((item & 1) * 64, 64)
            items_ref[p, 64 * k : 64 * k + 64, :] = kv_ref[item >> 1, pl.ds(at, 64), :]
        pltpu.make_async_copy(items_ref.at[p], out_ref.at[p], sems.at[p]).start()

    @pl.loop(0, 16)
    def _(p):
        pltpu.make_async_copy(items_ref.at[p], out_ref.at[p], sems.at[p]).wait()


def column(pieces, weight, received, shares):
    shape = jax.ShapeDtypeStruct
    return call(
        column_kernel,
        (shape((16 * HEADS, 128, 128), BF16), shape((16, STRIDE, 128), BF16)),
        [
            pltpu.VMEM((16, 128), jnp.int32),
            pltpu.VMEM((2048, 768), BF16),
            pltpu.VMEM((2, 768, 384), BF16),
            pltpu.VMEM((768, 768), BF16),
            pltpu.SemaphoreType.DMA((2,)),
            pltpu.SemaphoreType.DMA((16,)),
        ],
        (2_400_000_000, 10_000_000, 0),
        [],
        raw=[weight],
        near=[*pieces, received, shares],
        by_hand=(1,),
        held=(0,),
        tables=(shape((16, 128), jnp.int32), shape((1, 1), jnp.int32)),
    )


def extra_kernel(kv_ref, wanted_ref, items_ref):
    @pl.loop(0, 16)
    def _(p):
        for k in range(MORE):
            item = wanted_ref[p, SLOTS + k]
            at = pl.multiple_of((item & 1) * 64, 64)
            items_ref[p, 64 * k : 64 * k + 64, :] = kv_ref[item >> 1, pl.ds(at, 64), :]


def extra(kv, wanted):
    shape = jax.ShapeDtypeStruct((16, MORE * 64, 128), BF16)
    items = call(extra_kernel, shape, [], (0, 5_000_000, 0), [], near=[kv], scalars=[wanted])
    return exchanged(items, PLANE)


def unused_kernel(out_ref, row_ref):
    row_ref[...] = jnp.zeros_like(row_ref)
    pltpu.sync_copy(row_ref, out_ref.at[0, pl.ds(0, 16), :])


def unused():
    return pl.pallas_call(
        unused_kernel,
        out_shape=jax.ShapeDtypeStruct((16, MORE * 64, 128), BF16),
        out_specs=FAR,
        scratch_shapes=[pltpu.VMEM((16, 128), BF16)],
        compiler_params=pltpu.CompilerParams(vmem_limit_bytes=LIMIT),
    )()


def window_kernel(before_ref, states_ref, after_ref, weight_ref, q_ref, ext_ref, wq_ref, wkv_ref, rows_ref):
    wq_ref[...] = jnp.zeros_like(wq_ref)
    for h in range(HEADS):
        wq_ref[:, 128 * h : 128 * h + 64] = weight_ref[0, :, 64 * h : 64 * h + 64] * BF16(0.125)
    interleave(weight_ref, 1, wkv_ref)
    rows_ref[0:64, :] = before_ref[...]
    rows_ref[64:320, :] = states_ref[...]
    rows_ref[320:384, :] = after_ref[...]
    pair = nn(rows_ref[...], wkv_ref[...]).astype(BF16)
    query = nn(states_ref[...], wq_ref[...]).astype(BF16)
    for h in range(HEADS):
        ext_ref[h] = pair[:, 128 * h : 128 * h + 128]
        q_ref[h] = query[:, 128 * h : 128 * h + 128]


def window(before, states, after, weight):
    shape = jax.ShapeDtypeStruct
    square = shape((768, 768), BF16)
    return call(
        window_kernel,
        (shape((HEADS, 256, 128), BF16), shape((HEADS, 384, 128), BF16), square, square),
        [pltpu.VMEM((384, 768), BF16)],
        (800_000_000, 4_000_000, 0),
        [before, states, after, weight],
        held=(0, 1, 2, 3),
    )


def partial_kernel(wq_ref, wkv_ref, kv_ref, remote_ref, out_ref, pair_ref, rows_ref, q_ref, s_ref):
    for p in range(16):
        for c in range(3):
            lanes = (p % 2) * 384 + c * 128
            first = SLOTS * 64 + 16 * c
            rows_ref[p // 2 * 16 : p // 2 * 16 + 16, lanes : lanes + 128] = remote_ref[p, first : first + 16, :]
    query = nn(rows_ref[...], wq_ref[...]).astype(BF16)
    pair = nn(rows_ref[...], wkv_ref[...]).astype(BF16)
    for h in range(HEADS):
        q_ref[h] = query[:, 128 * h : 128 * h + 128]
        pair_ref[h] = pair[:, 128 * h : 128 * h + 128]
    lane = lax.broadcasted_iota(jnp.int32, (128, 128), 1)
    highs = jnp.zeros((128, 128), F32)
    totals = jnp.zeros((128, 128), F32)
    for h in range(HEADS):
        keys = [kv_ref[4 * c : 4 * c + 4, h].reshape(512, 128) for c in range(4)]
        high = jnp.full((128, 1), NEGATIVE, F32)
        for c in range(4):
            s = nt(q_ref[h], keys[c])
            s_ref[h % 2, :, c * 512 : c * 512 + 512] = s
            high = jnp.maximum(high, jnp.max(s, axis=1, keepdims=True))
        total = jnp.zeros((128, 1), F32)
        acc = jnp.zeros((128, 128), F32)
        for c in range(4):
            p = jnp.exp(s_ref[h % 2, :, c * 512 : c * 512 + 512] - high)
            total = total + jnp.sum(p, axis=1, keepdims=True)
            acc = acc + nn(p.astype(BF16), keys[c])
        out_ref[:, 64 * h : 64 * h + 64] = acc[:, 64:128]
        highs = jnp.where(lane == h, high, highs)
        totals = jnp.where(lane == h, total, totals)
    out_ref[:, 384:512] = highs
    out_ref[:, 512:640] = totals


def partial(wq, wkv, remote, kv):
    shape = jax.ShapeDtypeStruct
    return call(
        partial_kernel,
        (shape((128, 640), F32), shape((HEADS, 128, 128), BF16)),
        [
            pltpu.VMEM((128, 768), BF16),
            pltpu.VMEM((HEADS, 128, 128), BF16),
            pltpu.VMEM((2, 128, 2048), F32),
        ],
        (2_000_000_000, 10_000_000, 1_600_000),
        [],
        near=[wq, wkv, kv, remote],
        held=(1,),
    )


def merge_kernel(parts_ref, out_ref):
    highs = parts_ref[:, :, 384:512]
    factor = jnp.exp(highs - jnp.max(highs, axis=0, keepdims=True))
    total = jnp.sum(factor * parts_ref[:, :, 512:640], axis=0)
    outs = []
    for h in range(HEADS):
        acc = jnp.sum(parts_ref[:, :, 64 * h : 64 * h + 64] * factor[:, :, h : h + 1], axis=0)
        outs.append(acc / total[:, h : h + 1])
    rows = jnp.concatenate(outs, axis=1).astype(BF16)
    for p in range(32):
        out_ref[p] = rows


def merge(parts):
    return call(
        merge_kernel,
        jax.ShapeDtypeStruct((32, 8, 384), BF16),
        [],
        (2_000_000, 600_000, 10_000),
        [],
        near=[parts],
    )


def attend_kernel(first, count, q_ref, ext_ref, pair_ref, remote_ref, more_ref, slot_ref, here_ref, flag_ref, out_ref, items_ref, keys_ref):
    size = 16 * STRIDE

    def each(body):
        for b in range(4):
            for h in range(2 * count):
                for r in range(3):
                    body((b * 2 * count + h) * 3 + r, slot_ref[0, (b * HEADS + 2 * first + h) * 3 + r])

    def main(i, slot):
        at = pl.multiple_of(jnp.minimum(slot, size - 64), 16)
        items_ref[i] = remote_ref[pl.ds(at, 64), :]

    def beyond(i, slot):
        @pl.when(slot >= size)
        def _():
            items_ref[i] = more_ref[pl.ds(pl.multiple_of(slot - size, 64), 64), :]

    each(main)

    @pl.when(flag_ref[0, 0] > 0)
    def _():
        each(beyond)

    seq = (here_ref[0, 0] * 8 + here_ref[0, 1]) * 4 + here_ref[0, 2]
    lane = lax.broadcasted_iota(jnp.int32, (64, 512), 1)
    for pair in range(count):
        for b in range(4):
            outs = []
            for k in range(2):
                h = 2 * (first + pair) + k
                i = (b * 2 * count + 2 * pair + k) * 3
                buf = keys_ref.at[b * 2 + k]
                buf[0:192, :] = ext_ref[h, b * 64 : b * 64 + 192, :]
                for r in range(3):
                    buf[192 + 64 * r : 256 + 64 * r, :] = items_ref[i + r]
                buf[384:512, :] = pair_ref[h]
                keys = buf[...]
                s = nt(q_ref[h, b * 64 : b * 64 + 64, :], keys)
                if b == 0:
                    s = jnp.where((lane < 64) & (seq == 0), NEGATIVE, s)
                if b == 3:
                    s = jnp.where((lane >= 128) & (lane < 192) & (seq == 127), NEGATIVE, s)
                p = jnp.exp(s - jnp.max(s, axis=1, keepdims=True))
                w = (p * (1.0 / jnp.sum(p, axis=1, keepdims=True))).astype(BF16)
                outs.append(nn(w, keys)[:, 64:128])
            out_ref[b * 64 : b * 64 + 64, 128 * pair : 128 * pair + 128] = jnp.concatenate(outs, axis=1).astype(BF16)


def attend(first, count, q, ext, pair, remote, more, slots, here, flag):
    return call(
        functools.partial(attend_kernel, first, count),
        jax.ShapeDtypeStruct((256, 128 * count), BF16),
        [pltpu.VMEM((24 * count, 64, 128), BF16), pltpu.VMEM((8, 512, 128), BF16)],
        (200_000_000 * count, 1_500_000 * count, 270_000 * count),
        [],
        near=[q, ext, pair, remote, more],
        held=(0,),
        scalars=[slots, here, flag],
    )


def norm(v, gain):
    shifted = v - jnp.mean(v, axis=1, keepdims=True)
    spread = jnp.mean(shifted * shifted, axis=1, keepdims=True)
    return shifted * lax.rsqrt(spread + EPSILON) * gain


CHUNK = 512


def finish_kernel(
    own_ref,
    other_ref,
    own2_ref,
    other2_ref,
    states_ref,
    wo_own,
    wo_other,
    gain_ref,
    gain2_ref,
    up_own,
    up_other,
    down_own,
    down_other,
    rows,
    ids_ref,
    here_ref,
    out_ref,
    attended,
    states,
    wo,
    gains,
    up,
    down,
    sums,
    result,
    sem,
    sems,
):
    copies = [
        pltpu.make_async_copy(source, target, sem.at[i])
        for i, (source, target) in enumerate(
            [
                (own_ref, attended.at[0, :, pl.ds(0, 256)]),
                (other_ref, attended.at[1, :, pl.ds(0, 256)]),
                (own2_ref, attended.at[0, :, pl.ds(256, 128)]),
                (other2_ref, attended.at[1, :, pl.ds(256, 128)]),
                (wo_own, wo.at[0]),
                (wo_other, wo.at[1]),
                (states_ref, states),
                (gain_ref, gains.at[0]),
                (gain2_ref, gains.at[1]),
            ]
        )
    ]
    chunks = []
    for half, (above, below) in enumerate(((up_own, down_own), (up_other, down_other))):
        for i in range(0, 1536, CHUNK):
            number = len(chunks)
            part = pl.ds(i, CHUNK)
            chunks.append(
                (
                    pltpu.make_async_copy(above.at[:, part], up.at[number], sems.at[2 * number]),
                    pltpu.make_async_copy(below.at[part, :], down.at[number], sems.at[2 * number + 1]),
                )
            )
    for copy in copies:
        copy.start()
    for chunk in chunks:
        chunk[0].start()
        chunk[1].start()
    for copy in copies:
        copy.wait()
    core = here_ref[0, 3]
    seq = (here_ref[0, 0] * 8 + here_ref[0, 1]) * 4 + here_ref[0, 2]
    for g in range(2):

        @pl.when((ids_ref[0, g] >> 2) == seq)
        def _():
            for k, side in ((0, core), (1, 1 - core)):
                for i in range(4):
                    first = (g * 8 + 2 * i) * 2 + side
                    at = pl.multiple_of((ids_ref[0, g] & 3) * 64 + 16 * i, 16)
                    attended[k, pl.ds(at, 16), :] = jnp.concatenate([rows[first], rows[first + 2]], axis=0)

    projected = nn(attended[0], wo[0]) + nn(attended[1], wo[1])
    normed = norm(states[...].astype(F32) + projected, gains[0]).astype(BF16)
    for number, chunk in enumerate(chunks):
        chunk[0].wait()
        v = nn(normed, up[number])
        hidden = (v * (1.0 + lax.erf(v * 0.7071067811865476)) * 0.5).astype(BF16)
        chunk[1].wait()
        piece = nn(hidden, down[number])
        half = number // (1536 // CHUNK)
        if number % (1536 // CHUNK) == 0:
            sums[half] = piece
        else:
            sums[half] += piece
    result[...] = norm(normed.astype(F32) + (sums[0] + sums[1]), gains[1]).astype(BF16)
    pltpu.sync_copy(result, out_ref)


def finish(*operands):
    count = 2 * 1536 // CHUNK
    return pl.pallas_call(
        finish_kernel,
        out_shape=jax.ShapeDtypeStruct((256, 768), BF16),
        in_specs=[FAR] * 13 + [NEAR] + [SMEM] * 2,
        out_specs=FAR,
        scratch_shapes=[
            pltpu.VMEM((2, 256, 384), BF16),
            pltpu.VMEM((256, 768), BF16),
            pltpu.VMEM((2, 384, 768), BF16),
            pltpu.VMEM((2, 1, 768), F32),
            pltpu.VMEM((count, 768, CHUNK), BF16),
            pltpu.VMEM((count, CHUNK, 768), BF16),
            pltpu.VMEM((2, 256, 768), F32),
            pltpu.VMEM((256, 768), BF16),
            pltpu.SemaphoreType.DMA((9,)),
            pltpu.SemaphoreType.DMA((2 * count,)),
        ],
        cost_estimate=pl.CostEstimate(flops=2_700_000_000, bytes_accessed=12_000_000, transcendentals=800_000),
        compiler_params=pltpu.CompilerParams(vmem_limit_bytes=LIMIT),
    )(*operands)


def turned(value, axis, shift):
    count = lax.axis_size(axis)
    return lax.ppermute(value, axis, [(i, (i + shift) % count) for i in range(count)])


def exchanged(value, axes):
    return lax.all_to_all(value, axes, split_axis=0, concat_axis=0, tiled=True)


def swapped(value):
    return lax.ppermute(value, "mp", [(0, 1), (1, 0)])


def shards(
    states, qkv_weight, out_weight, up_weight, down_weight, attn_gain, mlp_gain, global_ids, random_owner, random_local
):
    x, z, y, core = (lax.axis_index(axis) for axis in ("x", "z", "y", "mp"))
    here = jnp.stack([x, z, y, core]).astype(jnp.int32).reshape(1, 4)
    ids = global_ids.reshape(1, 2)
    tied = lax.optimization_barrier

    up0 = lax.dynamic_slice_in_dim(states, core * 128, 128, 0)
    ends = [(i, i + 1) for i in range(127)]
    before = lax.ppermute(states[192:], SEQ, ends)
    after = lax.ppermute(states[:64], SEQ, [(j, i) for i, j in ends])
    up1, down1, far0 = turned(up0, "z", 1), turned(up0, "z", -1), swapped(up0)
    order = (0, 3, 1, 2)
    spread, slots = plan(states, random_owner.transpose(order), random_local.transpose(order), ids, here)
    received = exchanged(spread, PLANE)
    up1, down1, far0 = tied((up1, down1, far0))

    up2, down2 = turned(up1, "z", 1), turned(down1, "z", -1)
    far1, far7 = swapped(up1), swapped(down1)
    up2, down2, far1, far7, received = tied((up2, down2, far1, far7, received))

    root_owner = pick(x >= 2, global_ids[1], global_ids[0]) >> 2
    root = (root_owner >> 5) * 4 + (root_owner & 3)
    share = lax.dynamic_slice(received, (root, 0, 0), (1, 48, 128))
    shares = exchanged(jnp.broadcast_to(share, (8, 48, 128)), "z")
    up3, down3 = turned(up2, "z", 1), turned(down2, "z", -1)
    far2, far6 = swapped(up2), swapped(down2)
    up3, down3, far2, far6, shares, before, after = tied((up3, down3, far2, far6, shares, before, after))

    up4 = turned(up3, "z", 1)
    far3, far5 = swapped(up3), swapped(down3)
    pieces = [up0, up1, up2, up3, up4, down3, down2, down1, far0, far1, far2, far3, swapped(up4), far5, far6, far7]
    pairs, items, wanted, flag = column(pieces, qkv_weight, received, shares)
    more = lax.cond(flag[0, 0] > 0, lambda: extra(pairs, wanted), unused)
    items, more, weights = tied((items, more, (out_weight, up_weight, down_weight)))
    remote = exchanged(items, PLANE)
    wo_other, up_other, down_other = (swapped(weight) for weight in weights)
    q, ext, wq, wkv = window(before, states, after, qkv_weight)
    remote, ext = tied((remote, ext))
    part, pair = partial(wq, wkv, remote, pairs.reshape(16, HEADS, 128, 128))
    parts = exchanged(part.reshape(16, 8, 640), PLANE)
    rest = (q, ext, pair, remote.reshape(16 * STRIDE, 128), more.reshape(16 * MORE * 64, 128), slots, here, flag)
    attended = attend(0, 2, *rest)
    parts, attended = tied((parts, attended))
    rows = exchanged(merge(parts), PLANE + ("mp",))
    attended2 = attend(2, 1, *rest)
    return finish(
        attended,
        swapped(attended),
        attended2,
        swapped(attended2),
        states,
        out_weight,
        wo_other,
        attn_gain.reshape(1, -1),
        mlp_gain.reshape(1, -1),
        up_weight,
        up_other,
        down_weight,
        down_other,
        rows,
        ids,
        here,
    )


def solution(mesh):
    split = Mesh(mesh.devices.reshape(4, 8, 4, mesh.shape["mp"]), ("x", "z", "y", "mp"))
    placed = (
        P(SEQ, None),
        P(None, None, "mp"),
        P("mp", None),
        P(None, "mp"),
        P("mp", None),
        P(),
        P(),
        P(),
        P("mp", SEQ, None, None),
        P("mp", SEQ, None, None),
    )
    return jax.shard_map(shards, mesh=split, in_specs=placed, out_specs=P(SEQ, None), check_vma=False)
```
